32 devices in a mesh: grp: 2 (over x), seq: 16 (over z, y, core).
Axes of the slice: x: 2, y: 2, z: 4, core: 2. Of those that a mesh axis runs over, the one named last changes fastest.
Arguments:
- anchor_layers: float32 [2, 7077888], P(None, 'seq'), may hold values from -2 to 2
- anchor_other: float32 [2001408], P('seq'), may hold values from -4 to 4
- first_layers: float32 [2, 2, 7077888], P('grp', None, 'seq'), may hold values from -3.8146973e-06 to 3.8146973e-06
- first_other: float32 [2, 2001408], P('grp', 'seq'), may hold values from -3.8146973e-06 to 3.8146973e-06
- second_layers: float32 [2, 2, 7077888], P('grp', None, 'seq'), may hold values from 3.255518e-13 to 1.2997315e-12
- second_other: float32 [2, 2001408], P('grp', 'seq'), may hold values from 3.255518e-13 to 1.2997315e-12
- outer_layers: float32 [2, 7077888], P(None, 'seq'), may hold values from -0.15625 to 0.15625
- outer_other: float32 [2001408], P('seq'), may hold values from -0.15625 to 0.15625
- latents: float32 [8192, 20], P(('grp', 'seq')), may hold values from -6 to 6
- noise: float32 [8192, 20], P(('grp', 'seq')), may hold values from -6 to 6
- lengths: int32 [2, 12], P('grp'), may hold values from 1 to 512, 4096 in all within a row
- timesteps: int32 [2, 12], P('grp'), may hold values from 0 to 999
- null_flags: int32 [2, 12], P('grp'), may hold values 0 or 1
- captions: float32 [2, 12, 768], P('grp'), may hold values from -6 to 6
Outputs:
- weights_layers: float32 [2, 7077888], P(None, 'seq')
- weights_other: float32 [2001408], P('seq')
- moment_one_layers: float32 [2, 2, 7077888], P('grp', None, 'seq')
- moment_one_other: float32 [2, 2001408], P('grp', 'seq')
- moment_two_layers: float32 [2, 2, 7077888], P('grp', None, 'seq')
- moment_two_other: float32 [2, 2001408], P('grp', 'seq')
- average_layers: float32 [2, 7077888], P(None, 'seq')
- average_other: float32 [2001408], P('seq')
- momentum_layers: float32 [2, 7077888], P(None, 'seq')
- momentum_other: float32 [2001408], P('seq')
- loss_value: float32 [2], P('grp')
- clip_norm: float32 [2], P('grp')
The draws below stay inside these ranges and needn't reach their ends.
Inputs may be any that keep to these rules, and one draw needn't show every extreme that they name: `lengths`: the 12 items of a group cover its 4096 frames in order; the longest has exactly 512 frames.
All inputs are finite; a program needn't handle non-finite values. No bound on the sum of `null_flags` on one device may be relied on, other than what follows from the above.
Results may differ from the reference program's by a relative error of at most 0.012.
Values may be sent and summed in bfloat16 or wider, within the bound.
A program may use at most 384 MiB of HBM per device.

```python
import functools
import math
import jax
import jax.numpy as jnp
import numpy as np
from jax import lax

D = 768
HEADS = 12
HD = 64
FF = 3072
C = 20
DT = 768
E = 512
L = 2
TSTEPS = 1000
STEP_COUNT = 10
TOK_DEV = 256
ITEM_MAX = 512
FRAMES_G = 4096
FRAMES = 8192
ITEMS = 12
PL = 7077888
PO = 2001408
P_ALL = 16157184
N_GRP = 2
N_SEQ = 16


def draw_base(key, shape):
    return jax.random.truncated_normal(key, -4.0, 4.0, shape, jnp.float32)


def draw_anchor_layers(key, part):
    index = lax.broadcasted_iota(jnp.int32, (L, PL), 1)
    base = draw_base(jax.random.fold_in(key, 11), (L, PL))
    piece = PL // N_SEQ
    cut = D // N_SEQ * (4 * D + FF)
    position = index % piece
    column = position % (4 * D + FF)
    upper_scale = jnp.where(column < 2 * D, 1.4 * D ** (-0.5), jnp.where(column < 3 * D, D ** (-0.5), jnp.where(column < 4 * D, 2.0 * D ** (-0.5), D ** (-0.5))))
    scale = jnp.where(position < cut, upper_scale, FF ** (-0.5))
    return (base * scale).astype(jnp.float32)


def draw_anchor_other(key, part):
    index = lax.broadcasted_iota(jnp.int32, (PO,), 0)
    base = draw_base(jax.random.fold_in(key, 23), (PO,))
    bounds = [C * D, C * D, D * D, DT * D, D * E, DT * E]
    scales = [C ** (-0.5), D ** (-0.5), 0.1 * D ** (-0.5), 0.1 * DT ** (-0.5), D ** (-0.5), DT ** (-0.5)]
    start = 0
    result = base
    for count, scale in zip(bounds, scales):
        inside = (index >= start) & (index < start + count)
        result = jnp.where(inside, base * scale, result)
        start += count
    gain_count = (2 * L + 1) * D
    inside = (index >= start) & (index < start + gain_count)
    result = jnp.where(inside, 1.0 + 0.1 * base, result)
    return result.astype(jnp.float32)


def plant(values, own_key, least, high):
    extent = values.shape
    place = [jax.random.randint(jax.random.fold_in(own_key, axis), (), 0, extent[axis]) for axis in range(len(extent))]
    values = values.at[tuple(place)].set(least)
    longest = extent.index(max(extent))
    place[longest] = (place[longest] + 1) % extent[longest]
    return values.at[tuple(place)].set(high)


def levels(key, shape, shards, least, high):
    def one(dim, blocks):
        steps = jax.random.uniform(jax.random.fold_in(jax.random.fold_in(key, 6), dim), (blocks,), jnp.float32, least / len(shards), high / len(shards))
        return jnp.repeat(jnp.exp(steps), shape[dim] // blocks).reshape((-1,) + (1,) * (len(shape) - dim - 1))

    level = one(*shards[0])
    for cut in shards[1:]:
        level = level * one(*cut)
    return level


def profile(number_of, total, limit, lean):
    portions = [(1 << 20) // math.isqrt(grade ** lean) + 1 for grade in range(2, number_of + 1)]
    spare, holding = total - limit - (number_of - 1), [1] * (number_of - 1)
    while spare > 0:
        free = [i for i in range(number_of - 1) if holding[i] < limit]
        whole, left = sum([portions[i] for i in free]), spare
        for i in free:
            extra = min(limit - holding[i], max(1, left * portions[i] // whole), spare)
            holding[i] = holding[i] + extra
            spare = spare - extra
    return np.array([limit] + holding)


def ragged_sizes(rng, number_of, total, reach, lean):
    if number_of == 2:
        one = jax.random.randint(rng, (), max(1, total - reach), min(reach, total - 1) + 1)
        return jnp.stack([one, total - one])
    sizes = jnp.asarray(profile(number_of, total, reach, lean), jnp.int32)
    twos = (number_of - 1) // 2
    source_of, receiver = sizes[1:1 + 2 * twos:2], sizes[2:2 + 2 * twos:2]
    room = jnp.minimum(source_of - 1, reach - receiver)
    moved = jax.random.randint(jax.random.fold_in(rng, 1), (twos,), 0, 1 << 20) % (room + 1)
    sizes = sizes.at[1:1 + 2 * twos:2].set(source_of - moved).at[2:2 + 2 * twos:2].set(receiver + moved)
    return sizes[jax.random.permutation(jax.random.fold_in(rng, 2), number_of)]


def scatter_about(own_key, dims, width, limit, shards=(), kind=jnp.bfloat16):
    values = jax.random.normal(own_key, dims, jnp.float32) * width
    if len(shards) > 0:
        values = levels(own_key, dims, shards, -0.22, 0.18) * values
    return jnp.clip(values, min=-limit, max=limit).astype(kind)


def setup_inputs(seed: int = 0) -> dict:
    key_list = jax.random.split(jax.random.key(seed), 15)
    return {
        "anchor_layers": draw_anchor_layers(jax.random.fold_in(key_list[14], 71), 0),
        "anchor_other": draw_anchor_other(jax.random.fold_in(key_list[14], 71), 0),
        "first_layers": scatter_about(key_list[2], (N_GRP, L, PL), (0.00111 / P_ALL ** 0.5), 3.814697265625e-06, ((0, 2), (2, 16)), jnp.float32),
        "first_other": scatter_about(key_list[3], (N_GRP, PO), (0.00111 / P_ALL ** 0.5), 3.814697265625e-06, ((0, 2), (1, 16)), jnp.float32),
        "second_layers": jnp.clip(jnp.exp(math.log(1.2997314812954186e-12) - 1.3843914 * jax.random.uniform(key_list[4], (N_GRP, L, PL), jnp.float32) ** levels(key_list[4], (N_GRP, L, PL), ((0, 2), (2, 16)), -0.2, 0.2)), 3.25551787134018e-13, 1.2997314812954186e-12),
        "second_other": jnp.clip(jnp.exp(math.log(1.2997314812954186e-12) - 1.3843914 * jax.random.uniform(key_list[5], (N_GRP, PO), jnp.float32) ** levels(key_list[5], (N_GRP, PO), ((0, 2), (1, 16)), -0.2, 0.2)), 3.25551787134018e-13, 1.2997314812954186e-12),
        "outer_layers": scatter_about(key_list[6], (L, PL), 0.01, 0.15625, ((1, 16),), jnp.float32),
        "outer_other": scatter_about(key_list[7], (PO,), 0.01, 0.15625, ((0, 16),), jnp.float32),
        "latents": scatter_about(key_list[8], (FRAMES, C), 1.0, 6.0, ((0, 32),), jnp.float32),
        "noise": scatter_about(key_list[9], (FRAMES, C), 1.0, 6.0, ((0, 32),), jnp.float32),
        "lengths": jax.vmap(lambda own: ragged_sizes(own, ITEMS, FRAMES_G, ITEM_MAX, 1))(jax.random.split(key_list[10], N_GRP)).reshape((N_GRP, ITEMS)).astype(jnp.int32),
        "timesteps": plant(jax.random.randint(key_list[11], (N_GRP, ITEMS), 0, TSTEPS), jax.random.fold_in(key_list[11], 1), 0, TSTEPS - 1).astype(jnp.int32),
        "null_flags": plant((jax.random.randint(key_list[12], (N_GRP, ITEMS), 0, 5) < 1).astype(jnp.int32), jax.random.fold_in(key_list[12], 1), 0, 1),
        "captions": scatter_about(key_list[13], (N_GRP, ITEMS, DT), 1.0, 6.0, ((0, 2),), jnp.float32),
    }


HIGH = lax.Precision.HIGHEST
beta_one = 0.9
beta_two = 0.95
adam_eps = 1e-08
decay_rate = 0.01
inner_rate = 0.02
outer_rate = 0.7
outer_mu = 0.9
clip_at = 0.01
logit_scale = 30.0
contrast_weight = 0.05

@jax.custom_vjp
def low(v):
    return lax.optimization_barrier(v.astype(jnp.bfloat16)).astype(jnp.float32)

@jax.custom_vjp
def low_back(v):
    return v

def low_keep(v):
    return (low(v), None)

def low_pass(kept, grad):
    return (grad,)

def back_keep(v):
    return (v, None)

def back_low(kept, grad):
    return (low(grad),)
low.defvjp(low_keep, low_pass)
low_back.defvjp(back_keep, back_low)

def matmul(left, right):
    return jnp.dot(left, right, precision=HIGH, preferred_element_type=jnp.float32)

def carve(flat, shapes):
    pieces = []
    start = 0
    for shape in shapes:
        count = math.prod(shape)
        pieces.append(flat[start:start + count].reshape(shape))
        start += count
    return pieces

def carve_layer(flat):
    pieces = flat.reshape(N_SEQ, PL // N_SEQ)
    cut = D // N_SEQ * (4 * D + FF)
    upper = pieces[:, :cut].reshape(D, 4 * D + FF)
    lower = pieces[:, cut:].reshape(FF, D)
    return [upper[:, :3 * D], upper[:, 3 * D:4 * D], upper[:, 4 * D:], lower]

def other_shapes():
    return [(C, D), (D, C), (D, D), (DT, D), (D, E), (DT, E), (2 * L + 1, D), (DT,)]

def norm_rows(hidden, gain):
    centred = hidden - lax.optimization_barrier(jnp.mean(hidden, axis=-1, keepdims=True))
    return centred * lax.rsqrt(lax.optimization_barrier(jnp.mean(centred * centred, axis=-1, keepdims=True)) + 1e-05) * gain

def plan(steps):
    angle = (steps.astype(jnp.float32) / TSTEPS + 0.008) / 1.008 * (math.pi / 2)
    return jnp.cos(angle) ** 2

def time_features(steps):
    half = D // 2
    frequency = jnp.exp(-math.log(10000.0) * jnp.arange(half, dtype=jnp.float32) / half)
    angle = steps.astype(jnp.float32)[:, None] * frequency[None, :]
    return jnp.concatenate([jnp.cos(angle), jnp.sin(angle)], axis=1)

def contrast(audio_side, text_side):
    audio_unit = audio_side * lax.rsqrt(lax.optimization_barrier(jnp.sum(audio_side * audio_side, axis=-1, keepdims=True)) + 1e-06)
    text_unit = text_side * lax.rsqrt(lax.optimization_barrier(jnp.sum(text_side * text_side, axis=-1, keepdims=True)) + 1e-06)
    logits = logit_scale * jnp.dot(audio_unit, text_unit.T, precision=HIGH)
    diagonal = logit_scale * lax.optimization_barrier(jnp.sum(audio_unit * text_unit, axis=-1))
    row_terms = jax.nn.logsumexp(logits, axis=1) - diagonal
    column_terms = jax.nn.logsumexp(logits, axis=0) - diagonal
    return 0.5 * (jnp.mean(row_terms) + jnp.mean(column_terms))

def attend(projected, item):
    frames = projected.shape[0]
    margin = 2 * TOK_DEV
    queries = projected[:, :D]
    padded = jnp.pad(projected[:, D:], ((margin, margin), (0, 0)))
    key_item = jnp.pad(item, (margin, margin), constant_values=-1)

    def block(start):
        query = lax.dynamic_slice_in_dim(queries, start, TOK_DEV).reshape(TOK_DEV, HEADS, HD)
        window = lax.dynamic_slice_in_dim(padded, start, 5 * TOK_DEV)
        keys = window[:, :D].reshape(5 * TOK_DEV, HEADS, HD)
        values = window[:, D:].reshape(5 * TOK_DEV, HEADS, HD)
        query_item = lax.dynamic_slice_in_dim(item, start, TOK_DEV)
        window_item = lax.dynamic_slice_in_dim(key_item, start, 5 * TOK_DEV)
        scores = low_back(jnp.einsum('qhd,khd->hqk', query, keys, precision=HIGH) * HD ** (-0.5))
        keep = (query_item[:, None] == window_item[None, :])[None]
        scores = jnp.where(keep, scores, -1e+30)
        shares = low(jax.nn.softmax(scores, axis=-1))
        return jnp.einsum('hqk,khd->qhd', shares, values, precision=HIGH).reshape(TOK_DEV, D)
    starts = (jnp.arange(frames // TOK_DEV) * TOK_DEV).astype(jnp.int32)
    return lax.map(jax.checkpoint(block), starts).reshape(frames, D)

def layer_forward(hidden, weights, gain_one, gain_two, item):
    proj_qkv, proj_out, proj_up, proj_down = weights
    normed = low(norm_rows(hidden, gain_one))
    projected = low(low_back(matmul(normed, proj_qkv)))
    attended = low(low_back(attend(projected, item)))
    middle = hidden + low_back(matmul(attended, proj_out))
    second = low(norm_rows(middle, gain_two))
    upper = low_back(matmul(second, proj_up))
    activated = low(jax.nn.gelu(upper, approximate=True))
    return middle + low_back(matmul(activated, proj_down))

def forward_group(layers, others, latents, noise, lengths, steps, flags, captions):
    w_in, w_out, w_time, w_text, w_audio, w_caption, gains, null_text = carve(others, other_shapes())
    places = jnp.arange(FRAMES_G, dtype=jnp.int32)
    ends = jnp.cumsum(lengths).astype(jnp.int32)
    item = lax.optimization_barrier(jnp.sum((places[:, None] >= ends[None, :]).astype(jnp.int32), axis=1)).astype(jnp.int32)
    onehot = (item[:, None] == jnp.arange(ITEMS, dtype=jnp.int32)[None, :]).astype(jnp.float32)
    alpha_bar = plan(steps)
    mixing = matmul(onehot, jnp.stack([jnp.sqrt(alpha_bar), jnp.sqrt(1.0 - alpha_bar)], axis=1))
    noisy = mixing[:, 0:1] * latents + mixing[:, 1:2] * noise
    text = jnp.where(flags[:, None] == 1, null_text[None, :], captions)
    condition = jax.nn.silu(matmul(time_features(steps), w_time) + matmul(text, w_text))
    hidden = matmul(low(noisy), w_in) + matmul(onehot, condition)
    for depth in range(L):
        hidden = layer_forward(hidden, carve_layer(layers[depth]), gains[2 * depth], gains[2 * depth + 1], item)
    final = norm_rows(hidden, gains[2 * L])
    predicted = low_back(matmul(low(final), w_out))
    error = predicted - noise
    squared = jnp.sum(error * error) / (FRAMES_G * C)
    pooled = matmul(onehot.T, final) / lengths[:, None].astype(jnp.float32)
    clash = contrast(matmul(pooled, w_audio), matmul(captions, w_caption))
    return squared + contrast_weight * clash

def adam(grad, first, second, anchor):
    first = beta_one * first + (1.0 - beta_one) * grad
    second = beta_two * second + (1.0 - beta_two) * grad * grad
    stepped = first / (1.0 - beta_one ** STEP_COUNT)
    scaled = second / (1.0 - beta_two ** STEP_COUNT)
    delta = inner_rate * (stepped / (jnp.sqrt(scaled) + adam_eps) + decay_rate * anchor)
    return (first, second, delta)

def reference(anchor_layers, anchor_other, first_layers, first_other, second_layers, second_other, outer_layers, outer_other, latents, noise, lengths, timesteps, null_flags, captions):
    layers_low = low(anchor_layers)
    others_low = low(anchor_other)
    firsts_l, firsts_o, seconds_l, seconds_o, deltas_l, deltas_o, losses, norms = ([], [], [], [], [], [], [], [])
    for group in range(N_GRP):
        lower = group * FRAMES_G
        objective = functools.partial(forward_group, latents=latents[lower:lower + FRAMES_G], noise=noise[lower:lower + FRAMES_G], lengths=lengths[group], steps=timesteps[group], flags=null_flags[group], captions=captions[group])
        loss, pull = jax.vjp(objective, layers_low, others_low)
        grad_layers, grad_other = pull(jnp.ones_like(loss))
        total_norm = jnp.sqrt(jnp.sum(grad_layers * grad_layers) + jnp.sum(grad_other * grad_other))
        factor = jnp.minimum(1.0, clip_at / (total_norm + 1e-06))
        first_l, second_l, delta_l = adam(grad_layers * factor, first_layers[group], second_layers[group], anchor_layers)
        first_o, second_o, delta_o = adam(grad_other * factor, first_other[group], second_other[group], anchor_other)
        firsts_l.append(first_l)
        firsts_o.append(first_o)
        seconds_l.append(second_l)
        seconds_o.append(second_o)
        deltas_l.append(delta_l)
        deltas_o.append(delta_o)
        losses.append(loss)
        norms.append(total_norm)
    mean_layers = functools.reduce(lambda a, b: a + b, deltas_l) / N_GRP
    mean_other = functools.reduce(lambda a, b: a + b, deltas_o) / N_GRP
    momentum_layers = outer_mu * outer_layers + mean_layers
    momentum_other = outer_mu * outer_other + mean_other
    new_layers = anchor_layers - outer_rate * (mean_layers + outer_mu * momentum_layers)
    new_other = anchor_other - outer_rate * (mean_other + outer_mu * momentum_other)
    return (new_layers, new_other, jnp.stack(firsts_l), jnp.stack(firsts_o), jnp.stack(seconds_l), jnp.stack(seconds_o), mean_layers, mean_other, momentum_layers, momentum_other, jnp.stack(losses), jnp.stack(norms))
```

```python
import math

import jax
import jax.numpy as jnp
from jax import lax
from jax.sharding import PartitionSpec as P

D = 768
HEADS = 12
HD = 64
FF = 3072
E = 512
L = 2
TSTEPS = 1000
STEP_COUNT = 10


HIGH = lax.Precision.HIGHEST
beta_one = 0.9
beta_two = 0.95
adam_eps = 1e-08
decay_rate = 0.01
inner_rate = 0.02
outer_rate = 0.7
outer_mu = 0.9
clip_at = 0.01
logit_scale = 30.0
contrast_weight = 0.05


def passed_along(value, axis, steps):
    count = lax.axis_size(axis)
    initial, last = (max(0, -steps), min(count, count - steps))
    return lax.ppermute(value, axis, [(source, source + steps) for source in range(initial, last)])


def dense(left, right):
    return jnp.dot(left, right, preferred_element_type=jnp.float32)


def exact(left, right):
    return jnp.dot(left, right, precision=HIGH, preferred_element_type=jnp.float32)


def contract_rows(left, right, precision=None):
    return lax.dot_general(
        left,
        right,
        (((0,), (0,)), ((), ())),
        precision=precision,
        preferred_element_type=jnp.float32,
    )


def against_rows(left, right, precision=None):
    return lax.dot_general(
        left,
        right,
        (((1,), (1,)), ((), ())),
        precision=precision,
        preferred_element_type=jnp.float32,
    )


def carve(flat, shapes):
    pieces = []
    start = 0
    for shape in shapes:
        count = math.prod(shape)
        pieces.append(flat[start : start + count].reshape(shape))
        start += count
    return pieces


def carve_layer(flat, shards):
    pieces = flat.reshape(shards, -1)
    cut = D // shards * (4 * D + FF)
    upper = pieces[:, :cut].reshape(D, 4 * D + FF)
    lower = pieces[:, cut:].reshape(FF, D)
    return [upper[:, : 3 * D], upper[:, 3 * D : 4 * D], upper[:, 4 * D :], lower]


def other_shapes(channels, width, text_width, joint_width, blocks):
    return [
        (channels, width),
        (width, channels),
        (width, width),
        (text_width, width),
        (width, joint_width),
        (text_width, joint_width),
        (2 * blocks + 1, width),
        (text_width,),
    ]


def norm_rows(hidden, gain):
    centred = hidden - jnp.mean(hidden, axis=-1, keepdims=True)
    return centred * lax.rsqrt(jnp.mean(centred * centred, axis=-1, keepdims=True) + 1e-05) * gain


def plan(steps):
    angle = (steps.astype(jnp.float32) / TSTEPS + 0.008) / 1.008 * (math.pi / 2)
    return jnp.cos(angle) ** 2


def time_features(steps):
    half = D // 2
    frequency = jnp.exp(-math.log(10000.0) * jnp.arange(half, dtype=jnp.float32) / half)
    angle = steps.astype(jnp.float32)[:, None] * frequency[None, :]
    return jnp.concatenate([jnp.cos(angle), jnp.sin(angle)], axis=1)


def contrast(audio_side, text_side):
    audio_unit = audio_side * lax.rsqrt(
        jnp.sum(audio_side * audio_side, axis=-1, keepdims=True) + 1e-06
    )
    text_unit = text_side * lax.rsqrt(
        jnp.sum(text_side * text_side, axis=-1, keepdims=True) + 1e-06
    )
    logits = logit_scale * jnp.dot(audio_unit, text_unit.T, precision=HIGH)
    diagonal = logit_scale * jnp.sum(audio_unit * text_unit, axis=-1)
    row_terms = jax.nn.logsumexp(logits, axis=1) - diagonal
    column_terms = jax.nn.logsumexp(logits, axis=0) - diagonal
    return 0.5 * (jnp.mean(row_terms) + jnp.mean(column_terms))


def split_heads(rows_in):
    return rows_in.reshape(rows_in.shape[0], HEADS, HD).transpose(1, 0, 2)


def join_heads(heads_in):
    return heads_in.transpose(1, 0, 2).reshape(heads_in.shape[1], HEADS * HD)


def gather_window(local_pairs):
    pieces = {}
    for step in (2, 1, -1, -2):
        pieces[step] = passed_along(local_pairs, "seq", step)
    return jnp.concatenate([pieces[2], pieces[1], local_pairs, pieces[-1], pieces[-2]], axis=0)


def return_window(grad_window, rows):
    total = grad_window[2 * rows : 3 * rows]
    for slot, step in ((0, 2), (1, 1), (3, -1), (4, -2)):
        total = total + passed_along(
            grad_window[slot * rows : (slot + 1) * rows].astype(jnp.bfloat16), "seq", -step
        ).astype(jnp.float32)
    return total


def attend_forward(queries, keys, values, keep):
    scale = HD ** (-0.5)

    def one_head(operands):
        query, key_rows, value_rows = operands
        scores = jnp.where(keep, against_rows(query, key_rows) * scale, -1e30)
        peak = jnp.max(scores, axis=-1, keepdims=True)
        weights = jnp.exp(scores - peak)
        total = jnp.sum(weights, axis=-1, keepdims=True)
        shares = (weights / total).astype(jnp.bfloat16)
        return (dense(shares, value_rows), peak[:, 0], total[:, 0])

    outputs, peaks, totals = lax.map(
        one_head, (split_heads(queries), split_heads(keys), split_heads(values))
    )
    return (join_heads(outputs), peaks, totals)


def attend_backward(queries, keys, values, keep, peaks, totals, grad_out):
    scale = HD ** (-0.5)

    def one_head(operands):
        query, key_rows, value_rows, peak, total, grad_head = operands
        scores = jnp.where(keep, against_rows(query, key_rows) * scale, -1e30)
        shares = jnp.exp(scores - peak[:, None]) / total[:, None]
        grad_value = contract_rows(shares.astype(jnp.bfloat16), grad_head)
        grad_shares = against_rows(grad_head, value_rows)
        inner = jnp.sum(grad_shares * shares, axis=-1, keepdims=True)
        grad_scores = (shares * (grad_shares - inner)).astype(jnp.bfloat16)
        grad_query = dense(grad_scores, key_rows) * scale
        grad_key = contract_rows(grad_scores, query) * scale
        return (grad_query, grad_key, grad_value)

    grad_query, grad_key, grad_value = lax.map(
        one_head,
        (
            split_heads(queries),
            split_heads(keys),
            split_heads(values),
            peaks,
            totals,
            split_heads(grad_out),
        ),
    )
    return (join_heads(grad_query), join_heads(grad_key), join_heads(grad_value))


def layer_forward(hidden, weights, gain_one, gain_two, keep):
    proj_qkv, proj_out, proj_up, proj_down = weights
    width = proj_out.shape[0]
    normed = norm_rows(hidden, gain_one).astype(jnp.bfloat16)
    projected = dense(normed, proj_qkv).astype(jnp.bfloat16)
    window = gather_window(projected[:, width:])
    attended, peaks, totals = attend_forward(
        projected[:, :width], window[:, :width], window[:, width:], keep
    )
    attended = attended.astype(jnp.bfloat16)
    middle = hidden + dense(attended, proj_out)
    second = norm_rows(middle, gain_two).astype(jnp.bfloat16)
    upper = dense(second, proj_up)
    activated = jax.nn.gelu(upper, approximate=True).astype(jnp.bfloat16)
    return (
        middle + dense(activated, proj_down),
        (
            hidden,
            normed,
            projected,
            window,
            peaks,
            totals,
            attended,
            middle,
            second,
            upper,
            activated,
        ),
    )


def layer_backward(grad_hidden, weights, gain_one, gain_two, keep, saved):
    hidden, normed, projected, window, peaks, totals, attended, middle, second, upper, activated = (
        saved
    )
    proj_qkv, proj_out, proj_up, proj_down = weights
    width = proj_out.shape[0]
    rows = hidden.shape[0]
    branch_top = grad_hidden.astype(jnp.bfloat16)
    grad_activated = against_rows(branch_top, proj_down)
    unused, pull_gelu = jax.vjp(lambda value: jax.nn.gelu(value, approximate=True), upper)
    grad_upper = pull_gelu(grad_activated)[0].astype(jnp.bfloat16)
    grad_second = against_rows(grad_upper, proj_up)
    unused, pull_two = jax.vjp(norm_rows, middle, gain_two)
    grad_middle, grad_gain_two = pull_two(grad_second)
    grad_middle = grad_middle + grad_hidden
    branch_mid = grad_middle.astype(jnp.bfloat16)
    grad_attended = against_rows(branch_mid, proj_out).astype(jnp.bfloat16)
    grad_query, grad_keys, grad_values = attend_backward(
        projected[:, :width],
        window[:, :width],
        window[:, width:],
        keep,
        peaks,
        totals,
        grad_attended,
    )
    grad_pairs = return_window(jnp.concatenate([grad_keys, grad_values], axis=1), rows)
    grad_projected = jnp.concatenate([grad_query, grad_pairs], axis=1).astype(jnp.bfloat16)
    grad_normed = against_rows(grad_projected, proj_qkv)
    unused, pull_one = jax.vjp(norm_rows, hidden, gain_one)
    grad_input, grad_gain_one = pull_one(grad_normed)
    operand_pairs = (
        normed,
        grad_projected,
        attended,
        branch_mid,
        second,
        grad_upper,
        activated,
        branch_top,
    )
    return (grad_middle + grad_input, operand_pairs, grad_gain_one, grad_gain_two)


def reduce_layer(operand_pairs, shards):
    normed, grad_projected, attended, branch_mid, second, grad_upper, activated, branch_top = (
        operand_pairs
    )
    upper_full = jnp.concatenate(
        [
            contract_rows(normed, grad_projected),
            contract_rows(attended, branch_mid),
            contract_rows(second, grad_upper),
        ],
        axis=1,
    )
    lower_full = contract_rows(activated, branch_top)
    flat_grad = jnp.concatenate(
        [upper_full.reshape(shards, -1), lower_full.reshape(shards, -1)], axis=1
    ).reshape(-1)
    return lax.psum_scatter(flat_grad, "seq", scatter_dimension=0, tiled=True)


def adam(grad, first, second, anchor):
    first = beta_one * first + (1.0 - beta_one) * grad
    second = beta_two * second + (1.0 - beta_two) * grad * grad
    stepped = first / (1.0 - beta_one**STEP_COUNT)
    scaled = second / (1.0 - beta_two**STEP_COUNT)
    delta = inner_rate * (stepped / (jnp.sqrt(scaled) + adam_eps) + decay_rate * anchor)
    return (first, second, delta)


def per_device(
    anchor_layers,
    anchor_other,
    first_layers,
    first_other,
    second_layers,
    second_other,
    outer_layers,
    outer_other,
    latents,
    noise,
    lengths,
    timesteps,
    null_flags,
    captions,
):
    seq_count = lax.axis_size("seq")
    group_count = lax.axis_size("grp")
    rank = lax.axis_index("seq")
    rows = latents.shape[0]
    channels = latents.shape[1]
    frames_group = rows * seq_count
    lengths = lengths[0]
    timesteps = timesteps[0]
    null_flags = null_flags[0]
    captions = captions[0]
    item_count = lengths.shape[0]
    text_width = captions.shape[1]
    other_low = lax.all_gather(anchor_other.astype(jnp.bfloat16), "seq", axis=0, tiled=True)
    w_in, w_out, w_time, w_text, w_audio, w_caption, gains, null_text = carve(
        other_low, other_shapes(channels, D, text_width, E, L)
    )
    w_time_f = w_time.astype(jnp.float32)
    w_text_f = w_text.astype(jnp.float32)
    w_audio_f = w_audio.astype(jnp.float32)
    w_caption_f = w_caption.astype(jnp.float32)
    gains_f = gains.astype(jnp.float32)
    null_f = null_text.astype(jnp.float32)
    places = rank * rows + jnp.arange(rows, dtype=jnp.int32)
    order = jnp.arange(item_count, dtype=jnp.int32)
    ends = jnp.sum(jnp.where(order[None, :] <= order[:, None], lengths[None, :], 0), axis=1)
    starts = ends - lengths
    item = jnp.sum((places[:, None] >= ends[None, :]).astype(jnp.int32), axis=1)
    onehot = (item[:, None] == jnp.arange(item_count, dtype=jnp.int32)[None, :]).astype(jnp.float32)
    key_places = rank * rows + jnp.arange(-2 * rows, 3 * rows, dtype=jnp.int32)
    key_item = jnp.sum((key_places[:, None] >= ends[None, :]).astype(jnp.int32), axis=1)
    key_item = jnp.where((key_places >= 0) & (key_places < frames_group), key_item, -1)
    keep = item[:, None] == key_item[None, :]
    lengths_f = lengths[:, None].astype(jnp.float32)
    alpha_bar = plan(timesteps)
    mixing = exact(onehot, jnp.stack([jnp.sqrt(alpha_bar), jnp.sqrt(1.0 - alpha_bar)], axis=1))
    noisy_low = (mixing[:, 0:1] * latents + mixing[:, 1:2] * noise).astype(jnp.bfloat16)
    features = time_features(timesteps)

    def condition_of(time_weight, text_weight, null_vector):
        text = jnp.where(null_flags[:, None] == 1, null_vector[None, :], captions)
        return jax.nn.silu(exact(features, time_weight) + exact(text, text_weight))

    condition, pull_condition = jax.vjp(condition_of, w_time_f, w_text_f, null_f)
    hidden = dense(noisy_low, w_in) + exact(onehot, condition)
    saved_all = []
    for depth in range(L):
        flat = lax.all_gather(anchor_layers[depth].astype(jnp.bfloat16), "seq", axis=0, tiled=True)
        weights = carve_layer(flat, seq_count)
        hidden, saved = layer_forward(
            hidden, weights, gains_f[2 * depth], gains_f[2 * depth + 1], keep
        )
        saved_all.append(saved)
    final = norm_rows(hidden, gains_f[2 * L])
    final_low = final.astype(jnp.bfloat16)
    predicted = dense(final_low, w_out)
    error = predicted - noise
    part_pool = contract_rows(onehot, final, HIGH)
    squared_sum, pool_sum = lax.psum((jnp.sum(error * error), part_pool), "seq")
    pooled = pool_sum / lengths_f
    audio_side = exact(pooled, w_audio_f)
    text_side = exact(captions, w_caption_f)
    clash, pull_clash = jax.vjp(contrast, audio_side, text_side)
    loss = squared_sum / (frames_group * channels) + contrast_weight * clash
    grad_audio_side, grad_text_side = pull_clash(jnp.float32(contrast_weight))
    grad_pred = (2.0 / (frames_group * channels) * error).astype(jnp.bfloat16)
    grad_w_out = contract_rows(final_low, grad_pred)
    grad_w_audio = contract_rows(part_pool / lengths_f, grad_audio_side, HIGH)
    first_here = ((starts >= rank * rows) & (starts < rank * rows + rows)).astype(jnp.float32)
    grad_w_caption = contract_rows(captions * first_here[:, None], grad_text_side, HIGH)
    grad_pooled = against_rows(grad_audio_side, w_audio_f, HIGH) / lengths_f
    grad_final = against_rows(grad_pred, w_out) + exact(onehot, grad_pooled)
    unused, pull_final = jax.vjp(norm_rows, hidden, gains_f[2 * L])
    grad_hidden, grad_gain_final = pull_final(grad_final)
    layer_grads = [None] * L
    gain_grads = [None] * (2 * L + 1)
    gain_grads[2 * L] = grad_gain_final
    for depth in reversed(range(L)):
        flat = lax.all_gather(anchor_layers[depth].astype(jnp.bfloat16), "seq", axis=0, tiled=True)
        weights = carve_layer(flat, seq_count)
        grad_hidden, operand_pairs, grad_gain_one, grad_gain_two = layer_backward(
            grad_hidden, weights, gains_f[2 * depth], gains_f[2 * depth + 1], keep, saved_all[depth]
        )
        gain_grads[2 * depth] = grad_gain_one
        gain_grads[2 * depth + 1] = grad_gain_two
        layer_grads[depth] = reduce_layer(operand_pairs, seq_count)
    stacked = jnp.stack(layer_grads)
    grad_w_in = contract_rows(noisy_low.astype(jnp.float32), grad_hidden, HIGH)
    grad_condition = contract_rows(onehot, grad_hidden, HIGH)
    grad_w_time, grad_w_text, grad_null = pull_condition(grad_condition)
    other_flat = jnp.concatenate(
        [
            grad_w_in.ravel(),
            grad_w_out.ravel(),
            grad_w_time.ravel(),
            grad_w_text.ravel(),
            grad_w_audio.ravel(),
            grad_w_caption.ravel(),
            jnp.stack(gain_grads).ravel(),
            grad_null,
        ]
    )
    other_grad = lax.psum_scatter(other_flat, "seq", scatter_dimension=0, tiled=True)
    square_part = jnp.sum(stacked * stacked) + jnp.sum(other_grad * other_grad)
    total_norm = jnp.sqrt(lax.psum(square_part, "seq"))
    factor = jnp.minimum(1.0, clip_at / (total_norm + 1e-06))
    first_l, second_l, delta_l = adam(
        stacked * factor, first_layers[0], second_layers[0], anchor_layers
    )
    first_o, second_o, delta_o = adam(
        other_grad * factor, first_other[0], second_other[0], anchor_other
    )
    share_l, share_o = (
        lax.psum_scatter(
            delta_l.astype(jnp.bfloat16), "grp", scatter_dimension=1, tiled=True
        ).astype(jnp.float32),
        lax.psum_scatter(
            delta_o.astype(jnp.bfloat16), "grp", scatter_dimension=0, tiled=True
        ).astype(jnp.float32),
    )
    summed_l, summed_o = (
        lax.all_gather(share_l.astype(jnp.bfloat16), "grp", axis=1, tiled=True).astype(
            share_l.dtype
        ),
        lax.all_gather(share_o.astype(jnp.bfloat16), "grp", axis=0, tiled=True).astype(
            share_o.dtype
        ),
    )
    mean_layers = summed_l / group_count
    mean_other = summed_o / group_count
    momentum_layers = outer_mu * outer_layers + mean_layers
    momentum_other = outer_mu * outer_other + mean_other
    new_layers = anchor_layers - outer_rate * (mean_layers + outer_mu * momentum_layers)
    new_other = anchor_other - outer_rate * (mean_other + outer_mu * momentum_other)
    return (
        new_layers,
        new_other,
        first_l[None],
        first_o[None],
        second_l[None],
        second_o[None],
        mean_layers,
        mean_other,
        momentum_layers,
        momentum_other,
        loss.reshape(1),
        total_norm.reshape(1),
    )


def solution(mesh):
    placed = (
        P(None, "seq"),
        P("seq"),
        P("grp", None, "seq"),
        P("grp", "seq"),
        P("grp", None, "seq"),
        P("grp", "seq"),
        P(None, "seq"),
        P("seq"),
        P(("grp", "seq"), None),
        P(("grp", "seq"), None),
        P("grp", None),
        P("grp", None),
        P("grp", None),
        P("grp", None, None),
    )
    return jax.shard_map(
        per_device,
        mesh=mesh,
        in_specs=placed,
        out_specs=(
            P(None, "seq"),
            P("seq"),
            P("grp", None, "seq"),
            P("grp", "seq"),
            P("grp", None, "seq"),
            P("grp", "seq"),
            P(None, "seq"),
            P("seq"),
            P(None, "seq"),
            P("seq"),
            P("grp"),
            P("grp"),
        ),
        check_vma=False,
    )
```

```python
import functools
import math

import jax
import jax.numpy as jnp
from jax import lax
from jax.experimental import pallas as pl
from jax.experimental.pallas import tpu as pltpu
from jax.sharding import PartitionSpec as P

D = 768
HEADS = 12
HD = 64
FF = 3072
E = 512
L = 2
TSTEPS = 1000
STEP_COUNT = 10


HIGH = lax.Precision.HIGHEST
beta_one = 0.9
beta_two = 0.95
adam_eps = 1e-08
decay_rate = 0.01
inner_rate = 0.02
outer_rate = 0.7
outer_mu = 0.9
clip_at = 0.01
logit_scale = 30.0
contrast_weight = 0.05


def passed_along(value, axis, steps):
    count = lax.axis_size(axis)
    initial, last = (max(0, -steps), min(count, count - steps))
    return lax.ppermute(value, axis, [(source, source + steps) for source in range(initial, last)])


def dense(left, right):
    return jnp.dot(left, right, preferred_element_type=jnp.float32)


def exact(left, right):
    return jnp.dot(left, right, precision=HIGH, preferred_element_type=jnp.float32)


def contract_rows(left, right, precision=None):
    return lax.dot_general(
        left,
        right,
        (((0,), (0,)), ((), ())),
        precision=precision,
        preferred_element_type=jnp.float32,
    )


def against_rows(left, right, precision=None):
    return lax.dot_general(
        left,
        right,
        (((1,), (1,)), ((), ())),
        precision=precision,
        preferred_element_type=jnp.float32,
    )


def carve(flat, shapes):
    pieces = []
    start = 0
    for shape in shapes:
        count = math.prod(shape)
        pieces.append(flat[start : start + count].reshape(shape))
        start += count
    return pieces


def layer_rows(piece, shards):
    cut = D // shards * (4 * D + FF)
    return piece[:cut].reshape(D // shards, 4 * D + FF), piece[cut:].reshape(FF // shards, D)


def gather_layer(anchor, shards):
    upper, lower = layer_rows(anchor.astype(jnp.bfloat16), shards)
    upper = lax.all_gather(upper, "seq", axis=0, tiled=True)
    lower = lax.all_gather(lower, "seq", axis=0, tiled=True)
    return [upper[:, : 3 * D], upper[:, 3 * D : 4 * D], upper[:, 4 * D :], lower]


def other_shapes(channels, width, text_width, joint_width, blocks):
    return [
        (channels, width),
        (width, channels),
        (width, width),
        (text_width, width),
        (width, joint_width),
        (text_width, joint_width),
        (2 * blocks + 1, width),
        (text_width,),
    ]


def norm_rows(hidden, gain):
    centred = hidden - jnp.mean(hidden, axis=-1, keepdims=True)
    return centred * lax.rsqrt(jnp.mean(centred * centred, axis=-1, keepdims=True) + 1e-05) * gain


def plan(steps):
    angle = (steps.astype(jnp.float32) / TSTEPS + 0.008) / 1.008 * (math.pi / 2)
    return jnp.cos(angle) ** 2


def time_features(steps):
    half = D // 2
    frequency = jnp.exp(-math.log(10000.0) * jnp.arange(half, dtype=jnp.float32) / half)
    angle = steps.astype(jnp.float32)[:, None] * frequency[None, :]
    return jnp.concatenate([jnp.cos(angle), jnp.sin(angle)], axis=1)


def contrast(audio_side, text_side):
    audio_unit = audio_side * lax.rsqrt(
        jnp.sum(audio_side * audio_side, axis=-1, keepdims=True) + 1e-06
    )
    text_unit = text_side * lax.rsqrt(
        jnp.sum(text_side * text_side, axis=-1, keepdims=True) + 1e-06
    )
    logits = logit_scale * jnp.dot(audio_unit, text_unit.T, precision=HIGH)
    diagonal = logit_scale * jnp.sum(audio_unit * text_unit, axis=-1)
    row_terms = jax.nn.logsumexp(logits, axis=1) - diagonal
    column_terms = jax.nn.logsumexp(logits, axis=0) - diagonal
    return 0.5 * (jnp.mean(row_terms) + jnp.mean(column_terms))


def gather_window(local_pairs):
    pieces = {}
    for step in (2, 1, -1, -2):
        pieces[step] = passed_along(local_pairs, "seq", step)
    return jnp.concatenate([pieces[2], pieces[1], local_pairs, pieces[-1], pieces[-2]], axis=0)


def return_window(grad_window, rows):
    total = grad_window[2 * rows : 3 * rows].astype(jnp.float32)
    for slot, step in ((0, 2), (1, 1), (3, -1), (4, -2)):
        total = total + passed_along(
            grad_window[slot * rows : (slot + 1) * rows], "seq", -step
        ).astype(jnp.float32)
    return total


LANES = 128
PAIRS = HEADS * HD // LANES
VMEM_LIMIT = 50 * 1024 * 1024


def lane_masks(dtype):
    lane = lax.broadcasted_iota(jnp.int32, (1, LANES), 1)
    return [(lane < HD).astype(dtype), (lane >= HD).astype(dtype)]


def fill_bias(bias_ref, query_item_ref, key_item_ref):
    keep = key_item_ref[...] == query_item_ref[...]
    bias_ref[...] = jnp.where(keep, 0.0, -1e30).astype(jnp.float32)


def attend_forward_kernel(q_ref, kv_ref, query_item_ref, key_item_ref, o_ref, lse_ref, bias_ref):
    fill_bias(bias_ref, query_item_ref, key_item_ref)
    width = HEADS * HD
    masks = lane_masks(jnp.bfloat16)
    lse_ref[...] = jnp.zeros_like(lse_ref)
    for pair in range(PAIRS):
        cols = slice(pair * LANES, (pair + 1) * LANES)
        query = q_ref[:, cols] * jnp.bfloat16(HD ** (-0.5))
        key_rows = kv_ref[:, cols]
        value_rows = kv_ref[:, width + pair * LANES : width + (pair + 1) * LANES]
        halves = []
        for half in range(2):
            scores = against_rows(key_rows, query * masks[half]) + bias_ref[...]
            peak = jnp.max(scores, axis=0, keepdims=True)
            weights = jnp.exp(scores - peak)
            total = jnp.sum(weights, axis=0, keepdims=True)
            shares = (weights * (1.0 / total)).astype(jnp.bfloat16)
            mixed = contract_rows(value_rows, shares)
            halves.append(mixed[half * HD : (half + 1) * HD])
            lse_ref[2 * pair + half : 2 * pair + half + 1, :] = peak + jnp.log(total)
        o_ref[:, cols] = jnp.concatenate(halves, axis=0).T.astype(o_ref.dtype)


def attend_forward(queries, window, query_item, key_item):
    rows, width = queries.shape
    span = window.shape[0]
    return pl.pallas_call(
        attend_forward_kernel,
        out_shape=(
            jax.ShapeDtypeStruct((rows, width), jnp.bfloat16),
            jax.ShapeDtypeStruct((16, rows), jnp.float32),
        ),
        in_specs=[pl.BlockSpec(memory_space=pltpu.VMEM)] * 4,
        out_specs=(pl.BlockSpec(memory_space=pltpu.VMEM),) * 2,
        scratch_shapes=[pltpu.VMEM((span, rows), jnp.float32)],
        compiler_params=pltpu.CompilerParams(vmem_limit_bytes=VMEM_LIMIT),
        cost_estimate=pl.CostEstimate(
            flops=4 * rows * span * width,
            transcendentals=rows * span * HEADS,
            bytes_accessed=4 * rows * width + 4 * span * width,
        ),
        name="attend_forward",
    )(queries, window, query_item[None, :], key_item[:, None])


def attend_backward_kernel(
    q_ref, kv_ref, do_ref, lse_ref, query_item_ref, key_item_ref, dq_ref, dkv_ref, bias_ref
):
    fill_bias(bias_ref, query_item_ref, key_item_ref)
    width = HEADS * HD
    masks = lane_masks(jnp.bfloat16)
    for pair in range(PAIRS):
        cols = slice(pair * LANES, (pair + 1) * LANES)
        value_cols = slice(width + pair * LANES, width + (pair + 1) * LANES)
        query = q_ref[:, cols] * jnp.bfloat16(HD ** (-0.5))
        key_rows = kv_ref[:, cols]
        value_rows = kv_ref[:, value_cols]
        grad_out = do_ref[:, cols]
        halves = []
        grad_key = grad_value = None
        for half in range(2):
            query_half = query * masks[half]
            grad_half = grad_out * masks[half]
            scores = against_rows(key_rows, query_half) + bias_ref[...]
            shares = jnp.exp(scores - lse_ref[2 * pair + half : 2 * pair + half + 1, :])
            grad_shares = against_rows(value_rows, grad_half)
            inner = jnp.sum(grad_shares * shares, axis=0, keepdims=True)
            grad_scores = (shares * (grad_shares - inner)).astype(jnp.bfloat16)
            one_value = dense(shares.astype(jnp.bfloat16), grad_half)
            one_key = dense(grad_scores, query_half)
            grad_value = one_value if grad_value is None else grad_value + one_value
            grad_key = one_key if grad_key is None else grad_key + one_key
            one_query = contract_rows(key_rows, grad_scores)
            halves.append(one_query[half * HD : (half + 1) * HD])
        grad_query = jnp.concatenate(halves, axis=0).T * HD ** (-0.5)
        dq_ref[:, cols] = grad_query.astype(dq_ref.dtype)
        dkv_ref[:, cols] = grad_key.astype(dkv_ref.dtype)
        dkv_ref[:, value_cols] = grad_value.astype(dkv_ref.dtype)


def attend_backward(queries, window, grad_out, lse, query_item, key_item):
    rows, width = queries.shape
    span = window.shape[0]
    return pl.pallas_call(
        attend_backward_kernel,
        out_shape=(
            jax.ShapeDtypeStruct((rows, width), jnp.bfloat16),
            jax.ShapeDtypeStruct((span, 2 * width), jnp.bfloat16),
        ),
        in_specs=[pl.BlockSpec(memory_space=pltpu.VMEM)] * 6,
        out_specs=(pl.BlockSpec(memory_space=pltpu.VMEM),) * 2,
        scratch_shapes=[pltpu.VMEM((span, rows), jnp.float32)],
        compiler_params=pltpu.CompilerParams(vmem_limit_bytes=VMEM_LIMIT),
        cost_estimate=pl.CostEstimate(
            flops=10 * rows * span * width,
            transcendentals=rows * span * HEADS,
            bytes_accessed=8 * rows * width + 8 * span * width,
        ),
        name="attend_backward",
    )(queries, window, grad_out, lse, query_item[None, :], key_item[:, None])


def layer_forward(hidden, weights, gain_one, gain_two, items):
    proj_qkv, proj_out, proj_up, proj_down = weights
    width = proj_out.shape[0]
    normed = norm_rows(hidden, gain_one).astype(jnp.bfloat16)
    projected = dense(normed, proj_qkv).astype(jnp.bfloat16)
    window = gather_window(projected[:, width:])
    attended, lse = attend_forward(projected[:, :width], window, *items)
    middle = hidden + dense(attended, proj_out)
    second = norm_rows(middle, gain_two).astype(jnp.bfloat16)
    upper = dense(second, proj_up)
    activated = jax.nn.gelu(upper, approximate=True).astype(jnp.bfloat16)
    return (
        middle + dense(activated, proj_down),
        (
            hidden,
            normed,
            projected,
            window,
            lse,
            attended,
            middle,
            second,
            upper,
            activated,
        ),
    )


def layer_backward(grad_hidden, weights, gain_one, gain_two, items, saved):
    hidden, normed, projected, window, lse, attended, middle, second, upper, activated = saved
    proj_qkv, proj_out, proj_up, proj_down = weights
    width = proj_out.shape[0]
    rows = hidden.shape[0]
    branch_top = grad_hidden.astype(jnp.bfloat16)
    grad_activated = against_rows(branch_top, proj_down)
    unused, pull_gelu = jax.vjp(lambda value: jax.nn.gelu(value, approximate=True), upper)
    grad_upper = pull_gelu(grad_activated)[0].astype(jnp.bfloat16)
    grad_second = against_rows(grad_upper, proj_up)
    unused, pull_two = jax.vjp(norm_rows, middle, gain_two)
    grad_middle, grad_gain_two = pull_two(grad_second)
    grad_middle = grad_middle + grad_hidden
    branch_mid = grad_middle.astype(jnp.bfloat16)
    grad_attended = against_rows(branch_mid, proj_out).astype(jnp.bfloat16)
    grad_query, grad_window = attend_backward(
        projected[:, :width], window, grad_attended, lse, *items
    )
    grad_pairs = return_window(grad_window, rows)
    grad_query = grad_query.astype(jnp.float32)
    grad_projected = jnp.concatenate([grad_query, grad_pairs], axis=1).astype(jnp.bfloat16)
    grad_normed = against_rows(grad_projected, proj_qkv)
    unused, pull_one = jax.vjp(norm_rows, hidden, gain_one)
    grad_input, grad_gain_one = pull_one(grad_normed)
    operand_pairs = (
        normed,
        grad_projected,
        attended,
        branch_mid,
        second,
        grad_upper,
        activated,
        branch_top,
    )
    return (grad_middle + grad_input, operand_pairs, grad_gain_one, grad_gain_two)


def reduce_layer(operand_pairs, shards):
    normed, grad_projected, attended, branch_mid, second, grad_upper, activated, branch_top = (
        operand_pairs
    )
    upper_full = jnp.concatenate(
        [
            contract_rows(normed, grad_projected).astype(jnp.bfloat16),
            contract_rows(attended, branch_mid).astype(jnp.bfloat16),
            contract_rows(second, grad_upper).astype(jnp.bfloat16),
        ],
        axis=1,
    )
    lower_full = contract_rows(activated, branch_top).astype(jnp.bfloat16)
    upper_own = lax.psum_scatter(upper_full, "seq", scatter_dimension=0, tiled=True)
    lower_own = lax.psum_scatter(lower_full, "seq", scatter_dimension=0, tiled=True)
    return jnp.concatenate([upper_own.reshape(-1), lower_own.reshape(-1)]).astype(jnp.float32)


def adam(grad, first, second, anchor):
    first = beta_one * first + (1.0 - beta_one) * grad
    second = beta_two * second + (1.0 - beta_two) * grad * grad
    stepped = first / (1.0 - beta_one**STEP_COUNT)
    scaled = second / (1.0 - beta_two**STEP_COUNT)
    delta = inner_rate * (stepped / (jnp.sqrt(scaled) + adam_eps) + decay_rate * anchor)
    return (first, second, delta)


MESH = pl.DeviceIdType.MESH
SUBLANES = 8
CLOSE_RANKS = 16


def greet_seq(me, count):
    group = lax.axis_index("grp")
    barrier = pltpu.get_barrier_semaphore()

    def one(step, carry):
        pl.semaphore_signal(
            barrier, inc=1, device_id=(group, lax.rem(me + step, count)), device_id_type=MESH
        )
        return carry

    lax.fori_loop(1, count, one, 0)
    pl.semaphore_wait(barrier, count - 1)


def sum_kernel(count, x_ref, out_ref, parts, own, totals, send_one, recv_one, send_two, recv_two):
    me = lax.axis_index("seq")
    group = lax.axis_index("grp")
    greet_seq(me, count)

    def slice_copy(step):
        peer = lax.rem(me + step, count)
        return pltpu.make_async_remote_copy(
            src_ref=x_ref.at[peer],
            dst_ref=parts.at[step],
            send_sem=send_one.at[step],
            recv_sem=recv_one.at[step],
            device_id=(group, peer),
            device_id_type=MESH,
        )

    def total_copy(step):
        peer = lax.rem(me + step, count)
        return pltpu.make_async_remote_copy(
            src_ref=own,
            dst_ref=totals.at[step],
            send_sem=send_two.at[step],
            recv_sem=recv_two.at[step],
            device_id=(group, peer),
            device_id_type=MESH,
        )

    def start_of(make):
        def one(step, carry):
            make(step).start()
            return carry

        return one

    lax.fori_loop(1, count, start_of(slice_copy), 0)
    own[...] = x_ref[me]

    def gather_in(step, carry):
        slice_copy(step).wait()
        own[...] += parts[step]
        return carry

    lax.fori_loop(1, count, gather_in, 0)
    lax.fori_loop(1, count, start_of(total_copy), 0)
    out_ref[me] = own[...]

    def spread(step, carry):
        total_copy(step).wait()
        out_ref[lax.rem(me + count - step, count)] = totals[step]
        return carry

    lax.fori_loop(1, count, spread, 0)


def sum_over_seq(values, collective):
    count = lax.axis_size("seq")
    if count != CLOSE_RANKS:
        return lax.psum(values, "seq")
    sizes = [math.prod(value.shape) for value in values]
    block = -(-sum(sizes) // (count * SUBLANES * LANES)) * SUBLANES
    flat = jnp.concatenate([value.reshape(-1) for value in values])
    flat = jnp.pad(flat, (0, count * block * LANES - flat.shape[0]))
    shape = (count, block, LANES)
    total = pl.pallas_call(
        functools.partial(sum_kernel, count),
        out_shape=jax.ShapeDtypeStruct(shape, jnp.float32),
        in_specs=[pl.BlockSpec(memory_space=pltpu.VMEM)],
        out_specs=pl.BlockSpec(memory_space=pltpu.VMEM),
        scratch_shapes=[
            pltpu.VMEM(shape, jnp.float32),
            pltpu.VMEM(shape[1:], jnp.float32),
            pltpu.VMEM(shape, jnp.float32),
        ]
        + [pltpu.SemaphoreType.DMA((count,))] * 4,
        compiler_params=pltpu.CompilerParams(collective_id=collective, has_side_effects=True),
        cost_estimate=pl.CostEstimate(
            flops=math.prod(shape), transcendentals=0, bytes_accessed=16 * math.prod(shape)
        ),
        name="sum_over_seq",
    )(flat.reshape(shape))
    return carve(total.reshape(-1), [value.shape for value in values])


def share_kernel(count, x_ref, out_ref, parts, send_sem, recv_sem):
    me = lax.axis_index("seq")
    group = lax.axis_index("grp")
    greet_seq(me, count)

    def copy_of(step):
        return pltpu.make_async_remote_copy(
            src_ref=x_ref,
            dst_ref=parts.at[step],
            send_sem=send_sem.at[step],
            recv_sem=recv_sem.at[step],
            device_id=(group, lax.rem(me + step, count)),
            device_id_type=MESH,
        )

    def start(step, carry):
        copy_of(step).start()
        return carry

    lax.fori_loop(1, count, start, 0)
    out_ref[me] = x_ref[...]

    def finish(step, carry):
        copy_of(step).wait()
        out_ref[lax.rem(me + count - step, count)] = parts[step]
        return carry

    lax.fori_loop(1, count, finish, 0)


def sum_scalar_over_seq(value, collective):
    count = lax.axis_size("seq")
    if count != CLOSE_RANKS:
        return lax.psum(value, "seq")
    shape = (count, SUBLANES, LANES)
    shared = pl.pallas_call(
        functools.partial(share_kernel, count),
        out_shape=jax.ShapeDtypeStruct(shape, jnp.float32),
        in_specs=[pl.BlockSpec(memory_space=pltpu.VMEM)],
        out_specs=pl.BlockSpec(memory_space=pltpu.VMEM),
        scratch_shapes=[pltpu.VMEM(shape, jnp.float32)]
        + [pltpu.SemaphoreType.DMA((count,))] * 2,
        compiler_params=pltpu.CompilerParams(collective_id=collective, has_side_effects=True),
        name="share_over_seq",
    )(jnp.full(shape[1:], value, jnp.float32))
    return jnp.sum(shared[:, 0, 0])


def group_mean(delta, count):
    low = lax.reduce_precision(delta, 8, 7)
    total = low
    for step in range(1, count):
        moves = [(source, (source + step) % count) for source in range(count)]
        total = total + lax.ppermute(low.astype(jnp.bfloat16), "grp", moves).astype(jnp.float32)
    return total / count


def per_device(
    anchor_layers,
    anchor_other,
    first_layers,
    first_other,
    second_layers,
    second_other,
    outer_layers,
    outer_other,
    latents,
    noise,
    lengths,
    timesteps,
    null_flags,
    captions,
):
    seq_count = lax.axis_size("seq")
    group_count = lax.axis_size("grp")
    rank = lax.axis_index("seq")
    rows = latents.shape[0]
    channels = latents.shape[1]
    frames_group = rows * seq_count
    lengths = lengths[0]
    timesteps = timesteps[0]
    null_flags = null_flags[0]
    captions = captions[0]
    item_count = lengths.shape[0]
    text_width = captions.shape[1]
    other_size = anchor_other.shape[0]
    padded = -(-other_size // 2048) * 2048
    other_rows = jnp.pad(anchor_other.astype(jnp.bfloat16), (0, padded - other_size))
    other_rows = lax.all_gather(other_rows.reshape(-1, LANES), "seq", axis=0, tiled=True)
    other_low = other_rows.reshape(seq_count, padded)[:, :other_size].reshape(-1)
    w_in, w_out, w_time, w_text, w_audio, w_caption, gains, null_text = carve(
        other_low, other_shapes(channels, D, text_width, E, L)
    )
    w_time_f = w_time.astype(jnp.float32)
    w_text_f = w_text.astype(jnp.float32)
    w_audio_f = w_audio.astype(jnp.float32)
    w_caption_f = w_caption.astype(jnp.float32)
    gains_f = gains.astype(jnp.float32)
    null_f = null_text.astype(jnp.float32)
    places = rank * rows + jnp.arange(rows, dtype=jnp.int32)
    order = jnp.arange(item_count, dtype=jnp.int32)
    ends = jnp.sum(jnp.where(order[None, :] <= order[:, None], lengths[None, :], 0), axis=1)
    item = jnp.sum((places[:, None] >= ends[None, :]).astype(jnp.int32), axis=1)
    onehot = (item[:, None] == jnp.arange(item_count, dtype=jnp.int32)[None, :]).astype(jnp.float32)
    key_places = rank * rows + jnp.arange(-2 * rows, 3 * rows, dtype=jnp.int32)
    key_item = jnp.sum((key_places[:, None] >= ends[None, :]).astype(jnp.int32), axis=1)
    key_item = jnp.where((key_places >= 0) & (key_places < frames_group), key_item, -1)
    items = (item, key_item)
    lengths_f = lengths[:, None].astype(jnp.float32)
    alpha_bar = plan(timesteps)
    mixing = exact(onehot, jnp.stack([jnp.sqrt(alpha_bar), jnp.sqrt(1.0 - alpha_bar)], axis=1))
    noisy_low = (mixing[:, 0:1] * latents + mixing[:, 1:2] * noise).astype(jnp.bfloat16)
    features = time_features(timesteps)

    def condition_of(time_weight, text_weight, null_vector):
        text = jnp.where(null_flags[:, None] == 1, null_vector[None, :], captions)
        return jax.nn.silu(exact(features, time_weight) + exact(text, text_weight))

    condition, pull_condition = jax.vjp(condition_of, w_time_f, w_text_f, null_f)
    hidden = dense(noisy_low, w_in) + exact(onehot, condition)
    saved_all = []
    gathered = [gather_layer(anchor_layers[depth], seq_count) for depth in range(L)]
    for depth in range(L):
        weights = gathered[depth]
        hidden, saved = layer_forward(
            hidden, weights, gains_f[2 * depth], gains_f[2 * depth + 1], items
        )
        saved_all.append(saved)
    final = norm_rows(hidden, gains_f[2 * L])
    final_low = final.astype(jnp.bfloat16)
    predicted = dense(final_low, w_out)
    error = predicted - noise
    part_pool = contract_rows(onehot, final, HIGH)
    squared_sum, pool_sum = sum_over_seq((jnp.sum(error * error), part_pool), 1)
    pooled = pool_sum / lengths_f
    audio_side = exact(pooled, w_audio_f)
    text_side = exact(captions, w_caption_f)
    clash, pull_clash = jax.vjp(contrast, audio_side, text_side)
    loss = squared_sum / (frames_group * channels) + contrast_weight * clash
    grad_audio_side, grad_text_side = pull_clash(jnp.float32(contrast_weight))
    grad_pred = (2.0 / (frames_group * channels) * error).astype(jnp.bfloat16)
    grad_w_out = contract_rows(grad_pred, final_low)
    grad_w_audio = contract_rows(pooled, grad_audio_side, HIGH)
    grad_w_caption = contract_rows(captions, grad_text_side, HIGH)
    grad_pooled = against_rows(grad_audio_side, w_audio_f, HIGH) / lengths_f
    grad_final = against_rows(grad_pred, w_out) + exact(onehot, grad_pooled)
    unused, pull_final = jax.vjp(norm_rows, hidden, gains_f[2 * L])
    grad_hidden, grad_gain_final = pull_final(grad_final)
    layer_grads = [None] * L
    gain_grads = [None] * (2 * L + 1)
    gain_grads[2 * L] = grad_gain_final
    for depth in reversed(range(L)):
        weights = gathered[depth]
        grad_hidden, operand_pairs, grad_gain_one, grad_gain_two = layer_backward(
            grad_hidden, weights, gains_f[2 * depth], gains_f[2 * depth + 1], items, saved_all[depth]
        )
        gain_grads[2 * depth] = grad_gain_one
        gain_grads[2 * depth + 1] = grad_gain_two
        layer_grads[depth] = reduce_layer(operand_pairs, seq_count)
    stacked = jnp.stack(layer_grads)
    grad_w_in = contract_rows(noisy_low.astype(jnp.float32), grad_hidden, HIGH)
    grad_condition = contract_rows(onehot, grad_hidden, HIGH)
    grad_w_in, grad_w_out, grad_condition, gain_rows = sum_over_seq(
        (grad_w_in, grad_w_out, grad_condition, jnp.stack(gain_grads)), 2
    )
    grad_w_out = grad_w_out.T
    grad_w_time, grad_w_text, grad_null = pull_condition(grad_condition)
    other_flat = jnp.concatenate(
        [
            grad_w_in.ravel(),
            grad_w_out.ravel(),
            grad_w_time.ravel(),
            grad_w_text.ravel(),
            grad_w_audio.ravel(),
            grad_w_caption.ravel(),
            gain_rows.ravel(),
            grad_null,
        ]
    )
    other_grad = lax.dynamic_slice_in_dim(other_flat, rank * other_size, other_size)
    square_part = jnp.sum(stacked * stacked) + jnp.sum(other_grad * other_grad)
    total_norm = jnp.sqrt(sum_scalar_over_seq(square_part, 3))
    factor = jnp.minimum(1.0, clip_at / (total_norm + 1e-06))
    first_l, second_l, delta_l = adam(
        stacked * factor, first_layers[0], second_layers[0], anchor_layers
    )
    first_o, second_o, delta_o = adam(
        other_grad * factor, first_other[0], second_other[0], anchor_other
    )
    mean_layers = group_mean(delta_l, group_count)
    mean_other = group_mean(delta_o, group_count)
    momentum_layers = outer_mu * outer_layers + mean_layers
    momentum_other = outer_mu * outer_other + mean_other
    new_layers = anchor_layers - outer_rate * (mean_layers + outer_mu * momentum_layers)
    new_other = anchor_other - outer_rate * (mean_other + outer_mu * momentum_other)
    return (
        new_layers,
        new_other,
        first_l[None],
        first_o[None],
        second_l[None],
        second_o[None],
        mean_layers,
        mean_other,
        momentum_layers,
        momentum_other,
        loss.reshape(1),
        total_norm.reshape(1),
    )


def solution(mesh):
    placed = (
        P(None, "seq"),
        P("seq"),
        P("grp", None, "seq"),
        P("grp", "seq"),
        P("grp", None, "seq"),
        P("grp", "seq"),
        P(None, "seq"),
        P("seq"),
        P(("grp", "seq"), None),
        P(("grp", "seq"), None),
        P("grp", None),
        P("grp", None),
        P("grp", None),
        P("grp", None, None),
    )
    return jax.shard_map(
        per_device,
        mesh=mesh,
        in_specs=placed,
        out_specs=(
            P(None, "seq"),
            P("seq"),
            P("grp", None, "seq"),
            P("grp", "seq"),
            P("grp", None, "seq"),
            P("grp", "seq"),
            P(None, "seq"),
            P("seq"),
            P(None, "seq"),
            P("seq"),
            P("grp"),
            P("grp"),
        ),
        check_vma=False,
    )
```

```python
import functools
import math

import jax
import jax.numpy as jnp
from jax import lax
from jax.experimental import pallas as pl
from jax.experimental.pallas import tpu as pltpu
from jax.sharding import PartitionSpec as P

D = 768
HEADS = 12
HD = 64
FF = 3072
E = 512
L = 2
TSTEPS = 1000
STEP_COUNT = 10


HIGH = lax.Precision.HIGHEST
beta_one = 0.9
beta_two = 0.95
adam_eps = 1e-08
decay_rate = 0.01
inner_rate = 0.02
outer_rate = 0.7
outer_mu = 0.9
clip_at = 0.01
logit_scale = 30.0
contrast_weight = 0.05


def passed_along(value, axis, steps):
    count = lax.axis_size(axis)
    initial, last = (max(0, -steps), min(count, count - steps))
    return lax.ppermute(value, axis, [(source, source + steps) for source in range(initial, last)])


def dense(left, right):
    return jnp.dot(left, right, preferred_element_type=jnp.float32)


def exact(left, right):
    return jnp.dot(left, right, precision=HIGH, preferred_element_type=jnp.float32)


def contract_rows(left, right, precision=None):
    return lax.dot_general(
        left,
        right,
        (((0,), (0,)), ((), ())),
        precision=precision,
        preferred_element_type=jnp.float32,
    )


def against_rows(left, right, precision=None):
    return lax.dot_general(
        left,
        right,
        (((1,), (1,)), ((), ())),
        precision=precision,
        preferred_element_type=jnp.float32,
    )


def carve(flat, shapes):
    pieces = []
    start = 0
    for shape in shapes:
        count = math.prod(shape)
        pieces.append(flat[start : start + count].reshape(shape))
        start += count
    return pieces


def layer_rows(piece, shards):
    cut = D // shards * (4 * D + FF)
    return piece[:cut].reshape(D // shards, 4 * D + FF), piece[cut:].reshape(FF // shards, D)


def split_upper(upper, lower):
    return [upper[:, : 3 * D], upper[:, 3 * D : 4 * D], upper[:, 4 * D :], lower]


def other_shapes(channels, width, text_width, joint_width, blocks):
    return [
        (channels, width),
        (width, channels),
        (width, width),
        (text_width, width),
        (width, joint_width),
        (text_width, joint_width),
        (2 * blocks + 1, width),
        (text_width,),
    ]


def norm_rows(hidden, gain):
    centred = hidden - jnp.mean(hidden, axis=-1, keepdims=True)
    return centred * lax.rsqrt(jnp.mean(centred * centred, axis=-1, keepdims=True) + 1e-05) * gain


def plan(steps):
    angle = (steps.astype(jnp.float32) / TSTEPS + 0.008) / 1.008 * (math.pi / 2)
    return jnp.cos(angle) ** 2


def time_features(steps):
    half = D // 2
    frequency = jnp.exp(-math.log(10000.0) * jnp.arange(half, dtype=jnp.float32) / half)
    angle = steps.astype(jnp.float32)[:, None] * frequency[None, :]
    return jnp.concatenate([jnp.cos(angle), jnp.sin(angle)], axis=1)


def contrast(audio_side, text_side):
    audio_unit = audio_side * lax.rsqrt(
        jnp.sum(audio_side * audio_side, axis=-1, keepdims=True) + 1e-06
    )
    text_unit = text_side * lax.rsqrt(
        jnp.sum(text_side * text_side, axis=-1, keepdims=True) + 1e-06
    )
    logits = logit_scale * jnp.dot(audio_unit, text_unit.T, precision=HIGH)
    diagonal = logit_scale * jnp.sum(audio_unit * text_unit, axis=-1)
    row_terms = jax.nn.logsumexp(logits, axis=1) - diagonal
    column_terms = jax.nn.logsumexp(logits, axis=0) - diagonal
    return 0.5 * (jnp.mean(row_terms) + jnp.mean(column_terms))


def gather_window(local_pairs):
    pieces = {}
    for step in (2, 1, -1, -2):
        pieces[step] = passed_along(local_pairs, "seq", step)
    return jnp.concatenate([pieces[2], pieces[1], local_pairs, pieces[-1], pieces[-2]], axis=0)


def return_window(grad_window, rows):
    total = grad_window[2 * rows : 3 * rows].astype(jnp.float32)
    for slot, step in ((0, 2), (1, 1), (3, -1), (4, -2)):
        total = total + passed_along(
            grad_window[slot * rows : (slot + 1) * rows], "seq", -step
        ).astype(jnp.float32)
    return total


LANES = 128
PAIRS = HEADS * HD // LANES
VMEM_LIMIT = 50 * 1024 * 1024


def lane_masks(dtype):
    lane = lax.broadcasted_iota(jnp.int32, (1, LANES), 1)
    return [(lane < HD).astype(dtype), (lane >= HD).astype(dtype)]


def fill_bias(bias_ref, query_item_ref, key_item_ref):
    keep = key_item_ref[...] == query_item_ref[...]
    bias_ref[...] = jnp.where(keep, 0.0, -1e30).astype(jnp.float32)


def attend_forward_kernel(q_ref, kv_ref, query_item_ref, key_item_ref, o_ref, lse_ref, bias_ref):
    fill_bias(bias_ref, query_item_ref, key_item_ref)
    width = HEADS * HD
    masks = lane_masks(jnp.bfloat16)
    lse_ref[...] = jnp.zeros_like(lse_ref)
    for pair in range(PAIRS):
        cols = slice(pair * LANES, (pair + 1) * LANES)
        query = q_ref[:, cols] * jnp.bfloat16(HD ** (-0.5))
        key_rows = kv_ref[:, cols]
        value_rows = kv_ref[:, width + pair * LANES : width + (pair + 1) * LANES]
        halves = []
        for half in range(2):
            scores = against_rows(key_rows, query * masks[half]) + bias_ref[...]
            peak = jnp.max(scores, axis=0, keepdims=True)
            weights = jnp.exp(scores - peak)
            total = jnp.sum(weights, axis=0, keepdims=True)
            shares = (weights * (1.0 / total)).astype(jnp.bfloat16)
            mixed = contract_rows(value_rows, shares)
            halves.append(mixed[half * HD : (half + 1) * HD])
            lse_ref[2 * pair + half : 2 * pair + half + 1, :] = peak + jnp.log(total)
        o_ref[:, cols] = jnp.concatenate(halves, axis=0).T.astype(o_ref.dtype)


def attend_forward(queries, window, query_item, key_item):
    rows, width = queries.shape
    span = window.shape[0]
    return pl.pallas_call(
        attend_forward_kernel,
        out_shape=(
            jax.ShapeDtypeStruct((rows, width), jnp.bfloat16),
            jax.ShapeDtypeStruct((16, rows), jnp.float32),
        ),
        in_specs=[pl.BlockSpec(memory_space=pltpu.VMEM)] * 4,
        out_specs=(pl.BlockSpec(memory_space=pltpu.VMEM),) * 2,
        scratch_shapes=[pltpu.VMEM((span, rows), jnp.float32)],
        compiler_params=pltpu.CompilerParams(vmem_limit_bytes=VMEM_LIMIT),
        cost_estimate=pl.CostEstimate(
            flops=4 * rows * span * width,
            transcendentals=rows * span * HEADS,
            bytes_accessed=4 * rows * width + 4 * span * width,
        ),
        name="attend_forward",
    )(queries, window, query_item[None, :], key_item[:, None])


def attend_backward_kernel(
    q_ref, kv_ref, do_ref, lse_ref, query_item_ref, key_item_ref, dq_ref, dkv_ref, bias_ref
):
    fill_bias(bias_ref, query_item_ref, key_item_ref)
    width = HEADS * HD
    masks = lane_masks(jnp.bfloat16)
    for pair in range(PAIRS):
        cols = slice(pair * LANES, (pair + 1) * LANES)
        value_cols = slice(width + pair * LANES, width + (pair + 1) * LANES)
        query = q_ref[:, cols] * jnp.bfloat16(HD ** (-0.5))
        key_rows = kv_ref[:, cols]
        value_rows = kv_ref[:, value_cols]
        grad_out = do_ref[:, cols]
        halves = []
        grad_key = grad_value = None
        for half in range(2):
            query_half = query * masks[half]
            grad_half = grad_out * masks[half]
            scores = against_rows(key_rows, query_half) + bias_ref[...]
            shares = jnp.exp(scores - lse_ref[2 * pair + half : 2 * pair + half + 1, :])
            grad_shares = against_rows(value_rows, grad_half)
            inner = jnp.sum(grad_shares * shares, axis=0, keepdims=True)
            grad_scores = (shares * (grad_shares - inner)).astype(jnp.bfloat16)
            one_value = dense(shares.astype(jnp.bfloat16), grad_half)
            one_key = dense(grad_scores, query_half)
            grad_value = one_value if grad_value is None else grad_value + one_value
            grad_key = one_key if grad_key is None else grad_key + one_key
            one_query = contract_rows(key_rows, grad_scores)
            halves.append(one_query[half * HD : (half + 1) * HD])
        grad_query = jnp.concatenate(halves, axis=0).T * HD ** (-0.5)
        dq_ref[:, cols] = grad_query.astype(dq_ref.dtype)
        dkv_ref[:, cols] = grad_key.astype(dkv_ref.dtype)
        dkv_ref[:, value_cols] = grad_value.astype(dkv_ref.dtype)


def attend_backward(queries, window, grad_out, lse, query_item, key_item):
    rows, width = queries.shape
    span = window.shape[0]
    return pl.pallas_call(
        attend_backward_kernel,
        out_shape=(
            jax.ShapeDtypeStruct((rows, width), jnp.bfloat16),
            jax.ShapeDtypeStruct((span, 2 * width), jnp.bfloat16),
        ),
        in_specs=[pl.BlockSpec(memory_space=pltpu.VMEM)] * 6,
        out_specs=(pl.BlockSpec(memory_space=pltpu.VMEM),) * 2,
        scratch_shapes=[pltpu.VMEM((span, rows), jnp.float32)],
        compiler_params=pltpu.CompilerParams(vmem_limit_bytes=VMEM_LIMIT),
        cost_estimate=pl.CostEstimate(
            flops=10 * rows * span * width,
            transcendentals=rows * span * HEADS,
            bytes_accessed=8 * rows * width + 8 * span * width,
        ),
        name="attend_backward",
    )(queries, window, grad_out, lse, query_item[None, :], key_item[:, None])


def layer_forward(hidden, weights, gain_one, gain_two, items):
    proj_qkv, proj_out, proj_up, proj_down = weights
    width = proj_out.shape[0]
    normed = norm_rows(hidden, gain_one).astype(jnp.bfloat16)
    projected = dense(normed, proj_qkv).astype(jnp.bfloat16)
    window = gather_window(projected[:, width:])
    attended, lse = attend_forward(projected[:, :width], window, *items)
    middle = hidden + dense(attended, proj_out)
    second = norm_rows(middle, gain_two).astype(jnp.bfloat16)
    upper = dense(second, proj_up)
    activated = jax.nn.gelu(upper, approximate=True).astype(jnp.bfloat16)
    return (
        middle + dense(activated, proj_down),
        (
            hidden,
            normed,
            projected,
            window,
            lse,
            attended,
            middle,
            second,
            upper,
            activated,
        ),
    )


def layer_backward(grad_hidden, weights, gain_one, gain_two, items, saved):
    hidden, normed, projected, window, lse, attended, middle, second, upper, activated = saved
    proj_qkv, proj_out, proj_up, proj_down = weights
    width = proj_out.shape[0]
    rows = hidden.shape[0]
    branch_top = grad_hidden.astype(jnp.bfloat16)
    grad_activated = against_rows(branch_top, proj_down)
    unused, pull_gelu = jax.vjp(lambda value: jax.nn.gelu(value, approximate=True), upper)
    grad_upper = pull_gelu(grad_activated)[0].astype(jnp.bfloat16)
    grad_second = against_rows(grad_upper, proj_up)
    unused, pull_two = jax.vjp(norm_rows, middle, gain_two)
    grad_middle, grad_gain_two = pull_two(grad_second)
    grad_middle = grad_middle + grad_hidden
    branch_mid = grad_middle.astype(jnp.bfloat16)
    grad_attended = against_rows(branch_mid, proj_out).astype(jnp.bfloat16)
    grad_query, grad_window = attend_backward(
        projected[:, :width], window, grad_attended, lse, *items
    )
    grad_pairs = return_window(grad_window, rows)
    grad_query = grad_query.astype(jnp.float32)
    grad_projected = jnp.concatenate([grad_query, grad_pairs], axis=1).astype(jnp.bfloat16)
    grad_normed = against_rows(grad_projected, proj_qkv)
    unused, pull_one = jax.vjp(norm_rows, hidden, gain_one)
    grad_input, grad_gain_one = pull_one(grad_normed)
    operand_pairs = (
        normed,
        grad_projected,
        attended,
        branch_mid,
        second,
        grad_upper,
        activated,
        branch_top,
    )
    return (grad_middle + grad_input, operand_pairs, grad_gain_one, grad_gain_two)


def layer_gradients(operand_pairs):
    normed, grad_projected, attended, branch_mid, second, grad_upper, activated, branch_top = (
        operand_pairs
    )
    upper_full = jnp.concatenate(
        [
            contract_rows(normed, grad_projected).astype(jnp.bfloat16),
            contract_rows(attended, branch_mid).astype(jnp.bfloat16),
            contract_rows(second, grad_upper).astype(jnp.bfloat16),
        ],
        axis=1,
    )
    lower_full = contract_rows(activated, branch_top).astype(jnp.bfloat16)
    return upper_full, lower_full


def adam(grad, first, second, anchor):
    first = beta_one * first + (1.0 - beta_one) * grad
    second = beta_two * second + (1.0 - beta_two) * grad * grad
    stepped = first / (1.0 - beta_one**STEP_COUNT)
    scaled = second / (1.0 - beta_two**STEP_COUNT)
    delta = inner_rate * (stepped / (jnp.sqrt(scaled) + adam_eps) + decay_rate * anchor)
    return (first, second, delta)


MESH = pl.DeviceIdType.MESH
SUBLANES = 8
CLOSE_RANKS = 16


def greet_seq(me, count):
    group = lax.axis_index("grp")
    barrier = pltpu.get_barrier_semaphore()

    def one(step, carry):
        pl.semaphore_signal(
            barrier, inc=1, device_id=(group, lax.rem(me + step, count)), device_id_type=MESH
        )
        return carry

    lax.fori_loop(1, count, one, 0)
    pl.semaphore_wait(barrier, count - 1)


def sum_kernel(count, x_ref, out_ref, parts, own, totals, send_one, recv_one, send_two, recv_two):
    me = lax.axis_index("seq")
    group = lax.axis_index("grp")
    greet_seq(me, count)

    def slice_copy(step):
        peer = lax.rem(me + step, count)
        return pltpu.make_async_remote_copy(
            src_ref=x_ref.at[peer],
            dst_ref=parts.at[step],
            send_sem=send_one.at[step],
            recv_sem=recv_one.at[step],
            device_id=(group, peer),
            device_id_type=MESH,
        )

    def total_copy(step):
        peer = lax.rem(me + step, count)
        return pltpu.make_async_remote_copy(
            src_ref=own,
            dst_ref=totals.at[step],
            send_sem=send_two.at[step],
            recv_sem=recv_two.at[step],
            device_id=(group, peer),
            device_id_type=MESH,
        )

    def start_of(make):
        def one(step, carry):
            make(step).start()
            return carry

        return one

    lax.fori_loop(1, count, start_of(slice_copy), 0)
    own[...] = x_ref[me]

    def gather_in(step, carry):
        slice_copy(step).wait()
        own[...] += parts[step]
        return carry

    lax.fori_loop(1, count, gather_in, 0)
    lax.fori_loop(1, count, start_of(total_copy), 0)
    out_ref[me] = own[...]

    def spread(step, carry):
        total_copy(step).wait()
        out_ref[lax.rem(me + count - step, count)] = totals[step]
        return carry

    lax.fori_loop(1, count, spread, 0)


def sum_over_seq(values, collective):
    count = lax.axis_size("seq")
    if count != CLOSE_RANKS:
        return lax.psum(values, "seq")
    sizes = [math.prod(value.shape) for value in values]
    block = -(-sum(sizes) // (count * SUBLANES * LANES)) * SUBLANES
    flat = jnp.concatenate([value.reshape(-1) for value in values])
    flat = jnp.pad(flat, (0, count * block * LANES - flat.shape[0]))
    shape = (count, block, LANES)
    total = pl.pallas_call(
        functools.partial(sum_kernel, count),
        out_shape=jax.ShapeDtypeStruct(shape, jnp.float32),
        in_specs=[pl.BlockSpec(memory_space=pltpu.VMEM)],
        out_specs=pl.BlockSpec(memory_space=pltpu.VMEM),
        scratch_shapes=[
            pltpu.VMEM(shape, jnp.float32),
            pltpu.VMEM(shape[1:], jnp.float32),
            pltpu.VMEM(shape, jnp.float32),
        ]
        + [pltpu.SemaphoreType.DMA((count,))] * 4,
        compiler_params=pltpu.CompilerParams(collective_id=collective, has_side_effects=True),
        cost_estimate=pl.CostEstimate(
            flops=math.prod(shape), transcendentals=0, bytes_accessed=16 * math.prod(shape)
        ),
        name="sum_over_seq",
    )(flat.reshape(shape))
    return carve(total.reshape(-1), [value.shape for value in values])


def share_kernel(count, x_ref, out_ref, parts, send_sem, recv_sem):
    seq = lax.axis_size("seq")
    me = lax.axis_index("grp") * seq + lax.axis_index("seq")

    def place(step):
        peer = lax.rem(me + step, count)
        return peer // seq, lax.rem(peer, seq)

    barrier = pltpu.get_barrier_semaphore()

    def greet(step, carry):
        pl.semaphore_signal(barrier, inc=1, device_id=place(step), device_id_type=MESH)
        return carry

    lax.fori_loop(1, count, greet, 0)
    pl.semaphore_wait(barrier, count - 1)

    def copy_of(step):
        return pltpu.make_async_remote_copy(
            src_ref=x_ref,
            dst_ref=parts.at[step],
            send_sem=send_sem.at[step],
            recv_sem=recv_sem.at[step],
            device_id=place(step),
            device_id_type=MESH,
        )

    def start(step, carry):
        copy_of(step).start()
        return carry

    lax.fori_loop(1, count, start, 0)
    out_ref[me] = x_ref[...]

    def finish(step, carry):
        copy_of(step).wait()
        out_ref[lax.rem(me + count - step, count)] = parts[step]
        return carry

    lax.fori_loop(1, count, finish, 0)


def sums_by_group(value, collective):
    groups, count = lax.axis_size("grp"), lax.axis_size("seq")
    shape = (groups * count, SUBLANES, LANES)
    shared = pl.pallas_call(
        functools.partial(share_kernel, groups * count),
        out_shape=jax.ShapeDtypeStruct(shape, jnp.float32),
        in_specs=[pl.BlockSpec(memory_space=pltpu.VMEM)],
        out_specs=pl.BlockSpec(memory_space=pltpu.VMEM),
        scratch_shapes=[pltpu.VMEM(shape, jnp.float32)]
        + [pltpu.SemaphoreType.DMA((groups * count,))] * 2,
        compiler_params=pltpu.CompilerParams(collective_id=collective, has_side_effects=True),
        name="share_over_all",
    )(jnp.full(shape[1:], value, jnp.float32))
    return jnp.sum(shared[:, 0, 0].reshape(groups, count), axis=1)


GRID = (4, 2, 2)
GATHER_Y_LAG = 2
GATHER_X_LAG = 5
GATHER_AHEAD = 1
GATHER_LANES = 256


def place_of(me):
    return me // 4, lax.rem(me // 2, 2), lax.rem(me, 2)


def rank_of(along, across, core):
    return (along * 2 + across) * 2 + core


def gather_kernel(shared, *refs):
    pieces = len(shared)
    own_refs, out_refs = refs[:pieces], refs[pieces : 2 * pieces]
    local_sem, z_send, z_recv, y_send, y_recv, x_send, x_recv, c_send, c_recv = refs[2 * pieces :]
    group, me = lax.axis_index("grp"), lax.axis_index("seq")
    z, y, core = place_of(me)
    z_size = GRID[0]
    across, sibling, twin = (
        (group, rank_of(z, 1 - y, core)),
        (group, rank_of(z, y, 1 - core)),
        (1 - group, me),
    )
    barrier = pltpu.get_barrier_semaphore()
    for there in (across, sibling, twin):
        pl.semaphore_signal(barrier, inc=1, device_id=there, device_id_type=MESH)

    @pl.when(z > 0)
    def _():
        pl.semaphore_signal(
            barrier, inc=1, device_id=(group, rank_of(z - 1, y, core)), device_id_type=MESH
        )

    @pl.when(z < z_size - 1)
    def _():
        pl.semaphore_signal(
            barrier, inc=1, device_id=(group, rank_of(z + 1, y, core)), device_id_type=MESH
        )

    neighbours = (z > 0).astype(jnp.int32) + (z < z_size - 1).astype(jnp.int32)
    pl.semaphore_wait(barrier, 3 + neighbours)

    def half_of(ref, piece, half):
        if half is None:
            return ref
        span = ref.shape[-1] // 2
        return ref.at[:, pl.ds(pl.multiple_of(half * span, LANES), span)]

    def move(piece, half, there, along, over, send, recv, own=False):
        dst = half_of(out_refs[piece].at[rank_of(along, over, core)], piece, half)
        src = half_of(own_refs[piece], piece, half) if own else dst
        return pltpu.make_async_remote_copy(
            src_ref=src, dst_ref=dst, send_sem=send, recv_sem=recv, device_id=there, device_id_type=MESH
        )

    def z_move(piece, along, forward, own=False):
        there = (group, rank_of(z + (1 if forward else -1), y, core))
        half = group if shared[piece] else None
        return move(
            piece, half, there, along, y, z_send.at[piece, along, int(forward)], z_recv.at[piece, along], own
        )

    def y_move(piece, along, own=False, over=None):
        half = group if shared[piece] else None
        over = y if over is None else over
        return move(piece, half, across, along, over, y_send.at[piece, along], y_recv.at[piece, along], own)

    def x_move(piece, along, over, arriving=False):
        half = 1 - group if arriving else group
        slot = along * 2 + over
        return move(piece, half, twin, along, over, x_send.at[piece, slot], x_recv.at[piece, slot])

    def c_move(piece, along, over, half, slot, own=False):
        return move(
            piece,
            half,
            sibling,
            along,
            over,
            c_send.at[piece, along * 2 + over, slot],
            c_recv.at[piece, along * 2 + over, slot],
            own,
        )

    def each_along(distance, action):
        if distance == 0:
            action(z, True, True)
            return

        @pl.when(z - distance >= 0)
        def _():
            action(z - distance, True, False)

        @pl.when(z + distance < z_size)
        def _():
            action(z + distance, False, True)

    def own_sends(piece):
        pltpu.make_async_copy(own_refs[piece], out_refs[piece].at[me], local_sem.at[piece]).start()

        @pl.when(z + 1 < z_size)
        def _():
            z_move(piece, z, True, own=True).start()

        @pl.when(z > 0)
        def _():
            z_move(piece, z, False, own=True).start()

        y_move(piece, z, own=True).start()
        c_move(piece, z, y, None, 0, own=True).start()

    def z_arrivals(piece, distance):
        if distance == 0:
            return

        def one(along, onward, backward):
            z_move(piece, along, onward).wait_recv()

            @pl.when((z + 1 < z_size) if onward else (z > 0))
            def _():
                z_move(piece, along, onward).start()

            y_move(piece, along).start()
            if shared[piece]:
                x_move(piece, along, y).start()
            c_move(piece, along, y, group if shared[piece] else None, 0).start()

        each_along(distance, one)

    def y_arrivals(piece, distance):
        def one(along, *_):
            y_move(piece, along, over=1 - y).wait_recv()
            if shared[piece]:
                x_move(piece, along, 1 - y).start()
            c_move(piece, along, 1 - y, group if shared[piece] else None, 0).start()

        each_along(distance, one)

    def x_arrivals(piece, distance):
        if not shared[piece]:
            return

        def one(along, *_):
            for turn in range(2):
                over = y if turn == 0 else 1 - y
                if distance == 0 and turn == 0:
                    continue
                x_move(piece, along, over, arriving=True).wait_recv()
                c_move(piece, along, over, 1 - group, 1).start()

        each_along(distance, one)

    def drain(piece, distance):
        def one(along, onward, backward):
            own = distance == 0
            half = group if shared[piece] else None
            for turn in range(2):
                over = y if turn == 0 else 1 - y
                mine = own and turn == 0
                whole = None if mine else half
                c_move(piece, along, over, whole, 0).wait()
                if shared[piece] and not mine:
                    c_move(piece, along, over, 1 - group, 1).wait()
                    x_move(piece, along, over).wait_send()
            y_move(piece, along).wait_send()
            if onward:

                @pl.when(z + 1 < z_size)
                def _():
                    z_move(piece, along, True).wait_send()

            if backward:

                @pl.when(z > 0)
                def _():
                    z_move(piece, along, False).wait_send()

        each_along(distance, one)
        if distance == 0:
            pltpu.make_async_copy(own_refs[piece], out_refs[piece].at[me], local_sem.at[piece]).wait()

    slots = [(piece, distance) for piece in range(pieces) for distance in range(z_size)]
    own_sends(0)
    for turn in range(len(slots) + GATHER_X_LAG):
        if turn < len(slots):
            piece, distance = slots[turn]
            if distance == GATHER_AHEAD and piece + 1 < pieces:
                own_sends(piece + 1)
            z_arrivals(piece, distance)
        if 0 <= turn - GATHER_Y_LAG < len(slots):
            y_arrivals(*slots[turn - GATHER_Y_LAG])
        if 0 <= turn - GATHER_X_LAG < len(slots):
            x_arrivals(*slots[turn - GATHER_X_LAG])
    for slot in slots:
        drain(*slot)


def gather_pieces(pieces, shared, collective):
    count = lax.axis_size("seq")
    if count != math.prod(GRID) or lax.axis_size("grp") != 2:
        return [lax.all_gather(piece, "seq", axis=0) for piece in pieces]
    amount = len(pieces)
    sems = [
        (amount,),
        (amount, 4, 2),
        (amount, 4),
        (amount, 4),
        (amount, 4),
        (amount, 8),
        (amount, 8),
        (amount, 8, 2),
        (amount, 8, 2),
    ]
    return pl.pallas_call(
        functools.partial(gather_kernel, tuple(shared)),
        out_shape=[jax.ShapeDtypeStruct((count,) + piece.shape, piece.dtype) for piece in pieces],
        in_specs=[pl.BlockSpec(memory_space=pl.ANY)] * amount,
        out_specs=[pl.BlockSpec(memory_space=pl.ANY)] * amount,
        scratch_shapes=[pltpu.SemaphoreType.DMA(shape) for shape in sems],
        compiler_params=pltpu.CompilerParams(collective_id=collective, has_side_effects=True),
        name="gather_pieces",
    )(*pieces)


ROW_GROUP = 16
UPPER_CUTS = 3
LOWER_CUTS = 1
SCATTER_LAG = 2


def scatter_kernel(pieces, amount, *refs):
    grads, outs, twins = (refs[k * amount : (k + 1) * amount] for k in range(3))
    squares = refs[3 * amount]
    rest = refs[3 * amount + 1 :]
    count = len(pieces)
    own, beside, facing, from_left, from_right, ready = (
        rest[k * count : (k + 1) * count] for k in range(6)
    )
    load_sem, c_send, c_recv, y_send, y_recv, z_send, z_recv, x_send, x_recv = rest[6 * count :]
    group, me = lax.axis_index("grp"), lax.axis_index("seq")
    z, y, core = place_of(me)
    z_size = GRID[0]
    across, sibling = (group, rank_of(z, 1 - y, core)), (group, rank_of(z, y, 1 - core))
    twin = (1 - group, me)
    left, right = (group, rank_of(z - 1, y, core)), (group, rank_of(z + 1, y, core))
    has_left, has_right = z > 0, z < z_size - 1
    barrier = pltpu.get_barrier_semaphore()
    for there in (across, sibling, twin):
        pl.semaphore_signal(barrier, inc=1, device_id=there, device_id_type=MESH)

    @pl.when(has_left)
    def _():
        pl.semaphore_signal(barrier, inc=1, device_id=left, device_id_type=MESH)

    @pl.when(has_right)
    def _():
        pl.semaphore_signal(barrier, inc=1, device_id=right, device_id_type=MESH)

    neighbours = has_left.astype(jnp.int32) + has_right.astype(jnp.int32)
    pl.semaphore_wait(barrier, 3 + neighbours)
    squares[...] = jnp.zeros_like(squares)

    def part(piece, along, over, owner):
        which, row, rows, column, columns = pieces[piece]
        return grads[which].at[rank_of(along, over, owner), pl.ds(row, rows), pl.ds(column, columns)]

    def load(piece, along, over):
        slot = along * 2 + over
        return pltpu.make_async_copy(
            part(piece, along, over, core), own[piece].at[slot], load_sem.at[piece, slot]
        )

    def remote(src, dst, send, recv, there):
        return pltpu.make_async_remote_copy(
            src_ref=src, dst_ref=dst, send_sem=send, recv_sem=recv, device_id=there, device_id_type=MESH
        )

    def c_move(piece, along, over):
        slot = along * 2 + over
        return remote(
            part(piece, along, over, 1 - core),
            beside[piece].at[slot],
            c_send.at[piece, slot],
            c_recv.at[piece, slot],
            sibling,
        )

    def y_move(piece, along):
        return remote(
            own[piece].at[along * 2 + 1 - y],
            facing[piece].at[along],
            y_send.at[piece, along],
            y_recv.at[piece, along],
            across,
        )

    def z_move(piece, along, forward):
        side = 0 if forward else 1
        return remote(
            facing[piece].at[along],
            (from_left if forward else from_right)[piece].at[along],
            z_send.at[piece, along],
            z_recv.at[piece, along, side],
            right if forward else left,
        )

    def x_move(piece):
        which, row, height, column, columns = pieces[piece]
        return remote(
            ready[piece],
            twins[which].at[pl.ds(row, height), pl.ds(column, columns)],
            x_send.at[piece],
            x_recv.at[piece],
            twin,
        )

    def each_along(distance, action):
        if distance == 0:
            action(z, None)
            return

        @pl.when(z - distance >= 0)
        def _():
            action(z - distance, False)

        @pl.when(z + distance < z_size)
        def _():
            action(z + distance, True)

    def by_rows(piece, body):
        def one(step, carry):
            body(pl.ds(pl.multiple_of(step * ROW_GROUP, ROW_GROUP), ROW_GROUP))
            return carry

        lax.fori_loop(0, pieces[piece][2] // ROW_GROUP, one, 0)

    def wide(ref, slot, rows):
        return ref[slot, rows, :].astype(jnp.float32)

    def begin(piece):
        for distance in reversed(range(z_size)):

            def one(along, _):
                for over in range(2):
                    load(piece, along, over).start()
                    c_move(piece, along, over).start()

            each_along(distance, one)

    def c_stage(piece, distance):
        def one(along, _):
            for turn in range(2):
                over = 1 - y if turn == 0 else y
                slot = along * 2 + over
                load(piece, along, over).wait()
                c_move(piece, along, over).wait_recv()

                def add(rows):
                    total = wide(own[piece], slot, rows) + wide(beside[piece], slot, rows)
                    own[piece][slot, rows, :] = total.astype(jnp.bfloat16)

                by_rows(piece, add)
                if turn == 0:
                    y_move(piece, along).start()

        each_along(distance, one)

    def y_stage(piece, distance):
        which, row, height, column, columns = pieces[piece]

        def one(along, forward):
            y_move(piece, along).wait_recv()
            slot = along * 2 + y
            if forward is None:

                def add(rows):
                    total = wide(own[piece], slot, rows) + wide(facing[piece], along, rows)
                    there = pl.ds(pl.multiple_of(row + rows.start, ROW_GROUP), ROW_GROUP)
                    outs[which][there, pl.ds(column, columns)] = total

                by_rows(piece, add)
                for side, present, source in ((True, has_left, from_left), (False, has_right, from_right)):

                    @pl.when(present)
                    def _():
                        z_move(piece, along, side).wait_recv()

                        def more(rows):
                            there = pl.ds(pl.multiple_of(row + rows.start, ROW_GROUP), ROW_GROUP)
                            outs[which][there, pl.ds(column, columns)] += wide(source[piece], along, rows)

                        by_rows(piece, more)

                def finish(rows):
                    there = pl.ds(pl.multiple_of(row + rows.start, ROW_GROUP), ROW_GROUP)
                    total = outs[which][there, pl.ds(column, columns)]
                    ready[piece][rows, :] = total.astype(jnp.bfloat16)
                    square = total[:SUBLANES] * total[:SUBLANES] + total[SUBLANES:] * total[SUBLANES:]
                    for k in range(columns // LANES):
                        squares[...] += square[:, k * LANES : (k + 1) * LANES]

                by_rows(piece, finish)
                x_move(piece).start()
                return
            source, present = (from_left, has_left) if forward else (from_right, has_right)

            @pl.when(present)
            def _():
                z_move(piece, along, forward).wait_recv()

                def add(rows):
                    total = wide(own[piece], slot, rows) + wide(facing[piece], along, rows)
                    total = total + wide(source[piece], along, rows)
                    facing[piece][along, rows, :] = total.astype(jnp.bfloat16)

                by_rows(piece, add)

            @pl.when(jnp.logical_not(present))
            def _():
                def add(rows):
                    total = wide(own[piece], slot, rows) + wide(facing[piece], along, rows)
                    facing[piece][along, rows, :] = total.astype(jnp.bfloat16)

                by_rows(piece, add)

            z_move(piece, along, forward).start()

        each_along(distance, one)

    def drain(piece, distance):
        def one(along, forward):
            for over in range(2):
                c_move(piece, along, over).wait_send()
            y_move(piece, along).wait_send()
            if forward is not None:
                z_move(piece, along, forward).wait_send()

        each_along(distance, one)

    slots = [(piece, distance) for piece in range(count) for distance in reversed(range(z_size))]
    for piece in range(min(2, count)):
        begin(piece)
    for turn in range(len(slots) + SCATTER_LAG):
        if turn < len(slots):
            c_stage(*slots[turn])
            piece, distance = slots[turn]
            if distance == 0 and piece + 2 < count:
                begin(piece + 2)
        if turn >= SCATTER_LAG:
            y_stage(*slots[turn - SCATTER_LAG])
    for slot in slots:
        drain(*slot)
    for piece in range(count):
        x_move(piece).wait()


def scatter_layer(upper, lower, collective):
    count = math.prod(GRID)
    grads = [grad.reshape(count, grad.shape[0] // count, grad.shape[1]) for grad in (upper, lower)]
    pieces = []
    for which, cuts in ((0, UPPER_CUTS), (1, LOWER_CUTS)):
        rows, columns = grads[which].shape[1:]
        if which == 0:
            pieces += [(0, 0, rows, k * (columns // cuts), columns // cuts) for k in range(cuts)]
        else:
            pieces += [(1, k * (rows // cuts), rows // cuts, 0, columns) for k in range(cuts)]
    amount = len(pieces)
    places = math.prod(GRID[:2])

    def room(slots):
        return [pltpu.VMEM((slots, piece[2], piece[4]), jnp.bfloat16) for piece in pieces]

    sems = [
        (amount, places),
        (amount, places),
        (amount, places),
        (amount, GRID[0]),
        (amount, GRID[0]),
        (amount, GRID[0]),
        (amount, GRID[0], 2),
        (amount,),
        (amount,),
    ]
    own_upper, own_lower, twin_upper, twin_lower, squares = pl.pallas_call(
        functools.partial(scatter_kernel, tuple(pieces), 2),
        out_shape=[jax.ShapeDtypeStruct(grad.shape[1:], jnp.float32) for grad in grads]
        + [jax.ShapeDtypeStruct(grad.shape[1:], jnp.bfloat16) for grad in grads]
        + [jax.ShapeDtypeStruct((SUBLANES, LANES), jnp.float32)],
        in_specs=[pl.BlockSpec(memory_space=pl.ANY)] * 2,
        out_specs=[pl.BlockSpec(memory_space=pltpu.VMEM)] * 2
        + [pl.BlockSpec(memory_space=pl.ANY)] * 2
        + [pl.BlockSpec(memory_space=pltpu.VMEM)],
        scratch_shapes=room(places)
        + room(places)
        + room(GRID[0])
        + room(GRID[0])
        + room(GRID[0])
        + [pltpu.VMEM((piece[2], piece[4]), jnp.bfloat16) for piece in pieces]
        + [pltpu.SemaphoreType.DMA(shape) for shape in sems],
        compiler_params=pltpu.CompilerParams(
            collective_id=collective, has_side_effects=True, vmem_limit_bytes=VMEM_LIMIT
        ),
        name="scatter_layer",
    )(*grads)
    return (own_upper, own_lower), (twin_upper, twin_lower), jnp.sum(squares)


def lay_out_kernel(shards, view_ref, *outs):
    cut = D // shards * (4 * D + FF) // LANES
    for layer in range(L):
        upper, lower = outs[2 * layer : 2 * layer + 2]
        for ref, base in ((upper, 0), (lower, cut)):
            across = ref.shape[1] // LANES
            for row in range(0, ref.shape[0], ROW_GROUP):
                for column in range(across):
                    start = L * (base + row * across + column) + layer
                    rows = view_ref[pl.ds(start, ROW_GROUP, stride=L * across), :]
                    ref[row : row + ROW_GROUP, column * LANES : (column + 1) * LANES] = rows.astype(
                        jnp.bfloat16
                    )


def flat_view(array):
    layers, size = array.shape
    return array.reshape(layers, size // LANES, LANES).transpose(1, 0, 2).reshape(-1, LANES)


def lay_out(anchor, shards):
    if shards != math.prod(GRID):
        return [layer_rows(anchor[depth].astype(jnp.bfloat16), shards) for depth in range(L)]
    shapes = [(D // shards, 4 * D + FF), (FF // shards, D)] * L
    outs = pl.pallas_call(
        functools.partial(lay_out_kernel, shards),
        out_shape=[jax.ShapeDtypeStruct(shape, jnp.bfloat16) for shape in shapes],
        in_specs=[pl.BlockSpec(memory_space=pltpu.VMEM)],
        out_specs=[pl.BlockSpec(memory_space=pltpu.VMEM)] * len(shapes),
        compiler_params=pltpu.CompilerParams(vmem_limit_bytes=VMEM_LIMIT),
        name="lay_out",
    )(flat_view(anchor))
    return [(outs[2 * depth], outs[2 * depth + 1]) for depth in range(L)]


def flatten(parts):
    return jnp.concatenate([part.reshape(-1) for part in parts])


def group_mean(delta, count):
    low = lax.reduce_precision(delta, 8, 7)
    total = low
    for step in range(1, count):
        moves = [(source, (source + step) % count) for source in range(count)]
        total = total + lax.ppermute(low.astype(jnp.bfloat16), "grp", moves).astype(jnp.float32)
    return total / count


STEP_BLOCKS = 8


def delta_of(grad, first, second, anchor):
    return adam(grad, first, second, anchor)[2]


def step_kernel(cut, factors, *refs):
    own, twin = refs[: 2 * L], refs[2 * L : 4 * L]
    anchor, first, second, outer, twin_first, twin_second = refs[4 * L : 4 * L + 6]
    new, one, two, mean_out, momentum_out, own_flat, twin_flat = refs[4 * L + 6 :]
    step = pl.program_id(0)
    block = anchor.shape[0]

    @pl.when(step == 0)
    def _():
        for grads, flat in ((own, own_flat), (twin, twin_flat)):
            for layer in range(L):
                for ref, base in zip(grads[2 * layer : 2 * layer + 2], (0, cut)):
                    across = ref.shape[1] // LANES
                    for row in range(0, ref.shape[0], ROW_GROUP):
                        for column in range(across):
                            start = L * (base + row * across + column) + layer
                            flat[pl.ds(start, ROW_GROUP, stride=L * across), :] = ref[
                                row : row + ROW_GROUP, column * LANES : (column + 1) * LANES
                            ].astype(jnp.float32)

    def low(value):
        return value.astype(jnp.bfloat16).astype(jnp.float32)

    rows = pl.ds(pl.multiple_of(step * block, SUBLANES), block)
    grad, weight = own_flat[rows, :], anchor[...]
    first_own, second_own = first[...], second[...]
    clipped = grad * factors[0]
    one[...] = beta_one * first_own + (1.0 - beta_one) * clipped
    two[...] = beta_two * second_own + (1.0 - beta_two) * clipped * clipped
    delta_own = delta_of(low(grad) * factors[0], low(first_own), low(second_own), weight)
    delta_twin = delta_of(
        twin_flat[rows, :] * factors[1],
        twin_first[...].astype(jnp.float32),
        twin_second[...].astype(jnp.float32),
        weight,
    )
    mean = (delta_own + delta_twin) / 2
    momentum = outer_mu * outer[...] + mean
    mean_out[...] = mean
    momentum_out[...] = momentum
    new[...] = weight - outer_rate * (mean + outer_mu * momentum)


def step_layers(factors, own, twin, views, shards):
    rows = views[0].shape[0]
    block = rows // STEP_BLOCKS
    whole = pl.BlockSpec(memory_space=pltpu.VMEM)
    part = pl.BlockSpec((block, LANES), lambda k: (k, 0))
    return pl.pallas_call(
        functools.partial(step_kernel, D // shards * (4 * D + FF) // LANES),
        grid=(STEP_BLOCKS,),
        out_shape=[jax.ShapeDtypeStruct((rows, LANES), jnp.float32)] * 5,
        in_specs=[pl.BlockSpec(memory_space=pltpu.SMEM)] + [whole] * (4 * L) + [part] * 6,
        out_specs=[part] * 5,
        scratch_shapes=[pltpu.VMEM((rows, LANES), jnp.float32)] * 2,
        compiler_params=pltpu.CompilerParams(
            vmem_limit_bytes=VMEM_LIMIT, dimension_semantics=("arbitrary",)
        ),
        name="step_layers",
    )(factors, *own, *twin, *views)


def from_view(view):
    rows, lanes = view.shape
    return view.reshape(rows // L, L, lanes).transpose(1, 0, 2).reshape(L, rows // L * lanes)


def swapped(value):
    return lax.ppermute(value, "grp", [(0, 1), (1, 0)])


def per_device(
    anchor_layers,
    anchor_other,
    first_layers,
    first_other,
    second_layers,
    second_other,
    outer_layers,
    outer_other,
    latents,
    noise,
    lengths,
    timesteps,
    null_flags,
    captions,
):
    seq_count = lax.axis_size("seq")
    group_count = lax.axis_size("grp")
    rank = lax.axis_index("seq")
    group = lax.axis_index("grp")
    close = seq_count == math.prod(GRID) and group_count == 2
    rows = latents.shape[0]
    channels = latents.shape[1]
    frames_group = rows * seq_count
    lengths = lengths[0]
    timesteps = timesteps[0]
    null_flags = null_flags[0]
    captions = captions[0]
    item_count = lengths.shape[0]
    text_width = captions.shape[1]
    other_size = anchor_other.shape[0]
    padded = -(-other_size // 4096) * 4096
    other_rows = jnp.pad(anchor_other.astype(jnp.bfloat16), (0, padded - other_size))
    own_rows = lay_out(anchor_layers, seq_count)
    early = 1
    pieces = [other_rows.reshape(-1, GATHER_LANES)] + [rows for pair in own_rows[:early] for rows in pair]
    other_rows, *early_rows = gather_pieces(pieces, [True] + [True, False] * early, 4)
    if close:
        first_view, second_view = flat_view(first_layers[0]), flat_view(second_layers[0])
        sources, other_rows = lax.optimization_barrier(
            ((first_view, second_view, first_other[0], second_other[0]), other_rows)
        )
        twin_views = [swapped(value.astype(jnp.bfloat16)) for value in sources[:2]]
        twin_moments = [swapped(value.astype(jnp.bfloat16)).astype(jnp.float32) for value in sources[2:]]
    late_rows = [lax.all_gather(rows, "seq", axis=0) for pair in own_rows[early:] for rows in pair]
    layer_parts = [rows.reshape(-1, rows.shape[-1]) for rows in early_rows + late_rows]
    gathered = [split_upper(*layer_parts[2 * depth : 2 * depth + 2]) for depth in range(L)]
    other_low = other_rows.reshape(seq_count, padded)[:, :other_size].reshape(-1)
    w_in, w_out, w_time, w_text, w_audio, w_caption, gains, null_text = carve(
        other_low, other_shapes(channels, D, text_width, E, L)
    )
    w_time_f = w_time.astype(jnp.float32)
    w_text_f = w_text.astype(jnp.float32)
    w_audio_f = w_audio.astype(jnp.float32)
    w_caption_f = w_caption.astype(jnp.float32)
    gains_f = gains.astype(jnp.float32)
    null_f = null_text.astype(jnp.float32)
    places = rank * rows + jnp.arange(rows, dtype=jnp.int32)
    order = jnp.arange(item_count, dtype=jnp.int32)
    ends = jnp.sum(jnp.where(order[None, :] <= order[:, None], lengths[None, :], 0), axis=1)
    item = jnp.sum((places[:, None] >= ends[None, :]).astype(jnp.int32), axis=1)
    onehot = (item[:, None] == jnp.arange(item_count, dtype=jnp.int32)[None, :]).astype(jnp.float32)
    key_places = rank * rows + jnp.arange(-2 * rows, 3 * rows, dtype=jnp.int32)
    key_item = jnp.sum((key_places[:, None] >= ends[None, :]).astype(jnp.int32), axis=1)
    key_item = jnp.where((key_places >= 0) & (key_places < frames_group), key_item, -1)
    items = (item, key_item)
    lengths_f = lengths[:, None].astype(jnp.float32)
    alpha_bar = plan(timesteps)
    mixing = exact(onehot, jnp.stack([jnp.sqrt(alpha_bar), jnp.sqrt(1.0 - alpha_bar)], axis=1))
    noisy_low = (mixing[:, 0:1] * latents + mixing[:, 1:2] * noise).astype(jnp.bfloat16)
    features = time_features(timesteps)

    def condition_of(time_weight, text_weight, null_vector):
        text = jnp.where(null_flags[:, None] == 1, null_vector[None, :], captions)
        return jax.nn.silu(exact(features, time_weight) + exact(text, text_weight))

    condition, pull_condition = jax.vjp(condition_of, w_time_f, w_text_f, null_f)
    hidden = dense(noisy_low, w_in) + exact(onehot, condition)
    saved_all = []
    for depth in range(L):
        weights = gathered[depth]
        hidden, saved = layer_forward(
            hidden, weights, gains_f[2 * depth], gains_f[2 * depth + 1], items
        )
        saved_all.append(saved)
    final = norm_rows(hidden, gains_f[2 * L])
    final_low = final.astype(jnp.bfloat16)
    predicted = dense(final_low, w_out)
    error = predicted - noise
    part_pool = contract_rows(onehot, final, HIGH)
    squared_sum, pool_sum = sum_over_seq((jnp.sum(error * error), part_pool), 1)
    pooled = pool_sum / lengths_f
    audio_side = exact(pooled, w_audio_f)
    text_side = exact(captions, w_caption_f)
    clash, pull_clash = jax.vjp(contrast, audio_side, text_side)
    loss = squared_sum / (frames_group * channels) + contrast_weight * clash
    grad_audio_side, grad_text_side = pull_clash(jnp.float32(contrast_weight))
    grad_pred = (2.0 / (frames_group * channels) * error).astype(jnp.bfloat16)
    grad_w_out = contract_rows(grad_pred, final_low)
    grad_w_audio = contract_rows(pooled, grad_audio_side, HIGH)
    grad_w_caption = contract_rows(captions, grad_text_side, HIGH)
    grad_pooled = against_rows(grad_audio_side, w_audio_f, HIGH) / lengths_f
    grad_final = against_rows(grad_pred, w_out) + exact(onehot, grad_pooled)
    unused, pull_final = jax.vjp(norm_rows, hidden, gains_f[2 * L])
    grad_hidden, grad_gain_final = pull_final(grad_final)
    layer_grads = [None] * L
    own_grads = [None] * L
    twin_grads = [None] * L
    gain_grads = [None] * (2 * L + 1)
    gain_grads[2 * L] = grad_gain_final
    for depth in reversed(range(L)):
        weights = gathered[depth]
        grad_hidden, operand_pairs, grad_gain_one, grad_gain_two = layer_backward(
            grad_hidden, weights, gains_f[2 * depth], gains_f[2 * depth + 1], items, saved_all[depth]
        )
        gain_grads[2 * depth] = grad_gain_one
        gain_grads[2 * depth + 1] = grad_gain_two
        layer_grads[depth] = layer_gradients(operand_pairs)
        if depth > 0 and close:
            own_grads[depth] = [
                lax.psum_scatter(grad, "seq", scatter_dimension=0, tiled=True)
                for grad in layer_grads[depth]
            ]
    grad_w_in = contract_rows(noisy_low.astype(jnp.float32), grad_hidden, HIGH)
    grad_condition = contract_rows(onehot, grad_hidden, HIGH)
    grad_w_in, grad_w_out, grad_condition, gain_rows = sum_over_seq(
        (grad_w_in, grad_w_out, grad_condition, jnp.stack(gain_grads)), 2
    )
    grad_w_out = grad_w_out.T
    grad_w_time, grad_w_text, grad_null = pull_condition(grad_condition)
    other_flat = jnp.concatenate(
        [
            grad_w_in.ravel(),
            grad_w_out.ravel(),
            grad_w_time.ravel(),
            grad_w_text.ravel(),
            grad_w_audio.ravel(),
            grad_w_caption.ravel(),
            gain_rows.ravel(),
            grad_null,
        ]
    )
    other_grad = lax.dynamic_slice_in_dim(other_flat, rank * other_size, other_size)
    other_grad_square = jnp.sum(other_grad * other_grad)
    if close:
        other_grad_low = other_grad.astype(jnp.bfloat16)
        twin_other = swapped(other_grad_low).astype(jnp.float32)
        own_grads[0], twin_grads[0], square_part = scatter_layer(*layer_grads[0], 5)
        square_part = square_part + other_grad_square
        for depth in range(1, L):
            twin_grads[depth] = [swapped(grad) for grad in own_grads[depth]]
            for grad in own_grads[depth]:
                wide = grad.astype(jnp.float32)
                square_part = square_part + jnp.sum(wide * wide)
        norms = jnp.sqrt(sums_by_group(square_part, 3))
        total_norm = lax.dynamic_index_in_dim(norms, group, keepdims=False)
        twin_norm = lax.dynamic_index_in_dim(norms, 1 - group, keepdims=False)
        factor = jnp.minimum(1.0, clip_at / (total_norm + 1e-06))
        twin_factor = jnp.minimum(1.0, clip_at / (twin_norm + 1e-06))
        views = [flat_view(anchor_layers), first_view, second_view, flat_view(outer_layers)]
        stepped = step_layers(
            jnp.stack([factor, twin_factor]),
            [part for grads in own_grads for part in grads],
            [part for grads in twin_grads for part in grads],
            views + twin_views,
            seq_count,
        )
        new_layers, first_l, second_l, mean_layers, momentum_layers = map(from_view, stepped)
        first_o, second_o, _ = adam(other_grad * factor, first_other[0], second_other[0], anchor_other)

        def low(value):
            return lax.reduce_precision(value, 8, 7)

        delta_o = delta_of(low(other_grad) * factor, low(first_other[0]), low(second_other[0]), anchor_other)
        delta_twin = delta_of(twin_other * twin_factor, *twin_moments, anchor_other)
        mean_other = (delta_o + delta_twin) / 2
    else:
        stacked = jnp.stack(
            [
                flatten(
                    lax.psum_scatter(grad, "seq", scatter_dimension=0, tiled=True).astype(jnp.float32)
                    for grad in grads
                )
                for grads in layer_grads
            ]
        )
        total_norm = jnp.sqrt(lax.psum(jnp.sum(stacked * stacked) + other_grad_square, "seq"))
        factor = jnp.minimum(1.0, clip_at / (total_norm + 1e-06))
        first_l, second_l, delta_l = adam(
            stacked * factor, first_layers[0], second_layers[0], anchor_layers
        )
        first_o, second_o, delta_o = adam(
            other_grad * factor, first_other[0], second_other[0], anchor_other
        )
        mean_layers = group_mean(delta_l, group_count)
        mean_other = group_mean(delta_o, group_count)
        momentum_layers = outer_mu * outer_layers + mean_layers
        new_layers = anchor_layers - outer_rate * (mean_layers + outer_mu * momentum_layers)
    momentum_other = outer_mu * outer_other + mean_other
    new_other = anchor_other - outer_rate * (mean_other + outer_mu * momentum_other)
    return (
        new_layers,
        new_other,
        first_l[None],
        first_o[None],
        second_l[None],
        second_o[None],
        mean_layers,
        mean_other,
        momentum_layers,
        momentum_other,
        loss.reshape(1),
        total_norm.reshape(1),
    )


def solution(mesh):
    placed = (
        P(None, "seq"),
        P("seq"),
        P("grp", None, "seq"),
        P("grp", "seq"),
        P("grp", None, "seq"),
        P("grp", "seq"),
        P(None, "seq"),
        P("seq"),
        P(("grp", "seq"), None),
        P(("grp", "seq"), None),
        P("grp", None),
        P("grp", None),
        P("grp", None),
        P("grp", None, None),
    )
    return jax.shard_map(
        per_device,
        mesh=mesh,
        in_specs=placed,
        out_specs=(
            P(None, "seq"),
            P("seq"),
            P("grp", None, "seq"),
            P("grp", "seq"),
            P("grp", None, "seq"),
            P("grp", "seq"),
            P(None, "seq"),
            P("seq"),
            P(None, "seq"),
            P("seq"),
            P("grp"),
            P("grp"),
        ),
        check_vma=False,
    )
```

```python
import functools
import math

import jax
import jax.numpy as jnp
from jax import lax
from jax.experimental import pallas as pl
from jax.experimental.pallas import tpu as pltpu
from jax.sharding import PartitionSpec as P

D = 768
HEADS = 12
HD = 64
FF = 3072
E = 512
L = 2
TSTEPS = 1000
STEP_COUNT = 10


HIGH = lax.Precision.HIGHEST
beta_one = 0.9
beta_two = 0.95
adam_eps = 1e-08
decay_rate = 0.01
inner_rate = 0.02
outer_rate = 0.7
outer_mu = 0.9
clip_at = 0.01
logit_scale = 30.0
contrast_weight = 0.05


def block_of(rank, close):
    if not close:
        return rank
    turn = (rank // 4) % 2
    return rank + 2 * turn * (1 - 2 * ((rank // 2) % 2))


def passed_along(value, axis, steps, close):
    count = lax.axis_size(axis)
    holder = {block_of(rank, close): rank for rank in range(count)}
    initial, last = (max(0, -steps), min(count, count - steps))
    return lax.ppermute(
        value, axis, [(holder[source], holder[source + steps]) for source in range(initial, last)]
    )


def dense(left, right):
    return jnp.dot(left, right, preferred_element_type=jnp.float32)


def exact(left, right):
    return jnp.dot(left, right, precision=HIGH, preferred_element_type=jnp.float32)


def contract_rows(left, right, precision=None):
    return lax.dot_general(
        left,
        right,
        (((0,), (0,)), ((), ())),
        precision=precision,
        preferred_element_type=jnp.float32,
    )


def against_rows(left, right, precision=None):
    return lax.dot_general(
        left,
        right,
        (((1,), (1,)), ((), ())),
        precision=precision,
        preferred_element_type=jnp.float32,
    )


def carve(flat, shapes):
    pieces = []
    start = 0
    for shape in shapes:
        count = math.prod(shape)
        pieces.append(flat[start : start + count].reshape(shape))
        start += count
    return pieces


def layer_rows(piece, shards):
    cut = D // shards * (4 * D + FF)
    return piece[:cut].reshape(D // shards, 4 * D + FF), piece[cut:].reshape(FF // shards, D)


def split_upper(upper, lower):
    return [upper[:, : 3 * D], upper[:, 3 * D : 4 * D], upper[:, 4 * D :], lower]


def other_shapes(channels, width, text_width, joint_width, blocks):
    return [
        (channels, width),
        (width, channels),
        (width, width),
        (text_width, width),
        (width, joint_width),
        (text_width, joint_width),
        (2 * blocks + 1, width),
        (text_width,),
    ]


def norm_rows(hidden, gain):
    centred = hidden - jnp.mean(hidden, axis=-1, keepdims=True)
    return centred * lax.rsqrt(jnp.mean(centred * centred, axis=-1, keepdims=True) + 1e-05) * gain


def plan(steps):
    angle = (steps.astype(jnp.float32) / TSTEPS + 0.008) / 1.008 * (math.pi / 2)
    return jnp.cos(angle) ** 2


def time_features(steps):
    half = D // 2
    frequency = jnp.exp(-math.log(10000.0) * jnp.arange(half, dtype=jnp.float32) / half)
    angle = steps.astype(jnp.float32)[:, None] * frequency[None, :]
    return jnp.concatenate([jnp.cos(angle), jnp.sin(angle)], axis=1)


def contrast(audio_side, text_side):
    audio_unit = audio_side * lax.rsqrt(
        jnp.sum(audio_side * audio_side, axis=-1, keepdims=True) + 1e-06
    )
    text_unit = text_side * lax.rsqrt(
        jnp.sum(text_side * text_side, axis=-1, keepdims=True) + 1e-06
    )
    logits = logit_scale * jnp.dot(audio_unit, text_unit.T, precision=HIGH)
    diagonal = logit_scale * jnp.sum(audio_unit * text_unit, axis=-1)
    row_terms = jax.nn.logsumexp(logits, axis=1) - diagonal
    column_terms = jax.nn.logsumexp(logits, axis=0) - diagonal
    return 0.5 * (jnp.mean(row_terms) + jnp.mean(column_terms))


def gather_window(local_pairs, close):
    pieces = {}
    for step in (2, 1, -1, -2):
        pieces[step] = passed_along(local_pairs, "seq", step, close)
    return jnp.concatenate([pieces[2], pieces[1], local_pairs, pieces[-1], pieces[-2]], axis=0)


def return_window(grad_window, rows, close):
    total = grad_window[2 * rows : 3 * rows].astype(jnp.float32)
    for slot, step in ((0, 2), (1, 1), (3, -1), (4, -2)):
        total = total + passed_along(
            grad_window[slot * rows : (slot + 1) * rows], "seq", -step, close
        ).astype(jnp.float32)
    return total


LANES = 128
PAIRS = HEADS * HD // LANES
VMEM_LIMIT = 50 * 1024 * 1024


def lane_masks(dtype):
    lane = lax.broadcasted_iota(jnp.int32, (1, LANES), 1)
    return [(lane < HD).astype(dtype), (lane >= HD).astype(dtype)]


def fill_bias(bias_ref, query_item_ref, key_item_ref):
    keep = key_item_ref[...] == query_item_ref[...]
    bias_ref[...] = jnp.where(keep, 0.0, -1e30).astype(jnp.float32)


def attend_forward_kernel(q_ref, kv_ref, query_item_ref, key_item_ref, o_ref, lse_ref, bias_ref):
    fill_bias(bias_ref, query_item_ref, key_item_ref)
    width = HEADS * HD
    masks = lane_masks(jnp.bfloat16)
    lse_ref[...] = jnp.zeros_like(lse_ref)
    for pair in range(PAIRS):
        cols = slice(pair * LANES, (pair + 1) * LANES)
        query = q_ref[:, cols] * jnp.bfloat16(HD ** (-0.5))
        key_rows = kv_ref[:, cols]
        value_rows = kv_ref[:, width + pair * LANES : width + (pair + 1) * LANES]
        halves = []
        for half in range(2):
            scores = against_rows(key_rows, query * masks[half]) + bias_ref[...]
            peak = jnp.max(scores, axis=0, keepdims=True)
            weights = jnp.exp(scores - peak)
            total = jnp.sum(weights, axis=0, keepdims=True)
            shares = (weights * (1.0 / total)).astype(jnp.bfloat16)
            mixed = contract_rows(value_rows, shares)
            halves.append(mixed[half * HD : (half + 1) * HD])
            lse_ref[2 * pair + half : 2 * pair + half + 1, :] = peak + jnp.log(total)
        o_ref[:, cols] = jnp.concatenate(halves, axis=0).T.astype(o_ref.dtype)


def attend_forward(queries, window, query_item, key_item):
    rows, width = queries.shape
    span = window.shape[0]
    return pl.pallas_call(
        attend_forward_kernel,
        out_shape=(
            jax.ShapeDtypeStruct((rows, width), jnp.bfloat16),
            jax.ShapeDtypeStruct((16, rows), jnp.float32),
        ),
        in_specs=[pl.BlockSpec(memory_space=pltpu.VMEM)] * 4,
        out_specs=(pl.BlockSpec(memory_space=pltpu.VMEM),) * 2,
        scratch_shapes=[pltpu.VMEM((span, rows), jnp.float32)],
        compiler_params=pltpu.CompilerParams(vmem_limit_bytes=VMEM_LIMIT),
        cost_estimate=pl.CostEstimate(
            flops=4 * rows * span * width,
            transcendentals=rows * span * HEADS,
            bytes_accessed=4 * rows * width + 4 * span * width,
        ),
        name="attend_forward",
    )(queries, window, query_item[None, :], key_item[:, None])


def attend_backward_kernel(
    q_ref, kv_ref, do_ref, lse_ref, query_item_ref, key_item_ref, dq_ref, dkv_ref, bias_ref
):
    fill_bias(bias_ref, query_item_ref, key_item_ref)
    width = HEADS * HD
    masks = lane_masks(jnp.bfloat16)
    for pair in range(PAIRS):
        cols = slice(pair * LANES, (pair + 1) * LANES)
        value_cols = slice(width + pair * LANES, width + (pair + 1) * LANES)
        query = q_ref[:, cols] * jnp.bfloat16(HD ** (-0.5))
        key_rows = kv_ref[:, cols]
        value_rows = kv_ref[:, value_cols]
        grad_out = do_ref[:, cols]
        halves = []
        grad_key = grad_value = None
        for half in range(2):
            query_half = query * masks[half]
            grad_half = grad_out * masks[half]
            scores = against_rows(key_rows, query_half) + bias_ref[...]
            shares = jnp.exp(scores - lse_ref[2 * pair + half : 2 * pair + half + 1, :])
            grad_shares = against_rows(value_rows, grad_half)
            inner = jnp.sum(grad_shares * shares, axis=0, keepdims=True)
            grad_scores = (shares * (grad_shares - inner)).astype(jnp.bfloat16)
            one_value = dense(shares.astype(jnp.bfloat16), grad_half)
            one_key = dense(grad_scores, query_half)
            grad_value = one_value if grad_value is None else grad_value + one_value
            grad_key = one_key if grad_key is None else grad_key + one_key
            one_query = contract_rows(key_rows, grad_scores)
            halves.append(one_query[half * HD : (half + 1) * HD])
        grad_query = jnp.concatenate(halves, axis=0).T * HD ** (-0.5)
        dq_ref[:, cols] = grad_query.astype(dq_ref.dtype)
        dkv_ref[:, cols] = grad_key.astype(dkv_ref.dtype)
        dkv_ref[:, value_cols] = grad_value.astype(dkv_ref.dtype)


def attend_backward(queries, window, grad_out, lse, query_item, key_item):
    rows, width = queries.shape
    span = window.shape[0]
    return pl.pallas_call(
        attend_backward_kernel,
        out_shape=(
            jax.ShapeDtypeStruct((rows, width), jnp.bfloat16),
            jax.ShapeDtypeStruct((span, 2 * width), jnp.bfloat16),
        ),
        in_specs=[pl.BlockSpec(memory_space=pltpu.VMEM)] * 6,
        out_specs=(pl.BlockSpec(memory_space=pltpu.VMEM),) * 2,
        scratch_shapes=[pltpu.VMEM((span, rows), jnp.float32)],
        compiler_params=pltpu.CompilerParams(vmem_limit_bytes=VMEM_LIMIT),
        cost_estimate=pl.CostEstimate(
            flops=10 * rows * span * width,
            transcendentals=rows * span * HEADS,
            bytes_accessed=8 * rows * width + 8 * span * width,
        ),
        name="attend_backward",
    )(queries, window, grad_out, lse, query_item[None, :], key_item[:, None])


def layer_forward(hidden, normed, queries, window, weights, gain_two, items):
    proj_qkv, proj_out, proj_up, proj_down = weights
    attended, lse = attend_forward(queries, window, *items)
    middle = hidden + dense(attended, proj_out)
    second = norm_rows(middle, gain_two).astype(jnp.bfloat16)
    upper = dense(second, proj_up)
    activated = jax.nn.gelu(upper, approximate=True).astype(jnp.bfloat16)
    return (
        middle + dense(activated, proj_down),
        (normed, queries, window, lse, attended, middle, second, upper, activated),
    )


def layer_backward(grad_hidden, weights, gain_two, items, saved):
    normed, queries, window, lse, attended, middle, second, upper, activated = saved
    proj_qkv, proj_out, proj_up, proj_down = weights
    branch_top = grad_hidden.astype(jnp.bfloat16)
    grad_activated = against_rows(branch_top, proj_down)
    unused, pull_gelu = jax.vjp(lambda value: jax.nn.gelu(value, approximate=True), upper)
    grad_upper = pull_gelu(grad_activated)[0].astype(jnp.bfloat16)
    grad_second = against_rows(grad_upper, proj_up)
    unused, pull_two = jax.vjp(norm_rows, middle, gain_two)
    grad_middle, grad_gain_two = pull_two(grad_second)
    grad_middle = grad_middle + grad_hidden
    branch_mid = grad_middle.astype(jnp.bfloat16)
    grad_attended = against_rows(branch_mid, proj_out).astype(jnp.bfloat16)
    grad_query, grad_window = attend_backward(queries, window, grad_attended, lse, *items)
    operand_pairs = (attended, branch_mid, second, grad_upper, activated, branch_top)
    return grad_middle, grad_query, grad_window, operand_pairs, grad_gain_two


def layer_gradients(qkv_parts, operand_pairs):
    attended, branch_mid, second, grad_upper, activated, branch_top = operand_pairs
    pairs = qkv_parts + [(attended, branch_mid), (second, grad_upper)]
    upper_full = jnp.concatenate(
        [contract_rows(left, right).astype(jnp.bfloat16) for left, right in pairs], axis=1
    )
    lower_full = contract_rows(activated, branch_top).astype(jnp.bfloat16)
    return upper_full, lower_full


def frame_window(frames, gathered_frames, own_block, close):
    if close:
        count = gathered_frames.shape[0]
        parts = [
            lax.dynamic_index_in_dim(
                gathered_frames, jnp.clip(own_block + step, 0, count - 1), keepdims=False
            )
            for step in range(-2, 3)
        ]
    else:
        parts = [passed_along(frames, "seq", -step, close) for step in range(-2, 0)] + [frames]
        parts += [passed_along(frames, "seq", -step, close) for step in range(1, 3)]
    return jnp.concatenate(parts, axis=1)


def thirds_left(value):
    items = value.shape[0]
    thirds = value.reshape(items, -1, 3)
    zero = jnp.zeros_like(thirds[:, :, 0])
    even = jnp.concatenate([thirds[:, :, 0], thirds[:, :, 1], zero, zero], axis=0)
    odd = jnp.concatenate([zero, zero, thirds[:, :, 1], thirds[:, :, 2]], axis=0)
    return jnp.stack([even, odd], axis=2).reshape(4 * items, -1)


def thirds_right(value):
    half = value.shape[1] // 2
    wide = jnp.zeros_like(value)
    narrow = wide[:, :half]
    return jnp.concatenate(
        [
            jnp.concatenate([value, narrow], axis=1),
            jnp.concatenate([wide, value[:, :half]], axis=1),
            jnp.concatenate([value[:, half:], wide], axis=1),
            jnp.concatenate([narrow, value], axis=1),
        ],
        axis=0,
    )


def adam(grad, first, second, anchor):
    first = beta_one * first + (1.0 - beta_one) * grad
    second = beta_two * second + (1.0 - beta_two) * grad * grad
    stepped = first / (1.0 - beta_one**STEP_COUNT)
    scaled = second / (1.0 - beta_two**STEP_COUNT)
    delta = inner_rate * (stepped / (jnp.sqrt(scaled) + adam_eps) + decay_rate * anchor)
    return (first, second, delta)


MESH = pl.DeviceIdType.MESH
SUBLANES = 8
CLOSE_RANKS = 16


def greet_seq(me, count):
    group = lax.axis_index("grp")
    barrier = pltpu.get_barrier_semaphore()

    def one(step, carry):
        pl.semaphore_signal(
            barrier, inc=1, device_id=(group, lax.rem(me + step, count)), device_id_type=MESH
        )
        return carry

    lax.fori_loop(1, count, one, 0)
    pl.semaphore_wait(barrier, count - 1)


def sum_kernel(count, x_ref, out_ref, parts, own, totals, send_one, recv_one, send_two, recv_two):
    me = lax.axis_index("seq")
    group = lax.axis_index("grp")
    greet_seq(me, count)

    def slice_copy(step):
        peer = lax.rem(me + step, count)
        return pltpu.make_async_remote_copy(
            src_ref=x_ref.at[peer],
            dst_ref=parts.at[step],
            send_sem=send_one.at[step],
            recv_sem=recv_one.at[step],
            device_id=(group, peer),
            device_id_type=MESH,
        )

    def total_copy(step):
        peer = lax.rem(me + step, count)
        return pltpu.make_async_remote_copy(
            src_ref=own,
            dst_ref=totals.at[step],
            send_sem=send_two.at[step],
            recv_sem=recv_two.at[step],
            device_id=(group, peer),
            device_id_type=MESH,
        )

    def start_of(make):
        def one(step, carry):
            make(step).start()
            return carry

        return one

    lax.fori_loop(1, count, start_of(slice_copy), 0)
    own[...] = x_ref[me]

    def gather_in(step, carry):
        slice_copy(step).wait()
        own[...] += parts[step]
        return carry

    lax.fori_loop(1, count, gather_in, 0)
    lax.fori_loop(1, count, start_of(total_copy), 0)
    out_ref[me] = own[...]

    def spread(step, carry):
        total_copy(step).wait()
        out_ref[lax.rem(me + count - step, count)] = totals[step]
        return carry

    lax.fori_loop(1, count, spread, 0)


def sum_over_seq(values, collective):
    count = lax.axis_size("seq")
    if count != CLOSE_RANKS:
        return lax.psum(values, "seq")
    sizes = [math.prod(value.shape) for value in values]
    block = -(-sum(sizes) // (count * SUBLANES * LANES)) * SUBLANES
    flat = jnp.concatenate([value.reshape(-1) for value in values])
    flat = jnp.pad(flat, (0, count * block * LANES - flat.shape[0]))
    shape = (count, block, LANES)
    total = pl.pallas_call(
        functools.partial(sum_kernel, count),
        out_shape=jax.ShapeDtypeStruct(shape, jnp.float32),
        in_specs=[pl.BlockSpec(memory_space=pltpu.VMEM)],
        out_specs=pl.BlockSpec(memory_space=pltpu.VMEM),
        scratch_shapes=[
            pltpu.VMEM(shape, jnp.float32),
            pltpu.VMEM(shape[1:], jnp.float32),
            pltpu.VMEM(shape, jnp.float32),
        ]
        + [pltpu.SemaphoreType.DMA((count,))] * 4,
        compiler_params=pltpu.CompilerParams(collective_id=collective, has_side_effects=True),
        cost_estimate=pl.CostEstimate(
            flops=math.prod(shape), transcendentals=0, bytes_accessed=16 * math.prod(shape)
        ),
        name="sum_over_seq",
    )(flat.reshape(shape))
    return carve(total.reshape(-1), [value.shape for value in values])


def share_kernel(count, x_ref, out_ref, parts, send_sem, recv_sem):
    seq = lax.axis_size("seq")
    me = lax.axis_index("grp") * seq + lax.axis_index("seq")

    def place(step):
        peer = lax.rem(me + step, count)
        return peer // seq, lax.rem(peer, seq)

    barrier = pltpu.get_barrier_semaphore()

    def greet(step, carry):
        pl.semaphore_signal(barrier, inc=1, device_id=place(step), device_id_type=MESH)
        return carry

    lax.fori_loop(1, count, greet, 0)
    pl.semaphore_wait(barrier, count - 1)

    def copy_of(step):
        return pltpu.make_async_remote_copy(
            src_ref=x_ref,
            dst_ref=parts.at[step],
            send_sem=send_sem.at[step],
            recv_sem=recv_sem.at[step],
            device_id=place(step),
            device_id_type=MESH,
        )

    def start(step, carry):
        copy_of(step).start()
        return carry

    lax.fori_loop(1, count, start, 0)
    out_ref[me] = x_ref[...]

    def finish(step, carry):
        copy_of(step).wait()
        out_ref[lax.rem(me + count - step, count)] = parts[step]
        return carry

    lax.fori_loop(1, count, finish, 0)


def sums_by_group(value, collective):
    groups, count = lax.axis_size("grp"), lax.axis_size("seq")
    shape = (groups * count, SUBLANES, LANES)
    shared = pl.pallas_call(
        functools.partial(share_kernel, groups * count),
        out_shape=jax.ShapeDtypeStruct(shape, jnp.float32),
        in_specs=[pl.BlockSpec(memory_space=pltpu.VMEM)],
        out_specs=pl.BlockSpec(memory_space=pltpu.VMEM),
        scratch_shapes=[pltpu.VMEM(shape, jnp.float32)]
        + [pltpu.SemaphoreType.DMA((groups * count,))] * 2,
        compiler_params=pltpu.CompilerParams(collective_id=collective, has_side_effects=True),
        name="share_over_all",
    )(jnp.full(shape[1:], value, jnp.float32))
    return jnp.sum(shared[:, 0, 0].reshape(groups, count), axis=1)


GRID = (4, 2, 2)
GATHER_Y_LAG = 2
GATHER_X_LAG = 5
GATHER_AHEAD = 1
GATHER_LANES = 256


def place_of(me):
    return me // 4, lax.rem(me // 2, 2), lax.rem(me, 2)


def rank_of(along, across, core):
    return (along * 2 + across) * 2 + core


def gather_kernel(shared, *refs):
    pieces = len(shared)
    own_refs, out_refs = refs[:pieces], refs[pieces : 2 * pieces]
    local_sem, z_send, z_recv, y_send, y_recv, x_send, x_recv, c_send, c_recv = refs[2 * pieces :]
    group, me = lax.axis_index("grp"), lax.axis_index("seq")
    z, y, core = place_of(me)
    z_size = GRID[0]
    across, sibling, twin = (
        (group, rank_of(z, 1 - y, core)),
        (group, rank_of(z, y, 1 - core)),
        (1 - group, me),
    )
    barrier = pltpu.get_barrier_semaphore()
    for there in (across, sibling, twin):
        pl.semaphore_signal(barrier, inc=1, device_id=there, device_id_type=MESH)

    @pl.when(z > 0)
    def _():
        pl.semaphore_signal(
            barrier, inc=1, device_id=(group, rank_of(z - 1, y, core)), device_id_type=MESH
        )

    @pl.when(z < z_size - 1)
    def _():
        pl.semaphore_signal(
            barrier, inc=1, device_id=(group, rank_of(z + 1, y, core)), device_id_type=MESH
        )

    neighbours = (z > 0).astype(jnp.int32) + (z < z_size - 1).astype(jnp.int32)
    pl.semaphore_wait(barrier, 3 + neighbours)

    def half_of(ref, piece, half):
        if half is None:
            return ref
        span = ref.shape[-1] // 2
        return ref.at[:, pl.ds(pl.multiple_of(half * span, LANES), span)]

    def move(piece, half, there, along, over, send, recv, own=False):
        dst = half_of(out_refs[piece].at[rank_of(along, over, core)], piece, half)
        src = half_of(own_refs[piece], piece, half) if own else dst
        return pltpu.make_async_remote_copy(
            src_ref=src, dst_ref=dst, send_sem=send, recv_sem=recv, device_id=there, device_id_type=MESH
        )

    def z_move(piece, along, forward, own=False):
        there = (group, rank_of(z + (1 if forward else -1), y, core))
        half = group if shared[piece] else None
        return move(
            piece, half, there, along, y, z_send.at[piece, along, int(forward)], z_recv.at[piece, along], own
        )

    def y_move(piece, along, own=False, over=None):
        half = group if shared[piece] else None
        over = y if over is None else over
        return move(piece, half, across, along, over, y_send.at[piece, along], y_recv.at[piece, along], own)

    def x_move(piece, along, over, arriving=False):
        half = 1 - group if arriving else group
        slot = along * 2 + over
        return move(piece, half, twin, along, over, x_send.at[piece, slot], x_recv.at[piece, slot])

    def c_move(piece, along, over, half, slot, own=False):
        return move(
            piece,
            half,
            sibling,
            along,
            over,
            c_send.at[piece, along * 2 + over, slot],
            c_recv.at[piece, along * 2 + over, slot],
            own,
        )

    def each_along(distance, action):
        if distance == 0:
            action(z, True, True)
            return

        @pl.when(z - distance >= 0)
        def _():
            action(z - distance, True, False)

        @pl.when(z + distance < z_size)
        def _():
            action(z + distance, False, True)

    def own_sends(piece):
        pltpu.make_async_copy(own_refs[piece], out_refs[piece].at[me], local_sem.at[piece]).start()

        @pl.when(z + 1 < z_size)
        def _():
            z_move(piece, z, True, own=True).start()

        @pl.when(z > 0)
        def _():
            z_move(piece, z, False, own=True).start()

        y_move(piece, z, own=True).start()
        c_move(piece, z, y, None, 0, own=True).start()

    def z_arrivals(piece, distance):
        if distance == 0:
            return

        def one(along, onward, backward):
            z_move(piece, along, onward).wait_recv()

            @pl.when((z + 1 < z_size) if onward else (z > 0))
            def _():
                z_move(piece, along, onward).start()

            y_move(piece, along).start()
            if shared[piece]:
                x_move(piece, along, y).start()
            c_move(piece, along, y, group if shared[piece] else None, 0).start()

        each_along(distance, one)

    def y_arrivals(piece, distance):
        def one(along, *_):
            y_move(piece, along, over=1 - y).wait_recv()
            if shared[piece]:
                x_move(piece, along, 1 - y).start()
            c_move(piece, along, 1 - y, group if shared[piece] else None, 0).start()

        each_along(distance, one)

    def x_arrivals(piece, distance):
        if not shared[piece]:
            return

        def one(along, *_):
            for turn in range(2):
                over = y if turn == 0 else 1 - y
                if distance == 0 and turn == 0:
                    continue
                x_move(piece, along, over, arriving=True).wait_recv()
                c_move(piece, along, over, 1 - group, 1).start()

        each_along(distance, one)

    def drain(piece, distance):
        def one(along, onward, backward):
            own = distance == 0
            half = group if shared[piece] else None
            for turn in range(2):
                over = y if turn == 0 else 1 - y
                mine = own and turn == 0
                whole = None if mine else half
                c_move(piece, along, over, whole, 0).wait()
                if shared[piece] and not mine:
                    c_move(piece, along, over, 1 - group, 1).wait()
                    x_move(piece, along, over).wait_send()
            y_move(piece, along).wait_send()
            if onward:

                @pl.when(z + 1 < z_size)
                def _():
                    z_move(piece, along, True).wait_send()

            if backward:

                @pl.when(z > 0)
                def _():
                    z_move(piece, along, False).wait_send()

        each_along(distance, one)
        if distance == 0:
            pltpu.make_async_copy(own_refs[piece], out_refs[piece].at[me], local_sem.at[piece]).wait()

    slots = [(piece, distance) for piece in range(pieces) for distance in range(z_size)]
    own_sends(0)
    for turn in range(len(slots) + GATHER_X_LAG):
        if turn < len(slots):
            piece, distance = slots[turn]
            if distance == GATHER_AHEAD and piece + 1 < pieces:
                own_sends(piece + 1)
            z_arrivals(piece, distance)
        if 0 <= turn - GATHER_Y_LAG < len(slots):
            y_arrivals(*slots[turn - GATHER_Y_LAG])
        if 0 <= turn - GATHER_X_LAG < len(slots):
            x_arrivals(*slots[turn - GATHER_X_LAG])
    for slot in slots:
        drain(*slot)


def gather_pieces(pieces, shared, collective):
    count = lax.axis_size("seq")
    if count != math.prod(GRID) or lax.axis_size("grp") != 2:
        return [lax.all_gather(piece, "seq", axis=0) for piece in pieces]
    amount = len(pieces)
    sems = [
        (amount,),
        (amount, 4, 2),
        (amount, 4),
        (amount, 4),
        (amount, 4),
        (amount, 8),
        (amount, 8),
        (amount, 8, 2),
        (amount, 8, 2),
    ]
    return pl.pallas_call(
        functools.partial(gather_kernel, tuple(shared)),
        out_shape=[jax.ShapeDtypeStruct((count,) + piece.shape, piece.dtype) for piece in pieces],
        in_specs=[pl.BlockSpec(memory_space=pl.ANY)] * amount,
        out_specs=[pl.BlockSpec(memory_space=pl.ANY)] * amount,
        scratch_shapes=[pltpu.SemaphoreType.DMA(shape) for shape in sems],
        compiler_params=pltpu.CompilerParams(collective_id=collective, has_side_effects=True),
        name="gather_pieces",
    )(*pieces)


ROW_GROUP = 16
UPPER_CUTS = 3
LOWER_CUTS = 1
SCATTER_LAG = 2


def scatter_kernel(pieces, amount, *refs):
    grads, outs, twins = (refs[k * amount : (k + 1) * amount] for k in range(3))
    squares = refs[3 * amount]
    rest = refs[3 * amount + 1 :]
    count = len(pieces)
    own, beside, facing, from_left, from_right, ready = (
        rest[k * count : (k + 1) * count] for k in range(6)
    )
    load_sem, c_send, c_recv, y_send, y_recv, z_send, z_recv, x_send, x_recv = rest[6 * count :]
    group, me = lax.axis_index("grp"), lax.axis_index("seq")
    z, y, core = place_of(me)
    z_size = GRID[0]
    across, sibling = (group, rank_of(z, 1 - y, core)), (group, rank_of(z, y, 1 - core))
    twin = (1 - group, me)
    left, right = (group, rank_of(z - 1, y, core)), (group, rank_of(z + 1, y, core))
    has_left, has_right = z > 0, z < z_size - 1
    barrier = pltpu.get_barrier_semaphore()
    for there in (across, sibling, twin):
        pl.semaphore_signal(barrier, inc=1, device_id=there, device_id_type=MESH)

    @pl.when(has_left)
    def _():
        pl.semaphore_signal(barrier, inc=1, device_id=left, device_id_type=MESH)

    @pl.when(has_right)
    def _():
        pl.semaphore_signal(barrier, inc=1, device_id=right, device_id_type=MESH)

    neighbours = has_left.astype(jnp.int32) + has_right.astype(jnp.int32)
    pl.semaphore_wait(barrier, 3 + neighbours)
    squares[...] = jnp.zeros_like(squares)

    def part(piece, along, over, owner):
        which, row, rows, column, columns = pieces[piece]
        return grads[which].at[rank_of(along, over, owner), pl.ds(row, rows), pl.ds(column, columns)]

    def load(piece, along, over):
        slot = along * 2 + over
        return pltpu.make_async_copy(
            part(piece, along, over, core), own[piece].at[slot], load_sem.at[piece, slot]
        )

    def remote(src, dst, send, recv, there):
        return pltpu.make_async_remote_copy(
            src_ref=src, dst_ref=dst, send_sem=send, recv_sem=recv, device_id=there, device_id_type=MESH
        )

    def c_move(piece, along, over):
        slot = along * 2 + over
        return remote(
            part(piece, along, over, 1 - core),
            beside[piece].at[slot],
            c_send.at[piece, slot],
            c_recv.at[piece, slot],
            sibling,
        )

    def y_move(piece, along):
        return remote(
            own[piece].at[along * 2 + 1 - y],
            facing[piece].at[along],
            y_send.at[piece, along],
            y_recv.at[piece, along],
            across,
        )

    def z_move(piece, along, forward):
        side = 0 if forward else 1
        return remote(
            facing[piece].at[along],
            (from_left if forward else from_right)[piece].at[along],
            z_send.at[piece, along],
            z_recv.at[piece, along, side],
            right if forward else left,
        )

    def x_move(piece):
        which, row, height, column, columns = pieces[piece]
        return remote(
            ready[piece],
            twins[which].at[pl.ds(row, height), pl.ds(column, columns)],
            x_send.at[piece],
            x_recv.at[piece],
            twin,
        )

    def each_along(distance, action):
        if distance == 0:
            action(z, None)
            return

        @pl.when(z - distance >= 0)
        def _():
            action(z - distance, False)

        @pl.when(z + distance < z_size)
        def _():
            action(z + distance, True)

    def by_rows(piece, body):
        def one(step, carry):
            body(pl.ds(pl.multiple_of(step * ROW_GROUP, ROW_GROUP), ROW_GROUP))
            return carry

        lax.fori_loop(0, pieces[piece][2] // ROW_GROUP, one, 0)

    def wide(ref, slot, rows):
        return ref[slot, rows, :].astype(jnp.float32)

    def begin(piece):
        for distance in reversed(range(z_size)):

            def one(along, _):
                for over in range(2):
                    load(piece, along, over).start()
                    c_move(piece, along, over).start()

            each_along(distance, one)

    def c_stage(piece, distance):
        def one(along, _):
            for turn in range(2):
                over = 1 - y if turn == 0 else y
                slot = along * 2 + over
                load(piece, along, over).wait()
                c_move(piece, along, over).wait_recv()

                def add(rows):
                    total = wide(own[piece], slot, rows) + wide(beside[piece], slot, rows)
                    own[piece][slot, rows, :] = total.astype(jnp.bfloat16)

                by_rows(piece, add)
                if turn == 0:
                    y_move(piece, along).start()

        each_along(distance, one)

    def y_stage(piece, distance):
        which, row, height, column, columns = pieces[piece]

        def one(along, forward):
            y_move(piece, along).wait_recv()
            slot = along * 2 + y
            if forward is None:

                def add(rows):
                    total = wide(own[piece], slot, rows) + wide(facing[piece], along, rows)
                    there = pl.ds(pl.multiple_of(row + rows.start, ROW_GROUP), ROW_GROUP)
                    outs[which][there, pl.ds(column, columns)] = total

                by_rows(piece, add)
                for side, present, source in ((True, has_left, from_left), (False, has_right, from_right)):

                    @pl.when(present)
                    def _():
                        z_move(piece, along, side).wait_recv()

                        def more(rows):
                            there = pl.ds(pl.multiple_of(row + rows.start, ROW_GROUP), ROW_GROUP)
                            outs[which][there, pl.ds(column, columns)] += wide(source[piece], along, rows)

                        by_rows(piece, more)

                def finish(rows):
                    there = pl.ds(pl.multiple_of(row + rows.start, ROW_GROUP), ROW_GROUP)
                    total = outs[which][there, pl.ds(column, columns)]
                    ready[piece][rows, :] = total.astype(jnp.bfloat16)
                    square = total[:SUBLANES] * total[:SUBLANES] + total[SUBLANES:] * total[SUBLANES:]
                    for k in range(columns // LANES):
                        squares[...] += square[:, k * LANES : (k + 1) * LANES]

                by_rows(piece, finish)
                x_move(piece).start()
                return
            source, present = (from_left, has_left) if forward else (from_right, has_right)

            @pl.when(present)
            def _():
                z_move(piece, along, forward).wait_recv()

                def add(rows):
                    total = wide(own[piece], slot, rows) + wide(facing[piece], along, rows)
                    total = total + wide(source[piece], along, rows)
                    facing[piece][along, rows, :] = total.astype(jnp.bfloat16)

                by_rows(piece, add)

            @pl.when(jnp.logical_not(present))
            def _():
                def add(rows):
                    total = wide(own[piece], slot, rows) + wide(facing[piece], along, rows)
                    facing[piece][along, rows, :] = total.astype(jnp.bfloat16)

                by_rows(piece, add)

            z_move(piece, along, forward).start()

        each_along(distance, one)

    def drain(piece, distance):
        def one(along, forward):
            for over in range(2):
                c_move(piece, along, over).wait_send()
            y_move(piece, along).wait_send()
            if forward is not None:
                z_move(piece, along, forward).wait_send()

        each_along(distance, one)

    slots = [(piece, distance) for piece in range(count) for distance in reversed(range(z_size))]
    for piece in range(min(2, count)):
        begin(piece)
    for turn in range(len(slots) + SCATTER_LAG):
        if turn < len(slots):
            c_stage(*slots[turn])
            piece, distance = slots[turn]
            if distance == 0 and piece + 2 < count:
                begin(piece + 2)
        if turn >= SCATTER_LAG:
            y_stage(*slots[turn - SCATTER_LAG])
    for slot in slots:
        drain(*slot)
    for piece in range(count):
        x_move(piece).wait()


def scatter_layer(upper, lower, collective):
    count = math.prod(GRID)
    grads = [grad.reshape(count, grad.shape[0] // count, grad.shape[1]) for grad in (upper, lower)]
    pieces = []
    for which, cuts in ((0, UPPER_CUTS), (1, LOWER_CUTS)):
        rows, columns = grads[which].shape[1:]
        if which == 0:
            pieces += [(0, 0, rows, k * (columns // cuts), columns // cuts) for k in range(cuts)]
        else:
            pieces += [(1, k * (rows // cuts), rows // cuts, 0, columns) for k in range(cuts)]
    amount = len(pieces)
    places = math.prod(GRID[:2])

    def room(slots):
        return [pltpu.VMEM((slots, piece[2], piece[4]), jnp.bfloat16) for piece in pieces]

    sems = [
        (amount, places),
        (amount, places),
        (amount, places),
        (amount, GRID[0]),
        (amount, GRID[0]),
        (amount, GRID[0]),
        (amount, GRID[0], 2),
        (amount,),
        (amount,),
    ]
    own_upper, own_lower, twin_upper, twin_lower, squares = pl.pallas_call(
        functools.partial(scatter_kernel, tuple(pieces), 2),
        out_shape=[jax.ShapeDtypeStruct(grad.shape[1:], jnp.float32) for grad in grads]
        + [jax.ShapeDtypeStruct(grad.shape[1:], jnp.bfloat16) for grad in grads]
        + [jax.ShapeDtypeStruct((SUBLANES, LANES), jnp.float32)],
        in_specs=[pl.BlockSpec(memory_space=pl.ANY)] * 2,
        out_specs=[pl.BlockSpec(memory_space=pltpu.VMEM)] * 2
        + [pl.BlockSpec(memory_space=pl.ANY)] * 2
        + [pl.BlockSpec(memory_space=pltpu.VMEM)],
        scratch_shapes=room(places)
        + room(places)
        + room(GRID[0])
        + room(GRID[0])
        + room(GRID[0])
        + [pltpu.VMEM((piece[2], piece[4]), jnp.bfloat16) for piece in pieces]
        + [pltpu.SemaphoreType.DMA(shape) for shape in sems],
        compiler_params=pltpu.CompilerParams(
            collective_id=collective, has_side_effects=True, vmem_limit_bytes=VMEM_LIMIT
        ),
        name="scatter_layer",
    )(*grads)
    return (own_upper, own_lower), (twin_upper, twin_lower), jnp.sum(squares)


def lay_out_kernel(shards, view_ref, *outs):
    cut = D // shards * (4 * D + FF) // LANES
    for layer in range(L):
        upper, lower = outs[2 * layer : 2 * layer + 2]
        for ref, base in ((upper, 0), (lower, cut)):
            across = ref.shape[1] // LANES
            for row in range(0, ref.shape[0], ROW_GROUP):
                for column in range(across):
                    start = L * (base + row * across + column) + layer
                    rows = view_ref[pl.ds(start, ROW_GROUP, stride=L * across), :]
                    ref[row : row + ROW_GROUP, column * LANES : (column + 1) * LANES] = rows.astype(
                        jnp.bfloat16
                    )


def flat_view(array):
    layers, size = array.shape
    return array.reshape(layers, size // LANES, LANES).transpose(1, 0, 2).reshape(-1, LANES)


def lay_out(anchor, shards):
    if shards != math.prod(GRID):
        return [layer_rows(anchor[depth].astype(jnp.bfloat16), shards) for depth in range(L)]
    shapes = [(D // shards, 4 * D + FF), (FF // shards, D)] * L
    outs = pl.pallas_call(
        functools.partial(lay_out_kernel, shards),
        out_shape=[jax.ShapeDtypeStruct(shape, jnp.bfloat16) for shape in shapes],
        in_specs=[pl.BlockSpec(memory_space=pltpu.VMEM)],
        out_specs=[pl.BlockSpec(memory_space=pltpu.VMEM)] * len(shapes),
        compiler_params=pltpu.CompilerParams(vmem_limit_bytes=VMEM_LIMIT),
        name="lay_out",
    )(flat_view(anchor))
    return [(outs[2 * depth], outs[2 * depth + 1]) for depth in range(L)]


def flatten(parts):
    return jnp.concatenate([part.reshape(-1) for part in parts])


def group_mean(delta, count):
    low = lax.reduce_precision(delta, 8, 7)
    total = low
    for step in range(1, count):
        moves = [(source, (source + step) % count) for source in range(count)]
        total = total + lax.ppermute(low.astype(jnp.bfloat16), "grp", moves).astype(jnp.float32)
    return total / count


STEP_BLOCKS = 8


def delta_of(grad, first, second, anchor):
    return adam(grad, first, second, anchor)[2]


def step_kernel(cut, factors, *refs):
    own, twin = refs[: 2 * L], refs[2 * L : 4 * L]
    anchor, first, second, outer, twin_first, twin_second = refs[4 * L : 4 * L + 6]
    new, one, two, mean_out, momentum_out, own_flat, twin_flat = refs[4 * L + 6 :]
    step = pl.program_id(0)
    block = anchor.shape[0]

    @pl.when(step == 0)
    def _():
        for grads, flat in ((own, own_flat), (twin, twin_flat)):
            for layer in range(L):
                for ref, base in zip(grads[2 * layer : 2 * layer + 2], (0, cut)):
                    across = ref.shape[1] // LANES
                    for row in range(0, ref.shape[0], ROW_GROUP):
                        for column in range(across):
                            start = L * (base + row * across + column) + layer
                            flat[pl.ds(start, ROW_GROUP, stride=L * across), :] = ref[
                                row : row + ROW_GROUP, column * LANES : (column + 1) * LANES
                            ].astype(jnp.float32)

    def low(value):
        return value.astype(jnp.bfloat16).astype(jnp.float32)

    rows = pl.ds(pl.multiple_of(step * block, SUBLANES), block)
    grad, weight = own_flat[rows, :], anchor[...]
    first_own, second_own = first[...], second[...]
    clipped = grad * factors[0]
    one[...] = beta_one * first_own + (1.0 - beta_one) * clipped
    two[...] = beta_two * second_own + (1.0 - beta_two) * clipped * clipped
    delta_own = delta_of(low(grad) * factors[0], low(first_own), low(second_own), weight)
    delta_twin = delta_of(
        twin_flat[rows, :] * factors[1],
        twin_first[...].astype(jnp.float32),
        twin_second[...].astype(jnp.float32),
        weight,
    )
    mean = (delta_own + delta_twin) / 2
    momentum = outer_mu * outer[...] + mean
    mean_out[...] = mean
    momentum_out[...] = momentum
    new[...] = weight - outer_rate * (mean + outer_mu * momentum)


def step_layers(factors, own, twin, views, shards):
    rows = views[0].shape[0]
    block = rows // STEP_BLOCKS
    whole = pl.BlockSpec(memory_space=pltpu.VMEM)
    part = pl.BlockSpec((block, LANES), lambda k: (k, 0))
    return pl.pallas_call(
        functools.partial(step_kernel, D // shards * (4 * D + FF) // LANES),
        grid=(STEP_BLOCKS,),
        out_shape=[jax.ShapeDtypeStruct((rows, LANES), jnp.float32)] * 5,
        in_specs=[pl.BlockSpec(memory_space=pltpu.SMEM)] + [whole] * (4 * L) + [part] * 6,
        out_specs=[part] * 5,
        scratch_shapes=[pltpu.VMEM((rows, LANES), jnp.float32)] * 2,
        compiler_params=pltpu.CompilerParams(
            vmem_limit_bytes=VMEM_LIMIT, dimension_semantics=("arbitrary",)
        ),
        name="step_layers",
    )(factors, *own, *twin, *views)


def from_view(view):
    rows, lanes = view.shape
    return view.reshape(rows // L, L, lanes).transpose(1, 0, 2).reshape(L, rows // L * lanes)


def swapped(value):
    return lax.ppermute(value, "grp", [(0, 1), (1, 0)])


def per_device(
    anchor_layers,
    anchor_other,
    first_layers,
    first_other,
    second_layers,
    second_other,
    outer_layers,
    outer_other,
    latents,
    noise,
    lengths,
    timesteps,
    null_flags,
    captions,
):
    seq_count = lax.axis_size("seq")
    group_count = lax.axis_size("grp")
    rank = lax.axis_index("seq")
    group = lax.axis_index("grp")
    close = seq_count == math.prod(GRID) and group_count == 2
    rows = latents.shape[0]
    channels = latents.shape[1]
    frames_group = rows * seq_count
    lengths = lengths[0]
    timesteps = timesteps[0]
    null_flags = null_flags[0]
    captions = captions[0]
    item_count = lengths.shape[0]
    text_width = captions.shape[1]
    other_size = anchor_other.shape[0]
    padded = -(-other_size // 4096) * 4096
    other_rows = jnp.pad(anchor_other.astype(jnp.bfloat16), (0, padded - other_size))
    own_rows = lay_out(anchor_layers, seq_count)
    early = L
    own_block = block_of(rank, close)
    frames = jnp.concatenate([latents, noise], axis=1).T
    pieces = [frames, other_rows.reshape(-1, GATHER_LANES)]
    pieces += [part for pair in own_rows[:early] for part in pair]
    gathered_frames, other_rows, *early_rows = gather_pieces(
        pieces, [False, True] + [True, False] * early, 4
    )
    if close:
        first_view, second_view = flat_view(first_layers[0]), flat_view(second_layers[0])
        sources, other_rows = lax.optimization_barrier(
            ((first_view, second_view, first_other[0], second_other[0]), other_rows)
        )
        twin_views = [swapped(value.astype(jnp.bfloat16)) for value in sources[:2]]
        twin_moments = [swapped(value.astype(jnp.bfloat16)).astype(jnp.float32) for value in sources[2:]]
    late_rows = [lax.all_gather(part, "seq", axis=0) for pair in own_rows[early:] for part in pair]
    layer_parts = [part.reshape(-1, part.shape[-1]) for part in early_rows + late_rows]
    gathered = [split_upper(*layer_parts[2 * depth : 2 * depth + 2]) for depth in range(L)]
    other_low = other_rows.reshape(seq_count, padded)[:, :other_size].reshape(-1)
    w_in, w_out, w_time, w_text, w_audio, w_caption, gains, null_text = carve(
        other_low, other_shapes(channels, D, text_width, E, L)
    )
    w_time_f = w_time.astype(jnp.float32)
    w_text_f = w_text.astype(jnp.float32)
    w_audio_f = w_audio.astype(jnp.float32)
    w_caption_f = w_caption.astype(jnp.float32)
    gains_f = gains.astype(jnp.float32)
    null_f = null_text.astype(jnp.float32)
    places = own_block * rows + jnp.arange(rows, dtype=jnp.int32)
    order = jnp.arange(item_count, dtype=jnp.int32)
    ends = jnp.sum(jnp.where(order[None, :] <= order[:, None], lengths[None, :], 0), axis=1)
    item = jnp.sum((places[:, None] >= ends[None, :]).astype(jnp.int32), axis=1)
    key_places = own_block * rows + jnp.arange(-2 * rows, 3 * rows, dtype=jnp.int32)
    key_item = jnp.sum((key_places[:, None] >= ends[None, :]).astype(jnp.int32), axis=1)
    key_item = jnp.where((key_places >= 0) & (key_places < frames_group), key_item, -1)
    items = (item, key_item)
    window_hot = (key_item[:, None] == jnp.arange(item_count, dtype=jnp.int32)[None, :]).astype(
        jnp.float32
    )
    inner = slice(2 * rows, 3 * rows)
    onehot = window_hot[inner]
    lengths_f = lengths[:, None].astype(jnp.float32)
    alpha_bar = plan(timesteps)
    mixing = exact(window_hot, jnp.stack([jnp.sqrt(alpha_bar), jnp.sqrt(1.0 - alpha_bar)], axis=1))
    near = frame_window(frames, gathered_frames, own_block, close).T
    noise = near[inner, channels:]
    noisy_low = (mixing[:, 0:1] * near[:, :channels] + mixing[:, 1:2] * near[:, channels:]).astype(
        jnp.bfloat16
    )
    features = time_features(timesteps)

    text = jnp.where(null_flags[:, None] == 1, null_f[None, :], captions)
    before_silu = exact(features, w_time_f) + exact(text, w_text_f)
    condition, pull_silu = jax.vjp(jax.nn.silu, before_silu)
    hidden_window = dense(noisy_low, w_in) + exact(window_hot, condition)
    saved_all = []
    entering = []
    for depth in range(L):
        weights = gathered[depth]
        proj_qkv = weights[0]
        if depth == 0:
            normed_window = norm_rows(hidden_window, gains_f[0]).astype(jnp.bfloat16)
            hidden, normed = hidden_window[inner], normed_window[inner]
            queries = dense(normed, proj_qkv[:, :D]).astype(jnp.bfloat16)
            window = dense(normed_window, proj_qkv[:, D:]).astype(jnp.bfloat16)
        else:
            normed = norm_rows(hidden, gains_f[2 * depth]).astype(jnp.bfloat16)
            window = gather_window(dense(normed, proj_qkv[:, D:]).astype(jnp.bfloat16), close)
            queries = dense(normed, proj_qkv[:, :D]).astype(jnp.bfloat16)
        entering.append(hidden)
        hidden, saved = layer_forward(
            hidden, normed, queries, window, weights, gains_f[2 * depth + 1], items
        )
        saved_all.append(saved)
    final = norm_rows(hidden, gains_f[2 * L])
    final_low = final.astype(jnp.bfloat16)
    predicted = dense(final_low, w_out)
    error = predicted - noise
    part_pool = contract_rows(onehot, final, HIGH)
    squared_sum, pool_sum = sum_over_seq((jnp.sum(error * error), part_pool), 1)
    pooled = pool_sum / lengths_f
    audio_side = exact(pooled, w_audio_f)
    text_side = exact(captions, w_caption_f)
    clash, pull_clash = jax.vjp(contrast, audio_side, text_side)
    loss = squared_sum / (frames_group * channels) + contrast_weight * clash
    grad_audio_side, grad_text_side = pull_clash(jnp.float32(contrast_weight))
    grad_pred = (2.0 / (frames_group * channels) * error).astype(jnp.bfloat16)
    grad_w_out = contract_rows(grad_pred, final_low)
    grad_pooled = against_rows(grad_audio_side, w_audio_f, HIGH) / lengths_f
    grad_final = against_rows(grad_pred, w_out) + exact(onehot, grad_pooled)
    unused, pull_final = jax.vjp(norm_rows, hidden, gains_f[2 * L])
    grad_hidden, grad_gain_final = pull_final(grad_final)
    layer_grads = [None] * L
    own_grads = [None] * L
    twin_grads = [None] * L
    gain_grads = [None] * (2 * L + 1)
    gain_grads[2 * L] = grad_gain_final
    for depth in reversed(range(L)):
        weights = gathered[depth]
        proj_qkv = weights[0]
        grad_middle, grad_query, grad_pairs, operand_pairs, gain_grads[2 * depth + 1] = layer_backward(
            grad_hidden, weights, gains_f[2 * depth + 1], items, saved_all[depth]
        )
        normed = saved_all[depth][0]
        if depth == 0:
            qkv_parts = [(normed, grad_query), (normed_window, grad_pairs)]
            grad_normed = against_rows(grad_pairs, proj_qkv[:, D:])
            grad_own = grad_normed[inner] + against_rows(grad_query, proj_qkv[:, :D])
            grad_normed = jnp.concatenate(
                [grad_normed[: 2 * rows], grad_own, grad_normed[3 * rows :]], axis=0
            )
            unused, pull_one = jax.vjp(norm_rows, hidden_window, gains_f[0])
        else:
            grad_pairs = return_window(grad_pairs, rows, close).astype(jnp.bfloat16)
            grad_projected = jnp.concatenate([grad_query, grad_pairs], axis=1)
            qkv_parts = [(normed, grad_projected)]
            grad_normed = against_rows(grad_projected, proj_qkv)
            unused, pull_one = jax.vjp(norm_rows, entering[depth], gains_f[2 * depth])
        grad_input, gain_grads[2 * depth] = pull_one(grad_normed)
        layer_grads[depth] = layer_gradients(qkv_parts, operand_pairs)
        if depth > 0:
            grad_hidden = grad_middle + grad_input
            if close:
                grad_hidden, layer_grads[depth] = lax.optimization_barrier(
                    (grad_hidden, layer_grads[depth])
                )
        else:
            grad_hidden = jnp.concatenate(
                [grad_input[: 2 * rows], grad_input[inner] + grad_middle, grad_input[3 * rows :]], axis=0
            )
        if depth > 0 and close:
            own_grads[depth] = [
                lax.psum_scatter(grad, "seq", scatter_dimension=0, tiled=True)
                for grad in layer_grads[depth]
            ]
    grad_w_in = contract_rows(noisy_low.astype(jnp.float32), grad_hidden, HIGH)
    grad_condition = contract_rows(window_hot, grad_hidden, HIGH)
    grad_w_in, grad_w_out, grad_condition, gain_rows = sum_over_seq(
        (grad_w_in, grad_w_out, grad_condition, jnp.stack(gain_grads)), 2
    )
    grad_before = pull_silu(grad_condition)[0]
    grad_null = jnp.sum(
        jnp.where(null_flags[:, None] == 1, against_rows(grad_before, w_text_f, HIGH), 0.0), axis=0
    )
    straight = jnp.concatenate([grad_w_in, grad_w_out.T.reshape(channels, D), gain_rows, grad_null[None]])
    lead = 2 * channels
    identity = jnp.eye(straight.shape[0], dtype=jnp.float32)
    features_at, text_at = lead, lead + D
    audio_at = text_at + text_width
    caption_at = audio_at + D * E // D
    gains_at = caption_at + text_width * E // D
    view_rows = gains_at + gain_rows.shape[0] + 1

    def placed_left(value, start):
        return jnp.pad(value, ((0, 0), (start, view_rows - start - value.shape[1])))

    left = jnp.concatenate(
        [
            placed_left(identity[:, :lead], 0) + placed_left(identity[:, lead:], gains_at),
            placed_left(features, features_at),
            placed_left(text, text_at),
            placed_left(thirds_left(pooled), audio_at),
            placed_left(thirds_left(captions), caption_at),
        ],
        axis=0,
    )
    right = jnp.concatenate(
        [
            straight,
            grad_before,
            grad_before,
            thirds_right(grad_audio_side),
            thirds_right(grad_text_side),
        ],
        axis=0,
    )
    own_rows_count = -(-other_size // D) + 1
    left = jnp.pad(left, ((0, 0), (0, own_rows_count)))
    own_start = rank * other_size
    own_left = lax.dynamic_slice_in_dim(left, own_start // D, own_rows_count, axis=1)
    own_view = contract_rows(own_left, right, HIGH)
    other_grad = lax.dynamic_slice_in_dim(own_view.reshape(-1), own_start % D, other_size)
    other_grad_square = jnp.sum(other_grad * other_grad)
    if close:
        other_grad_low = other_grad.astype(jnp.bfloat16)
        twin_other = swapped(other_grad_low).astype(jnp.float32)
        own_grads[0], twin_grads[0], square_part = scatter_layer(*layer_grads[0], 5)
        square_part = square_part + other_grad_square
        for depth in range(1, L):
            twin_grads[depth] = [swapped(grad) for grad in own_grads[depth]]
            for grad in own_grads[depth]:
                wide = grad.astype(jnp.float32)
                square_part = square_part + jnp.sum(wide * wide)
        norms = jnp.sqrt(sums_by_group(square_part, 3))
        total_norm = lax.dynamic_index_in_dim(norms, group, keepdims=False)
        twin_norm = lax.dynamic_index_in_dim(norms, 1 - group, keepdims=False)
        factor = jnp.minimum(1.0, clip_at / (total_norm + 1e-06))
        twin_factor = jnp.minimum(1.0, clip_at / (twin_norm + 1e-06))
        views = [flat_view(anchor_layers), first_view, second_view, flat_view(outer_layers)]
        stepped = step_layers(
            jnp.stack([factor, twin_factor]),
            [part for grads in own_grads for part in grads],
            [part for grads in twin_grads for part in grads],
            views + twin_views,
            seq_count,
        )
        new_layers, first_l, second_l, mean_layers, momentum_layers = map(from_view, stepped)
        first_o, second_o, _ = adam(other_grad * factor, first_other[0], second_other[0], anchor_other)

        def low(value):
            return lax.reduce_precision(value, 8, 7)

        delta_o = delta_of(low(other_grad) * factor, low(first_other[0]), low(second_other[0]), anchor_other)
        delta_twin = delta_of(twin_other * twin_factor, *twin_moments, anchor_other)
        mean_other = (delta_o + delta_twin) / 2
    else:
        stacked = jnp.stack(
            [
                flatten(
                    lax.psum_scatter(grad, "seq", scatter_dimension=0, tiled=True).astype(jnp.float32)
                    for grad in grads
                )
                for grads in layer_grads
            ]
        )
        total_norm = jnp.sqrt(lax.psum(jnp.sum(stacked * stacked) + other_grad_square, "seq"))
        factor = jnp.minimum(1.0, clip_at / (total_norm + 1e-06))
        first_l, second_l, delta_l = adam(
            stacked * factor, first_layers[0], second_layers[0], anchor_layers
        )
        first_o, second_o, delta_o = adam(
            other_grad * factor, first_other[0], second_other[0], anchor_other
        )
        mean_layers = group_mean(delta_l, group_count)
        mean_other = group_mean(delta_o, group_count)
        momentum_layers = outer_mu * outer_layers + mean_layers
        new_layers = anchor_layers - outer_rate * (mean_layers + outer_mu * momentum_layers)
    momentum_other = outer_mu * outer_other + mean_other
    new_other = anchor_other - outer_rate * (mean_other + outer_mu * momentum_other)
    return (
        new_layers,
        new_other,
        first_l[None],
        first_o[None],
        second_l[None],
        second_o[None],
        mean_layers,
        mean_other,
        momentum_layers,
        momentum_other,
        loss.reshape(1),
        total_norm.reshape(1),
    )


def solution(mesh):
    placed = (
        P(None, "seq"),
        P("seq"),
        P("grp", None, "seq"),
        P("grp", "seq"),
        P("grp", None, "seq"),
        P("grp", "seq"),
        P(None, "seq"),
        P("seq"),
        P(("grp", "seq"), None),
        P(("grp", "seq"), None),
        P("grp", None),
        P("grp", None),
        P("grp", None),
        P("grp", None, None),
    )
    return jax.shard_map(
        per_device,
        mesh=mesh,
        in_specs=placed,
        out_specs=(
            P(None, "seq"),
            P("seq"),
            P("grp", None, "seq"),
            P("grp", "seq"),
            P("grp", None, "seq"),
            P("grp", "seq"),
            P(None, "seq"),
            P("seq"),
            P(None, "seq"),
            P("seq"),
            P("grp"),
            P("grp"),
        ),
        check_vma=False,
    )
```

```python
import functools
import math

import jax
import jax.numpy as jnp
from jax import lax
from jax.experimental import pallas as pl
from jax.experimental.pallas import tpu as pltpu
from jax.sharding import PartitionSpec as P

D = 768
HEADS = 12
HD = 64
FF = 3072
E = 512
L = 2
TSTEPS = 1000
STEP_COUNT = 10


HIGH = lax.Precision.HIGHEST
beta_one = 0.9
beta_two = 0.95
adam_eps = 1e-08
decay_rate = 0.01
inner_rate = 0.02
outer_rate = 0.7
outer_mu = 0.9
clip_at = 0.01
logit_scale = 30.0
contrast_weight = 0.05


def block_of(rank, close):
    if not close:
        return rank
    turn = (rank // 4) % 2
    return rank + 2 * turn * (1 - 2 * ((rank // 2) % 2))


def passed_along(value, axis, steps, close):
    count = lax.axis_size(axis)
    holder = {block_of(rank, close): rank for rank in range(count)}
    initial, last = (max(0, -steps), min(count, count - steps))
    return lax.ppermute(
        value, axis, [(holder[source], holder[source + steps]) for source in range(initial, last)]
    )


def dense(left, right):
    return jnp.dot(left, right, preferred_element_type=jnp.float32)


def exact(left, right):
    return jnp.dot(left, right, precision=HIGH, preferred_element_type=jnp.float32)


def contract_rows(left, right, precision=None):
    return lax.dot_general(
        left,
        right,
        (((0,), (0,)), ((), ())),
        precision=precision,
        preferred_element_type=jnp.float32,
    )


def against_rows(left, right, precision=None):
    return lax.dot_general(
        left,
        right,
        (((1,), (1,)), ((), ())),
        precision=precision,
        preferred_element_type=jnp.float32,
    )


def carve(flat, shapes):
    pieces = []
    start = 0
    for shape in shapes:
        count = math.prod(shape)
        pieces.append(flat[start : start + count].reshape(shape))
        start += count
    return pieces


def layer_rows(piece, shards):
    cut = D // shards * (4 * D + FF)
    return piece[:cut].reshape(D // shards, 4 * D + FF), piece[cut:].reshape(FF // shards, D)


def split_upper(upper, lower):
    return [upper[:, : 3 * D], upper[:, 3 * D : 4 * D], upper[:, 4 * D :], lower]


def other_shapes(channels, width, text_width, joint_width, blocks):
    return [
        (channels, width),
        (width, channels),
        (width, width),
        (text_width, width),
        (width, joint_width),
        (text_width, joint_width),
        (2 * blocks + 1, width),
        (text_width,),
    ]


def norm_rows(hidden, gain):
    centred = hidden - jnp.mean(hidden, axis=-1, keepdims=True)
    return centred * lax.rsqrt(jnp.mean(centred * centred, axis=-1, keepdims=True) + 1e-05) * gain


def plan(steps):
    angle = (steps.astype(jnp.float32) / TSTEPS + 0.008) / 1.008 * (math.pi / 2)
    return jnp.cos(angle) ** 2


def time_features(steps):
    half = D // 2
    frequency = jnp.exp(-math.log(10000.0) * jnp.arange(half, dtype=jnp.float32) / half)
    angle = steps.astype(jnp.float32)[:, None] * frequency[None, :]
    return jnp.concatenate([jnp.cos(angle), jnp.sin(angle)], axis=1)


def contrast(audio_side, text_side):
    audio_unit = audio_side * lax.rsqrt(
        jnp.sum(audio_side * audio_side, axis=-1, keepdims=True) + 1e-06
    )
    text_unit = text_side * lax.rsqrt(
        jnp.sum(text_side * text_side, axis=-1, keepdims=True) + 1e-06
    )
    logits = logit_scale * jnp.dot(audio_unit, text_unit.T, precision=HIGH)
    diagonal = logit_scale * jnp.sum(audio_unit * text_unit, axis=-1)
    row_terms = jax.nn.logsumexp(logits, axis=1) - diagonal
    column_terms = jax.nn.logsumexp(logits, axis=0) - diagonal
    return 0.5 * (jnp.mean(row_terms) + jnp.mean(column_terms))


def gather_window(local_pairs, close):
    pieces = {}
    for step in (2, 1, -1, -2):
        pieces[step] = passed_along(local_pairs, "seq", step, close)
    return jnp.concatenate([pieces[2], pieces[1], local_pairs, pieces[-1], pieces[-2]], axis=0)


def return_window(grad_window, rows, close):
    total = grad_window[2 * rows : 3 * rows].astype(jnp.float32)
    for slot, step in ((0, 2), (1, 1), (3, -1), (4, -2)):
        total = total + passed_along(
            grad_window[slot * rows : (slot + 1) * rows], "seq", -step, close
        ).astype(jnp.float32)
    return total


LANES = 128
LOG2E = math.log2(math.e)
PAIRS = HEADS * HD // LANES
VMEM_LIMIT = 50 * 1024 * 1024


def lane_masks(dtype):
    lane = lax.broadcasted_iota(jnp.int32, (1, LANES), 1)
    return [(lane < HD).astype(dtype), (lane >= HD).astype(dtype)]


def fill_bias(bias_ref, query_item_ref, key_item_ref):
    keep = key_item_ref[...] == query_item_ref[...]
    bias_ref[...] = jnp.where(keep, 0.0, -1e30).astype(jnp.float32)


def attend_forward_kernel(q_ref, kv_ref, query_item_ref, key_item_ref, o_ref, lse_ref, bias_ref):
    fill_bias(bias_ref, query_item_ref, key_item_ref)
    width = HEADS * HD
    masks = lane_masks(jnp.bfloat16)
    lse_ref[...] = jnp.zeros_like(lse_ref)
    for pair in range(PAIRS):
        cols = slice(pair * LANES, (pair + 1) * LANES)
        query = q_ref[:, cols] * jnp.bfloat16(HD ** (-0.5))
        key_rows = kv_ref[:, cols]
        value_rows = kv_ref[:, width + pair * LANES : width + (pair + 1) * LANES]
        halves = []
        for half in range(2):
            scores = against_rows(key_rows, query * masks[half]) * LOG2E + bias_ref[...]
            peak = jnp.max(scores, axis=0, keepdims=True)
            weights = jnp.exp2(scores - peak)
            total = jnp.sum(weights, axis=0, keepdims=True)
            mixed = contract_rows(value_rows, weights.astype(jnp.bfloat16)) * (1.0 / total)
            halves.append(mixed[half * HD : (half + 1) * HD])
            lse_ref[2 * pair + half : 2 * pair + half + 1, :] = peak + jnp.log2(total)
        o_ref[:, cols] = jnp.concatenate(halves, axis=0).T.astype(o_ref.dtype)


def attend_forward(queries, window, query_item, key_item):
    rows, width = queries.shape
    span = window.shape[0]
    return pl.pallas_call(
        attend_forward_kernel,
        out_shape=(
            jax.ShapeDtypeStruct((rows, width), jnp.bfloat16),
            jax.ShapeDtypeStruct((16, rows), jnp.float32),
        ),
        in_specs=[pl.BlockSpec(memory_space=pltpu.VMEM)] * 4,
        out_specs=(pl.BlockSpec(memory_space=pltpu.VMEM),) * 2,
        scratch_shapes=[pltpu.VMEM((span, rows), jnp.float32)],
        compiler_params=pltpu.CompilerParams(vmem_limit_bytes=VMEM_LIMIT),
        cost_estimate=pl.CostEstimate(
            flops=4 * rows * span * width,
            transcendentals=rows * span * HEADS,
            bytes_accessed=4 * rows * width + 4 * span * width,
        ),
        name="attend_forward",
    )(queries, window, query_item[None, :], key_item[:, None])


def attend_backward_kernel(
    q_ref, kv_ref, do_ref, lse_ref, query_item_ref, key_item_ref, dq_ref, dkv_ref, bias_ref
):
    fill_bias(bias_ref, query_item_ref, key_item_ref)
    width = HEADS * HD
    masks = lane_masks(jnp.bfloat16)
    for pair in range(PAIRS):
        cols = slice(pair * LANES, (pair + 1) * LANES)
        value_cols = slice(width + pair * LANES, width + (pair + 1) * LANES)
        query = q_ref[:, cols] * jnp.bfloat16(HD ** (-0.5))
        key_rows = kv_ref[:, cols]
        value_rows = kv_ref[:, value_cols]
        grad_out = do_ref[:, cols]
        halves = []
        grad_key = grad_value = None
        for half in range(2):
            query_half = query * masks[half]
            grad_half = grad_out * masks[half]
            scores = against_rows(key_rows, query_half) * LOG2E + bias_ref[...]
            shares = jnp.exp2(scores - lse_ref[2 * pair + half : 2 * pair + half + 1, :])
            grad_shares = against_rows(value_rows, grad_half)
            inner = jnp.sum(grad_shares * shares, axis=0, keepdims=True)
            grad_scores = (shares * (grad_shares - inner)).astype(jnp.bfloat16)
            one_value = dense(shares.astype(jnp.bfloat16), grad_half)
            one_key = dense(grad_scores, query_half)
            grad_value = one_value if grad_value is None else grad_value + one_value
            grad_key = one_key if grad_key is None else grad_key + one_key
            one_query = contract_rows(key_rows, grad_scores)
            halves.append(one_query[half * HD : (half + 1) * HD])
        grad_query = jnp.concatenate(halves, axis=0).T * HD ** (-0.5)
        dq_ref[:, cols] = grad_query.astype(dq_ref.dtype)
        dkv_ref[:, cols] = grad_key.astype(dkv_ref.dtype)
        dkv_ref[:, value_cols] = grad_value.astype(dkv_ref.dtype)


def attend_backward(queries, window, grad_out, lse, query_item, key_item):
    rows, width = queries.shape
    span = window.shape[0]
    return pl.pallas_call(
        attend_backward_kernel,
        out_shape=(
            jax.ShapeDtypeStruct((rows, width), jnp.bfloat16),
            jax.ShapeDtypeStruct((span, 2 * width), jnp.bfloat16),
        ),
        in_specs=[pl.BlockSpec(memory_space=pltpu.VMEM)] * 6,
        out_specs=(pl.BlockSpec(memory_space=pltpu.VMEM),) * 2,
        scratch_shapes=[pltpu.VMEM((span, rows), jnp.float32)],
        compiler_params=pltpu.CompilerParams(vmem_limit_bytes=VMEM_LIMIT),
        cost_estimate=pl.CostEstimate(
            flops=10 * rows * span * width,
            transcendentals=rows * span * HEADS,
            bytes_accessed=8 * rows * width + 8 * span * width,
        ),
        name="attend_backward",
    )(queries, window, grad_out, lse, query_item[None, :], key_item[:, None])


def layer_forward(hidden, normed, queries, window, weights, gain_two, items):
    proj_qkv, proj_out, proj_up, proj_down = weights
    attended, lse = attend_forward(queries, window, *items)
    middle = hidden + dense(attended, proj_out)
    second = norm_rows(middle, gain_two).astype(jnp.bfloat16)
    upper = dense(second, proj_up)
    activated = jax.nn.gelu(upper, approximate=True).astype(jnp.bfloat16)
    return (
        middle + dense(activated, proj_down),
        (normed, queries, window, lse, attended, middle, second, upper, activated),
    )


def layer_backward(grad_hidden, weights, gain_two, items, saved, early):
    normed, queries, window, lse, attended, middle, second, upper, activated = saved
    proj_qkv, proj_out, proj_up, proj_down = weights
    branch_top = grad_hidden.astype(jnp.bfloat16)
    grad_activated = against_rows(branch_top, proj_down)
    unused, pull_gelu = jax.vjp(lambda value: jax.nn.gelu(value, approximate=True), upper)
    grad_upper = pull_gelu(grad_activated)[0].astype(jnp.bfloat16)
    grad_second = against_rows(grad_upper, proj_up)
    unused, pull_two = jax.vjp(norm_rows, middle, gain_two)
    grad_middle, grad_gain_two = pull_two(grad_second)
    grad_middle = grad_middle + grad_hidden
    branch_mid = grad_middle.astype(jnp.bfloat16)
    grad_attended = against_rows(branch_mid, proj_out).astype(jnp.bfloat16)
    lower_full = contract_rows(activated, branch_top).astype(jnp.bfloat16)
    pairs = [(attended, branch_mid), (second, grad_upper)]
    if early:
        grad_attended, rest_full = lax.optimization_barrier((grad_attended, side_by_side(pairs)))
    grad_query, grad_window = attend_backward(queries, window, grad_attended, lse, *items)
    return grad_middle, grad_query, grad_window, (rest_full if early else pairs), lower_full, grad_gain_two


def side_by_side(pairs):
    return jnp.concatenate(
        [contract_rows(left, right).astype(jnp.bfloat16) for left, right in pairs], axis=1
    )


def frame_window(frames, gathered_frames, own_block, close):
    if close:
        count = gathered_frames.shape[0]
        parts = [
            lax.dynamic_index_in_dim(
                gathered_frames, jnp.clip(own_block + step, 0, count - 1), keepdims=False
            )
            for step in range(-2, 3)
        ]
    else:
        parts = [passed_along(frames, "seq", -step, close) for step in range(-2, 0)] + [frames]
        parts += [passed_along(frames, "seq", -step, close) for step in range(1, 3)]
    return jnp.concatenate(parts, axis=1)


def thirds(value, right, at):
    joint = right.shape[1]
    half = joint // 2
    inside = (at >= 0) & (at < value.shape[1] * joint // D)
    matrix_row, odd = at // 2 * 3, at % 2
    wanted = jnp.stack(
        [
            jnp.where(inside & (odd == parity), matrix_row + offset, -1)
            for parity, offset in ((0, 0), (0, 1), (1, 1), (1, 2))
        ]
    )
    width = jnp.arange(value.shape[1], dtype=jnp.int32)
    choice = (width[:, None, None] == wanted[None]).astype(jnp.float32)
    left = jnp.einsum("iw,wkv->kiv", value, choice, precision=HIGH)
    rights = jnp.stack(
        [
            jnp.pad(right, ((0, 0), (0, half))),
            jnp.pad(right[:, :half], ((0, 0), (joint, 0))),
            jnp.pad(right[:, half:], ((0, 0), (0, joint))),
            jnp.pad(right, ((0, 0), (half, 0))),
        ]
    )
    return jnp.einsum("kiv,kid->vd", left, rights, precision=HIGH)


def adam(grad, first, second, anchor):
    first = beta_one * first + (1.0 - beta_one) * grad
    second = beta_two * second + (1.0 - beta_two) * grad * grad
    stepped = first * (1.0 / (1.0 - beta_one**STEP_COUNT))
    scaled = second * (1.0 / (1.0 - beta_two**STEP_COUNT))
    delta = inner_rate * (stepped / (jnp.sqrt(scaled) + adam_eps) + decay_rate * anchor)
    return (first, second, delta)


MESH = pl.DeviceIdType.MESH
SUBLANES = 8
CLOSE_RANKS = 16


def greet_seq(me, count):
    group = lax.axis_index("grp")
    barrier = pltpu.get_barrier_semaphore()

    def one(step, carry):
        pl.semaphore_signal(
            barrier, inc=1, device_id=(group, lax.rem(me + step, count)), device_id_type=MESH
        )
        return carry

    lax.fori_loop(1, count, one, 0)
    pl.semaphore_wait(barrier, count - 1)


def sum_kernel(count, x_ref, out_ref, parts, own, totals, send_one, recv_one, send_two, recv_two):
    me = lax.axis_index("seq")
    group = lax.axis_index("grp")
    greet_seq(me, count)

    def slice_copy(step):
        peer = lax.rem(me + step, count)
        return pltpu.make_async_remote_copy(
            src_ref=x_ref.at[peer],
            dst_ref=parts.at[step],
            send_sem=send_one.at[step],
            recv_sem=recv_one.at[step],
            device_id=(group, peer),
            device_id_type=MESH,
        )

    def total_copy(step):
        peer = lax.rem(me + step, count)
        return pltpu.make_async_remote_copy(
            src_ref=own,
            dst_ref=totals.at[step],
            send_sem=send_two.at[step],
            recv_sem=recv_two.at[step],
            device_id=(group, peer),
            device_id_type=MESH,
        )

    def start_of(make):
        def one(step, carry):
            make(step).start()
            return carry

        return one

    lax.fori_loop(1, count, start_of(slice_copy), 0)
    own[...] = x_ref[me]

    def gather_in(step, carry):
        slice_copy(step).wait()
        own[...] += parts[step]
        return carry

    lax.fori_loop(1, count, gather_in, 0)
    lax.fori_loop(1, count, start_of(total_copy), 0)
    out_ref[me] = own[...]

    def spread(step, carry):
        total_copy(step).wait()
        out_ref[lax.rem(me + count - step, count)] = totals[step]
        return carry

    lax.fori_loop(1, count, spread, 0)


def in_slices(values, count):
    size = sum(math.prod(value.shape) for value in values)
    block = -(-size // (count * SUBLANES * LANES)) * SUBLANES
    flat = jnp.concatenate([value.reshape(-1) for value in values])
    return jnp.pad(flat, (0, count * block * LANES - size)).reshape(count, block, LANES)


def sum_over_seq(values, collective):
    count = lax.axis_size("seq")
    if count != CLOSE_RANKS:
        return lax.psum(values, "seq")
    small = in_slices(values, count)
    shape = small.shape
    total = pl.pallas_call(
        functools.partial(sum_kernel, count),
        out_shape=jax.ShapeDtypeStruct(shape, jnp.float32),
        in_specs=[pl.BlockSpec(memory_space=pltpu.VMEM)],
        out_specs=pl.BlockSpec(memory_space=pltpu.VMEM),
        scratch_shapes=[
            pltpu.VMEM(shape, jnp.float32),
            pltpu.VMEM(shape[1:], jnp.float32),
            pltpu.VMEM(shape, jnp.float32),
        ]
        + [pltpu.SemaphoreType.DMA((count,))] * 4,
        compiler_params=pltpu.CompilerParams(collective_id=collective, has_side_effects=True),
        cost_estimate=pl.CostEstimate(
            flops=math.prod(shape), transcendentals=0, bytes_accessed=16 * math.prod(shape)
        ),
        name="sum_over_seq",
    )(small)
    return carve(total.reshape(-1), [value.shape for value in values])


def share_kernel(count, x_ref, out_ref, parts, send_sem, recv_sem):
    seq = lax.axis_size("seq")
    me = lax.axis_index("grp") * seq + lax.axis_index("seq")

    def place(step):
        peer = lax.rem(me + step, count)
        return peer // seq, lax.rem(peer, seq)

    barrier = pltpu.get_barrier_semaphore()

    def greet(step, carry):
        pl.semaphore_signal(barrier, inc=1, device_id=place(step), device_id_type=MESH)
        return carry

    lax.fori_loop(1, count, greet, 0)
    pl.semaphore_wait(barrier, count - 1)

    def copy_of(step):
        return pltpu.make_async_remote_copy(
            src_ref=x_ref,
            dst_ref=parts.at[step],
            send_sem=send_sem.at[step],
            recv_sem=recv_sem.at[step],
            device_id=place(step),
            device_id_type=MESH,
        )

    def start(step, carry):
        copy_of(step).start()
        return carry

    lax.fori_loop(1, count, start, 0)
    out_ref[me] = x_ref[...]

    def finish(step, carry):
        copy_of(step).wait()
        out_ref[lax.rem(me + count - step, count)] = parts[step]
        return carry

    lax.fori_loop(1, count, finish, 0)


def sums_by_group(value, collective):
    groups, count = lax.axis_size("grp"), lax.axis_size("seq")
    shape = (groups * count, SUBLANES, LANES)
    shared = pl.pallas_call(
        functools.partial(share_kernel, groups * count),
        out_shape=jax.ShapeDtypeStruct(shape, jnp.float32),
        in_specs=[pl.BlockSpec(memory_space=pltpu.VMEM)],
        out_specs=pl.BlockSpec(memory_space=pltpu.VMEM),
        scratch_shapes=[pltpu.VMEM(shape, jnp.float32)]
        + [pltpu.SemaphoreType.DMA((groups * count,))] * 2,
        compiler_params=pltpu.CompilerParams(collective_id=collective, has_side_effects=True),
        name="share_over_all",
    )(jnp.full(shape[1:], value, jnp.float32))
    return jnp.sum(shared[:, 0, 0].reshape(groups, count), axis=1)


GRID = (4, 2, 2)
GATHER_Y_LAG = 2
GATHER_X_LAG = 5
GATHER_AHEAD = 1


def place_of(me):
    return me // 4, lax.rem(me // 2, 2), lax.rem(me, 2)


def rank_of(along, across, core):
    return (along * 2 + across) * 2 + core


def gather_kernel(shared, *refs):
    pieces = len(shared)
    own_refs, out_refs = refs[:pieces], refs[pieces : 2 * pieces]
    local_sem, z_send, z_recv, y_send, y_recv, x_send, x_recv, c_send, c_recv = refs[2 * pieces :]
    group, me = lax.axis_index("grp"), lax.axis_index("seq")
    z, y, core = place_of(me)
    z_size = GRID[0]
    across, sibling, twin = (
        (group, rank_of(z, 1 - y, core)),
        (group, rank_of(z, y, 1 - core)),
        (1 - group, me),
    )
    barrier = pltpu.get_barrier_semaphore()
    for there in (across, sibling, twin):
        pl.semaphore_signal(barrier, inc=1, device_id=there, device_id_type=MESH)

    @pl.when(z > 0)
    def _():
        pl.semaphore_signal(
            barrier, inc=1, device_id=(group, rank_of(z - 1, y, core)), device_id_type=MESH
        )

    @pl.when(z < z_size - 1)
    def _():
        pl.semaphore_signal(
            barrier, inc=1, device_id=(group, rank_of(z + 1, y, core)), device_id_type=MESH
        )

    neighbours = (z > 0).astype(jnp.int32) + (z < z_size - 1).astype(jnp.int32)
    pl.semaphore_wait(barrier, 3 + neighbours)

    def half_of(ref, piece, half):
        if half is None:
            return ref
        if ref.shape[-1] == LANES:
            span = ref.shape[-2] // 2
            return ref.at[pl.ds(pl.multiple_of(half * span, ROW_GROUP), span), :]
        span = ref.shape[-1] // 2
        return ref.at[:, pl.ds(pl.multiple_of(half * span, LANES), span)]

    def move(piece, half, there, along, over, send, recv, own=False):
        dst = half_of(out_refs[piece].at[rank_of(along, over, core)], piece, half)
        src = half_of(own_refs[piece], piece, half) if own else dst
        return pltpu.make_async_remote_copy(
            src_ref=src, dst_ref=dst, send_sem=send, recv_sem=recv, device_id=there, device_id_type=MESH
        )

    def z_move(piece, along, forward, own=False):
        there = (group, rank_of(z + (1 if forward else -1), y, core))
        half = group if shared[piece] else None
        return move(
            piece, half, there, along, y, z_send.at[piece, along, int(forward)], z_recv.at[piece, along], own
        )

    def y_move(piece, along, own=False, over=None):
        half = group if shared[piece] else None
        over = y if over is None else over
        return move(piece, half, across, along, over, y_send.at[piece, along], y_recv.at[piece, along], own)

    def x_move(piece, along, over, arriving=False):
        half = 1 - group if arriving else group
        slot = along * 2 + over
        return move(piece, half, twin, along, over, x_send.at[piece, slot], x_recv.at[piece, slot])

    def c_move(piece, along, over, half, slot, own=False):
        return move(
            piece,
            half,
            sibling,
            along,
            over,
            c_send.at[piece, along * 2 + over, slot],
            c_recv.at[piece, along * 2 + over, slot],
            own,
        )

    def each_along(distance, action):
        if distance == 0:
            action(z, True, True)
            return

        @pl.when(z - distance >= 0)
        def _():
            action(z - distance, True, False)

        @pl.when(z + distance < z_size)
        def _():
            action(z + distance, False, True)

    def own_sends(piece):
        pltpu.make_async_copy(own_refs[piece], out_refs[piece].at[me], local_sem.at[piece]).start()

        @pl.when(z + 1 < z_size)
        def _():
            z_move(piece, z, True, own=True).start()

        @pl.when(z > 0)
        def _():
            z_move(piece, z, False, own=True).start()

        y_move(piece, z, own=True).start()
        c_move(piece, z, y, None, 0, own=True).start()

    def z_arrivals(piece, distance):
        if distance == 0:
            return

        def one(along, onward, backward):
            z_move(piece, along, onward).wait_recv()

            @pl.when((z + 1 < z_size) if onward else (z > 0))
            def _():
                z_move(piece, along, onward).start()

            y_move(piece, along).start()
            if shared[piece]:
                x_move(piece, along, y).start()
            c_move(piece, along, y, group if shared[piece] else None, 0).start()

        each_along(distance, one)

    def y_arrivals(piece, distance):
        def one(along, *_):
            y_move(piece, along, over=1 - y).wait_recv()
            if shared[piece]:
                x_move(piece, along, 1 - y).start()
            c_move(piece, along, 1 - y, group if shared[piece] else None, 0).start()

        each_along(distance, one)

    def x_arrivals(piece, distance):
        if not shared[piece]:
            return

        def one(along, *_):
            for turn in range(2):
                over = y if turn == 0 else 1 - y
                if distance == 0 and turn == 0:
                    continue
                x_move(piece, along, over, arriving=True).wait_recv()
                c_move(piece, along, over, 1 - group, 1).start()

        each_along(distance, one)

    def drain(piece, distance):
        def one(along, onward, backward):
            own = distance == 0
            half = group if shared[piece] else None
            for turn in range(2):
                over = y if turn == 0 else 1 - y
                mine = own and turn == 0
                whole = None if mine else half
                c_move(piece, along, over, whole, 0).wait()
                if shared[piece] and not mine:
                    c_move(piece, along, over, 1 - group, 1).wait()
                    x_move(piece, along, over).wait_send()
            y_move(piece, along).wait_send()
            if onward:

                @pl.when(z + 1 < z_size)
                def _():
                    z_move(piece, along, True).wait_send()

            if backward:

                @pl.when(z > 0)
                def _():
                    z_move(piece, along, False).wait_send()

        each_along(distance, one)
        if distance == 0:
            pltpu.make_async_copy(own_refs[piece], out_refs[piece].at[me], local_sem.at[piece]).wait()

    slots = [(piece, distance) for piece in range(pieces) for distance in range(z_size)]
    own_sends(0)
    for turn in range(len(slots) + GATHER_X_LAG):
        if turn < len(slots):
            piece, distance = slots[turn]
            if distance == GATHER_AHEAD and piece + 1 < pieces:
                own_sends(piece + 1)
            z_arrivals(piece, distance)
        if 0 <= turn - GATHER_Y_LAG < len(slots):
            y_arrivals(*slots[turn - GATHER_Y_LAG])
        if 0 <= turn - GATHER_X_LAG < len(slots):
            x_arrivals(*slots[turn - GATHER_X_LAG])
    for slot in slots:
        drain(*slot)


def gather_pieces(pieces, shared, collective):
    count = lax.axis_size("seq")
    if count != math.prod(GRID) or lax.axis_size("grp") != 2:
        return [lax.all_gather(piece, "seq", axis=0) for piece in pieces]
    amount = len(pieces)
    sems = [
        (amount,),
        (amount, 4, 2),
        (amount, 4),
        (amount, 4),
        (amount, 4),
        (amount, 8),
        (amount, 8),
        (amount, 8, 2),
        (amount, 8, 2),
    ]
    return pl.pallas_call(
        functools.partial(gather_kernel, tuple(shared)),
        out_shape=[jax.ShapeDtypeStruct((count,) + piece.shape, piece.dtype) for piece in pieces],
        in_specs=[pl.BlockSpec(memory_space=pl.ANY)] * amount,
        out_specs=[pl.BlockSpec(memory_space=pl.ANY)] * amount,
        scratch_shapes=[pltpu.SemaphoreType.DMA(shape) for shape in sems],
        compiler_params=pltpu.CompilerParams(collective_id=collective, has_side_effects=True),
        name="gather_pieces",
    )(*pieces)


ROW_GROUP = 16
UPPER_CUTS = 3
SCATTER_LAG = 2


def scatter_kernel(pieces, amount, carried, *refs):
    grads, passing = refs[:amount], refs[amount : amount + carried]
    small = refs[amount + carried]
    refs = refs[amount + carried + 1 :]
    outs, twins = refs[:amount], refs[amount : 2 * amount]
    passed = refs[2 * amount : 2 * amount + carried]
    squares, small_out = refs[2 * amount + carried : 2 * amount + carried + 2]
    rest = refs[2 * amount + carried + 2 :]
    count = len(pieces)
    ranks = lax.axis_size("seq")
    own, beside, facing, from_left, from_right, ready = (
        rest[k * count : (k + 1) * count] for k in range(6)
    )
    load_sem, c_send, c_recv, y_send, y_recv, z_send, z_recv, x_send, x_recv = rest[
        6 * count : 6 * count + 9
    ]
    pass_send, pass_recv, parts, own_sum, totals, send_one, recv_one, send_two, recv_two = rest[
        6 * count + 9 :
    ]
    group, me = lax.axis_index("grp"), lax.axis_index("seq")
    z, y, core = place_of(me)
    z_size = GRID[0]
    across, sibling = (group, rank_of(z, 1 - y, core)), (group, rank_of(z, y, 1 - core))
    twin = (1 - group, me)
    left, right = (group, rank_of(z - 1, y, core)), (group, rank_of(z + 1, y, core))
    has_left, has_right = z > 0, z < z_size - 1
    barrier = pltpu.get_barrier_semaphore()
    pl.semaphore_signal(barrier, inc=1, device_id=twin, device_id_type=MESH)

    def greet(step, carry):
        there = (group, lax.rem(me + step, ranks))
        pl.semaphore_signal(barrier, inc=1, device_id=there, device_id_type=MESH)
        return carry

    lax.fori_loop(1, ranks, greet, 0)
    pl.semaphore_wait(barrier, ranks)
    squares[...] = jnp.zeros_like(squares)

    def part(piece, along, over, owner):
        which, row, rows, column, columns = pieces[piece]
        return grads[which].at[rank_of(along, over, owner), pl.ds(row, rows), pl.ds(column, columns)]

    def load(piece, along, over):
        slot = along * 2 + over
        return pltpu.make_async_copy(
            part(piece, along, over, core), own[piece].at[slot], load_sem.at[piece, slot]
        )

    def remote(src, dst, send, recv, there):
        return pltpu.make_async_remote_copy(
            src_ref=src, dst_ref=dst, send_sem=send, recv_sem=recv, device_id=there, device_id_type=MESH
        )

    def c_move(piece, along, over):
        slot = along * 2 + over
        return remote(
            part(piece, along, over, 1 - core),
            beside[piece].at[slot],
            c_send.at[piece, slot],
            c_recv.at[piece, slot],
            sibling,
        )

    def y_move(piece, along):
        return remote(
            own[piece].at[along * 2 + 1 - y],
            facing[piece].at[along],
            y_send.at[piece, along],
            y_recv.at[piece, along],
            across,
        )

    def z_move(piece, along, forward):
        side = 0 if forward else 1
        return remote(
            facing[piece].at[along],
            (from_left if forward else from_right)[piece].at[along],
            z_send.at[piece, along],
            z_recv.at[piece, along, side],
            right if forward else left,
        )

    def x_move(piece):
        which, row, height, column, columns = pieces[piece]
        return remote(
            ready[piece],
            twins[which].at[pl.ds(row, height), pl.ds(column, columns)],
            x_send.at[piece],
            x_recv.at[piece],
            twin,
        )

    def pass_move(k):
        return remote(passing[k], passed[k], pass_send.at[k], pass_recv.at[k], twin)

    def slice_move(step):
        peer = lax.rem(me + step, ranks)
        return remote(
            small.at[peer], parts.at[step], send_one.at[step], recv_one.at[step], (group, peer)
        )

    def total_move(step):
        peer = lax.rem(me + step, ranks)
        return remote(own_sum, totals.at[step], send_two.at[step], recv_two.at[step], (group, peer))

    def small_begin():
        def one(step, carry):
            slice_move(step).start()
            return carry

        lax.fori_loop(1, ranks, one, 0)
        own_sum[...] = small[me]

    def small_middle():
        def gather_in(step, carry):
            slice_move(step).wait()
            own_sum[...] += parts[step]
            return carry

        lax.fori_loop(1, ranks, gather_in, 0)

        def one(step, carry):
            total_move(step).start()
            return carry

        lax.fori_loop(1, ranks, one, 0)
        small_out[me] = own_sum[...]

    def small_end():
        def spread(step, carry):
            total_move(step).wait()
            small_out[lax.rem(me + ranks - step, ranks)] = totals[step]
            return carry

        lax.fori_loop(1, ranks, spread, 0)

    def each_along(distance, action):
        if distance == 0:
            action(z, None)
            return

        @pl.when(z - distance >= 0)
        def _():
            action(z - distance, False)

        @pl.when(z + distance < z_size)
        def _():
            action(z + distance, True)

    def by_rows(piece, body):
        def one(step, carry):
            body(pl.ds(pl.multiple_of(step * ROW_GROUP, ROW_GROUP), ROW_GROUP))
            return carry

        lax.fori_loop(0, pieces[piece][2] // ROW_GROUP, one, 0)

    def wide(ref, slot, rows):
        return ref[slot, rows, :].astype(jnp.float32)

    def begin(piece):
        for distance in reversed(range(z_size)):

            def one(along, _):
                for over in range(2):
                    load(piece, along, over).start()
                    c_move(piece, along, over).start()

            each_along(distance, one)

    def c_stage(piece, distance):
        def one(along, _):
            for turn in range(2):
                over = 1 - y if turn == 0 else y
                slot = along * 2 + over
                load(piece, along, over).wait()
                c_move(piece, along, over).wait_recv()

                def add(rows):
                    total = wide(own[piece], slot, rows) + wide(beside[piece], slot, rows)
                    own[piece][slot, rows, :] = total.astype(jnp.bfloat16)

                by_rows(piece, add)
                if turn == 0:
                    y_move(piece, along).start()

        each_along(distance, one)

    def y_stage(piece, distance):
        which, row, height, column, columns = pieces[piece]

        def one(along, forward):
            y_move(piece, along).wait_recv()
            slot = along * 2 + y
            if forward is None:

                def add(rows):
                    total = wide(own[piece], slot, rows) + wide(facing[piece], along, rows)
                    there = pl.ds(pl.multiple_of(row + rows.start, ROW_GROUP), ROW_GROUP)
                    outs[which][there, pl.ds(column, columns)] = total

                by_rows(piece, add)
                for side, present, source in ((True, has_left, from_left), (False, has_right, from_right)):

                    @pl.when(present)
                    def _():
                        z_move(piece, along, side).wait_recv()

                        def more(rows):
                            there = pl.ds(pl.multiple_of(row + rows.start, ROW_GROUP), ROW_GROUP)
                            outs[which][there, pl.ds(column, columns)] += wide(source[piece], along, rows)

                        by_rows(piece, more)

                def finish(rows):
                    there = pl.ds(pl.multiple_of(row + rows.start, ROW_GROUP), ROW_GROUP)
                    total = outs[which][there, pl.ds(column, columns)]
                    ready[piece][rows, :] = total.astype(jnp.bfloat16)
                    square = total[:SUBLANES] * total[:SUBLANES] + total[SUBLANES:] * total[SUBLANES:]
                    for k in range(columns // LANES):
                        squares[...] += square[:, k * LANES : (k + 1) * LANES]

                by_rows(piece, finish)
                x_move(piece).start()
                return
            source, present = (from_left, has_left) if forward else (from_right, has_right)

            @pl.when(present)
            def _():
                z_move(piece, along, forward).wait_recv()

                def add(rows):
                    total = wide(own[piece], slot, rows) + wide(facing[piece], along, rows)
                    total = total + wide(source[piece], along, rows)
                    facing[piece][along, rows, :] = total.astype(jnp.bfloat16)

                by_rows(piece, add)

            @pl.when(jnp.logical_not(present))
            def _():
                def add(rows):
                    total = wide(own[piece], slot, rows) + wide(facing[piece], along, rows)
                    facing[piece][along, rows, :] = total.astype(jnp.bfloat16)

                by_rows(piece, add)

            z_move(piece, along, forward).start()

        each_along(distance, one)

    def drain(piece, distance):
        def one(along, forward):
            for over in range(2):
                c_move(piece, along, over).wait_send()
            y_move(piece, along).wait_send()
            if forward is not None:
                z_move(piece, along, forward).wait_send()

        each_along(distance, one)

    slots = [(piece, distance) for piece in range(count) for distance in reversed(range(z_size))]
    begin(0)
    small_begin()
    for piece in range(1, min(2, count)):
        begin(piece)
    for k in range(carried):
        pass_move(k).start()
    for turn in range(len(slots) + SCATTER_LAG):
        if turn < len(slots):
            c_stage(*slots[turn])
            if turn == z_size:
                small_middle()
            piece, distance = slots[turn]
            if distance == 0 and piece + 2 < count:
                begin(piece + 2)
        if turn >= SCATTER_LAG:
            y_stage(*slots[turn - SCATTER_LAG])
    for slot in slots:
        drain(*slot)
    for piece in range(count):
        x_move(piece).wait()
    for k in range(carried):
        pass_move(k).wait()
    small_end()


def scatter_grads(grads, cuts, passing, values, collective):
    count = math.prod(GRID)
    grads = [grad.reshape(count, grad.shape[0] // count, grad.shape[1]) for grad in grads]
    pieces = []
    for which, cut in enumerate(cuts):
        rows, columns = grads[which].shape[1:]
        pieces += [(which, 0, rows, k * (columns // cut), columns // cut) for k in range(cut)]
    amount = len(pieces)
    places = math.prod(GRID[:2])

    def room(slots):
        return [pltpu.VMEM((slots, piece[2], piece[4]), jnp.bfloat16) for piece in pieces]

    sems = [
        (amount, places),
        (amount, places),
        (amount, places),
        (amount, GRID[0]),
        (amount, GRID[0]),
        (amount, GRID[0]),
        (amount, GRID[0], 2),
        (amount,),
        (amount,),
    ]
    small = in_slices(values, count)
    slot = small.shape[1:]
    carried = len(passing)
    sems += [(carried,)] * 2
    kinds = len(grads)
    *arrays, squares, total = pl.pallas_call(
        functools.partial(scatter_kernel, tuple(pieces), kinds, carried),
        out_shape=[jax.ShapeDtypeStruct(grad.shape[1:], jnp.float32) for grad in grads]
        + [jax.ShapeDtypeStruct(grad.shape[1:], jnp.bfloat16) for grad in grads]
        + [jax.ShapeDtypeStruct(part.shape, part.dtype) for part in passing]
        + [jax.ShapeDtypeStruct((SUBLANES, LANES), jnp.float32)]
        + [jax.ShapeDtypeStruct(small.shape, jnp.float32)],
        in_specs=[pl.BlockSpec(memory_space=pl.ANY)] * (kinds + carried)
        + [pl.BlockSpec(memory_space=pltpu.VMEM)],
        out_specs=[pl.BlockSpec(memory_space=pltpu.VMEM)] * kinds
        + [pl.BlockSpec(memory_space=pl.ANY)] * (kinds + carried)
        + [pl.BlockSpec(memory_space=pltpu.VMEM)] * 2,
        scratch_shapes=room(places)
        + room(places)
        + room(GRID[0])
        + room(GRID[0])
        + room(GRID[0])
        + [pltpu.VMEM((piece[2], piece[4]), jnp.bfloat16) for piece in pieces]
        + [pltpu.SemaphoreType.DMA(shape) for shape in sems]
        + [
            pltpu.VMEM(small.shape, jnp.float32),
            pltpu.VMEM(slot, jnp.float32),
            pltpu.VMEM(small.shape, jnp.float32),
        ]
        + [pltpu.SemaphoreType.DMA((count,))] * 4,
        compiler_params=pltpu.CompilerParams(
            collective_id=collective, has_side_effects=True, vmem_limit_bytes=VMEM_LIMIT
        ),
        name="scatter_grads",
    )(*grads, *passing, small)
    return (
        arrays[:kinds],
        arrays[kinds : 2 * kinds],
        arrays[2 * kinds :],
        jnp.sum(squares),
        carve(total.reshape(-1), [value.shape for value in values]),
    )


def lay_out_kernel(shards, view_ref, *outs):
    cut = D // shards * (4 * D + FF) // LANES
    for layer in range(L):
        upper, lower = outs[2 * layer : 2 * layer + 2]
        for ref, base in ((upper, 0), (lower, cut)):
            across = ref.shape[1] // LANES
            for row in range(0, ref.shape[0], ROW_GROUP):
                for column in range(across):
                    start = L * (base + row * across + column) + layer
                    rows = view_ref[pl.ds(start, ROW_GROUP, stride=L * across), :]
                    ref[row : row + ROW_GROUP, column * LANES : (column + 1) * LANES] = rows.astype(
                        jnp.bfloat16
                    )


def flat_view(array):
    layers, size = array.shape
    return array.reshape(layers, size // LANES, LANES).transpose(1, 0, 2).reshape(-1, LANES)


def unpack_kernel(size, x_ref, lead_ref, time_ref, text_ref, audio_ref, caption_ref, tail_ref, flat):
    count, rows = x_ref.shape[:2]
    lane = lax.broadcasted_iota(jnp.int32, (rows, LANES), 1)
    for rank in range(count):
        base, phase = divmod(rank * size, LANES)
        shard = x_ref[rank].astype(jnp.float32)
        if phase == 0:
            flat[base : base + rows, :] = shard
            continue
        turned = pltpu.roll(shard, phase, axis=1)
        pltpu.store(flat.at[pl.ds(base, rows), :], turned, mask=lane >= phase)
        pltpu.store(flat.at[pl.ds(base + 1, rows), :], turned, mask=lane < phase)
    start = lead_ref.shape[0]
    lead_ref[...] = flat[:start, :]
    for ref in (time_ref, text_ref, audio_ref, caption_ref):
        across = ref.shape[1] // LANES
        for row in range(0, ref.shape[0], ROW_GROUP):
            for column in range(across):
                ref[row : row + ROW_GROUP, column * LANES : (column + 1) * LANES] = flat[
                    pl.ds(start + row * across + column, ROW_GROUP, stride=across), :
                ].astype(jnp.bfloat16)
        start += ref.shape[0] * across
    tail_ref[...] = flat[start : start + tail_ref.shape[0], :]


def unpack_others(gathered, size, channels, text_width):
    count, rows, lanes = gathered.shape
    lead = 2 * channels * D // LANES
    shapes = [(D, D), (text_width, D), (D, E), (text_width, E)]
    tail = (2 * L + 1 + 1) * D // LANES
    whole = -(-count * size // LANES)
    outs = pl.pallas_call(
        functools.partial(unpack_kernel, size),
        out_shape=[jax.ShapeDtypeStruct((lead, LANES), jnp.float32)]
        + [jax.ShapeDtypeStruct(shape, jnp.bfloat16) for shape in shapes]
        + [jax.ShapeDtypeStruct((tail, LANES), jnp.float32)],
        in_specs=[pl.BlockSpec(memory_space=pltpu.VMEM)],
        out_specs=[pl.BlockSpec(memory_space=pltpu.VMEM)] * 6,
        scratch_shapes=[pltpu.VMEM((whole + 2 * rows, LANES), jnp.float32)],
        compiler_params=pltpu.CompilerParams(vmem_limit_bytes=VMEM_LIMIT),
        name="unpack_others",
    )(gathered)
    w_in, w_out = outs[0].reshape(2, channels * D)
    tail_rows = outs[5].reshape(-1, D)
    return (
        w_in.reshape(channels, D).astype(jnp.bfloat16),
        w_out.reshape(D, channels).astype(jnp.bfloat16),
        *outs[1:5],
        tail_rows[:-1],
        tail_rows[-1],
    )


def lay_out(anchor, shards):
    if shards != math.prod(GRID):
        return [layer_rows(anchor[depth].astype(jnp.bfloat16), shards) for depth in range(L)]
    shapes = [(D // shards, 4 * D + FF), (FF // shards, D)] * L
    outs = pl.pallas_call(
        functools.partial(lay_out_kernel, shards),
        out_shape=[jax.ShapeDtypeStruct(shape, jnp.bfloat16) for shape in shapes],
        in_specs=[pl.BlockSpec(memory_space=pltpu.VMEM)],
        out_specs=[pl.BlockSpec(memory_space=pltpu.VMEM)] * len(shapes),
        compiler_params=pltpu.CompilerParams(vmem_limit_bytes=VMEM_LIMIT),
        name="lay_out",
    )(flat_view(anchor))
    return [(outs[2 * depth], outs[2 * depth + 1]) for depth in range(L)]


def flatten(parts):
    return jnp.concatenate([part.reshape(-1) for part in parts])


def group_mean(delta, count):
    low = lax.reduce_precision(delta, 8, 7)
    total = low
    for step in range(1, count):
        moves = [(source, (source + step) % count) for source in range(count)]
        total = total + lax.ppermute(low.astype(jnp.bfloat16), "grp", moves).astype(jnp.float32)
    return total / count


STEP_BLOCKS = 8


def delta_of(grad, first, second, anchor):
    return adam(grad, first, second, anchor)[2]


def step_kernel(cut, places, factors, *refs):
    amount = len(places)
    own, twin = refs[:amount], refs[amount : 2 * amount]
    anchor, first, second, outer, twin_first, twin_second = refs[2 * amount : 2 * amount + 6]
    new, one, two, mean_out, momentum_out, own_flat, twin_flat = refs[2 * amount + 6 :]
    step = pl.program_id(0)
    block = anchor.shape[0]

    @pl.when(step == 0)
    def _():
        for grads, flat in ((own, own_flat), (twin, twin_flat)):
            for ref, (layer, first_column) in zip(grads, places):
                base, width = (cut, ref.shape[1]) if first_column is None else (0, 4 * D + FF)
                across, skip = width // LANES, (first_column or 0) // LANES
                for row in range(0, ref.shape[0], ROW_GROUP):
                    for column in range(ref.shape[1] // LANES):
                        start = L * (base + row * across + skip + column) + layer
                        flat[pl.ds(start, ROW_GROUP, stride=L * across), :] = ref[
                            row : row + ROW_GROUP, column * LANES : (column + 1) * LANES
                        ].astype(jnp.float32)

    rows = pl.ds(pl.multiple_of(step * block, SUBLANES), block)
    grad, weight = own_flat[rows, :], anchor[...]
    first_own, second_own = first[...], second[...]
    clipped = grad * factors[0]
    one[...] = beta_one * first_own + (1.0 - beta_one) * clipped
    two[...] = beta_two * second_own + (1.0 - beta_two) * clipped * clipped
    rounded = grad.astype(jnp.bfloat16).astype(jnp.float32)
    delta_own = delta_of(rounded * factors[0], first_own, second_own, weight)
    delta_twin = delta_of(twin_flat[rows, :] * factors[1], twin_first[...], twin_second[...], weight)
    mean = (delta_own + delta_twin) * 0.5
    momentum = outer_mu * outer[...] + mean
    mean_out[...] = mean
    momentum_out[...] = momentum
    new[...] = weight - outer_rate * (mean + outer_mu * momentum)


def step_layers(factors, own, twin, views, shards):
    rows = views[0].shape[0]
    places = tuple((layer, column) for _, layer, column in own)
    own = [grad for grad, _, _ in own]
    block = rows // STEP_BLOCKS
    whole = pl.BlockSpec(memory_space=pltpu.VMEM)
    part = pl.BlockSpec((block, LANES), lambda k: (k, 0))
    return pl.pallas_call(
        functools.partial(step_kernel, D // shards * (4 * D + FF) // LANES, places),
        grid=(STEP_BLOCKS,),
        out_shape=[jax.ShapeDtypeStruct((rows, LANES), jnp.float32)] * 5,
        in_specs=[pl.BlockSpec(memory_space=pltpu.SMEM)] + [whole] * (2 * len(own)) + [part] * 6,
        out_specs=[part] * 5,
        scratch_shapes=[pltpu.VMEM((rows, LANES), jnp.float32)] * 2,
        compiler_params=pltpu.CompilerParams(
            vmem_limit_bytes=VMEM_LIMIT, dimension_semantics=("arbitrary",)
        ),
        name="step_layers",
    )(factors, *own, *twin, *views)


def from_view(view):
    rows, lanes = view.shape
    return view.reshape(rows // L, L, lanes).transpose(1, 0, 2).reshape(L, rows // L * lanes)


def swapped(value):
    return lax.ppermute(value, "grp", [(0, 1), (1, 0)])


def per_device(
    anchor_layers,
    anchor_other,
    first_layers,
    first_other,
    second_layers,
    second_other,
    outer_layers,
    outer_other,
    latents,
    noise,
    lengths,
    timesteps,
    null_flags,
    captions,
):
    seq_count = lax.axis_size("seq")
    group_count = lax.axis_size("grp")
    rank = lax.axis_index("seq")
    group = lax.axis_index("grp")
    close = seq_count == math.prod(GRID) and group_count == 2
    rows = latents.shape[0]
    channels = latents.shape[1]
    frames_group = rows * seq_count
    lengths = lengths[0]
    timesteps = timesteps[0]
    null_flags = null_flags[0]
    captions = captions[0]
    item_count = lengths.shape[0]
    text_width = captions.shape[1]
    other_size = anchor_other.shape[0]
    padded = -(-other_size // 4096) * 4096
    other_rows = jnp.pad(anchor_other.astype(jnp.bfloat16), (0, padded - other_size))
    own_rows = lay_out(anchor_layers, seq_count)
    early = L
    own_block = block_of(rank, close)
    frames = jnp.concatenate([latents, noise], axis=1).T
    pieces = [frames, other_rows.reshape(-1, LANES)]
    pieces += [part for pair in own_rows[:early] for part in pair]
    gathered_frames, other_rows, *early_rows = gather_pieces(
        pieces, [False, True] + [True, False] * early, 4
    )
    if close:
        first_view, second_view = flat_view(first_layers[0]), flat_view(second_layers[0])
        sources, other_rows = lax.optimization_barrier(
            ((first_view, second_view, first_other[0], second_other[0]), other_rows)
        )
        twin_views = [swapped(value) for value in sources[:2]]
        twin_moments = [swapped(value) for value in sources[2:]]
    late_rows = [lax.all_gather(part, "seq", axis=0) for pair in own_rows[early:] for part in pair]
    layer_parts = [part.reshape(-1, part.shape[-1]) for part in early_rows + late_rows]
    gathered = [split_upper(*layer_parts[2 * depth : 2 * depth + 2]) for depth in range(L)]
    if close:
        other_parts = unpack_others(other_rows, other_size, channels, text_width)
    else:
        other_low = other_rows.reshape(seq_count, padded)[:, :other_size].reshape(-1)
        other_parts = carve(other_low, other_shapes(channels, D, text_width, E, L))
    w_in, w_out, w_time, w_text, w_audio, w_caption, gains, null_text = other_parts
    w_time_f = w_time.astype(jnp.float32)
    w_text_f = w_text.astype(jnp.float32)
    w_audio_f = w_audio.astype(jnp.float32)
    w_caption_f = w_caption.astype(jnp.float32)
    gains_f = gains.astype(jnp.float32)
    null_f = null_text.astype(jnp.float32)
    places = own_block * rows + jnp.arange(rows, dtype=jnp.int32)
    order = jnp.arange(item_count, dtype=jnp.int32)
    ends = jnp.sum(jnp.where(order[None, :] <= order[:, None], lengths[None, :], 0), axis=1)
    item = jnp.sum((places[:, None] >= ends[None, :]).astype(jnp.int32), axis=1)
    key_places = own_block * rows + jnp.arange(-2 * rows, 3 * rows, dtype=jnp.int32)
    key_item = jnp.sum((key_places[:, None] >= ends[None, :]).astype(jnp.int32), axis=1)
    key_item = jnp.where((key_places >= 0) & (key_places < frames_group), key_item, -1)
    items = (item, key_item)
    window_hot = (key_item[:, None] == jnp.arange(item_count, dtype=jnp.int32)[None, :]).astype(
        jnp.float32
    )
    inner = slice(2 * rows, 3 * rows)
    onehot = window_hot[inner]
    lengths_f = lengths[:, None].astype(jnp.float32)
    alpha_bar = plan(timesteps)
    mixing = exact(window_hot, jnp.stack([jnp.sqrt(alpha_bar), jnp.sqrt(1.0 - alpha_bar)], axis=1))
    near = frame_window(frames, gathered_frames, own_block, close).T
    noise = near[inner, channels:]
    noisy_low = (mixing[:, 0:1] * near[:, :channels] + mixing[:, 1:2] * near[:, channels:]).astype(
        jnp.bfloat16
    )
    features = time_features(timesteps)

    text = jnp.where(null_flags[:, None] == 1, null_f[None, :], captions)
    before_silu = exact(features, w_time_f) + exact(text, w_text_f)
    condition, pull_silu = jax.vjp(jax.nn.silu, before_silu)
    hidden_window = dense(noisy_low, w_in) + exact(window_hot, condition)
    saved_all = []
    entering = []
    for depth in range(L):
        weights = gathered[depth]
        proj_qkv = weights[0]
        if depth == 0:
            normed_window = norm_rows(hidden_window, gains_f[0]).astype(jnp.bfloat16)
            hidden, normed = hidden_window[inner], normed_window[inner]
            queries = dense(normed, proj_qkv[:, :D]).astype(jnp.bfloat16)
            window = dense(normed_window, proj_qkv[:, D:]).astype(jnp.bfloat16)
        else:
            normed = norm_rows(hidden, gains_f[2 * depth]).astype(jnp.bfloat16)
            window = gather_window(dense(normed, proj_qkv[:, D:]).astype(jnp.bfloat16), close)
            queries = dense(normed, proj_qkv[:, :D]).astype(jnp.bfloat16)
        entering.append(hidden)
        hidden, saved = layer_forward(
            hidden, normed, queries, window, weights, gains_f[2 * depth + 1], items
        )
        saved_all.append(saved)
    final = norm_rows(hidden, gains_f[2 * L])
    final_low = final.astype(jnp.bfloat16)
    predicted = dense(final_low, w_out)
    error = predicted - noise
    part_pool = contract_rows(onehot, final, HIGH)
    squared_sum, pool_sum = sum_over_seq((jnp.sum(error * error), part_pool), 1)
    pooled = pool_sum / lengths_f
    audio_side = exact(pooled, w_audio_f)
    text_side = exact(captions, w_caption_f)
    clash, pull_clash = jax.vjp(contrast, audio_side, text_side)
    loss = squared_sum / (frames_group * channels) + contrast_weight * clash
    grad_audio_side, grad_text_side = pull_clash(jnp.float32(contrast_weight))
    grad_pred = (2.0 / (frames_group * channels) * error).astype(jnp.bfloat16)
    grad_w_out = contract_rows(grad_pred, final_low)
    grad_pooled = against_rows(grad_audio_side, w_audio_f, HIGH) / lengths_f
    grad_final = against_rows(grad_pred, w_out) + exact(onehot, grad_pooled)
    unused, pull_final = jax.vjp(norm_rows, hidden, gains_f[2 * L])
    grad_hidden, grad_gain_final = pull_final(grad_final)
    layer_grads = [None] * L
    sent_early = [None] * L
    gain_grads = [None] * (2 * L + 1)
    gain_grads[2 * L] = grad_gain_final
    for depth in reversed(range(L)):
        weights = gathered[depth]
        proj_qkv = weights[0]
        early = depth > 0 and close
        grad_middle, grad_query, grad_pairs, rest, lower_full, gain_grads[2 * depth + 1] = layer_backward(
            grad_hidden, weights, gains_f[2 * depth + 1], items, saved_all[depth], early
        )
        if early:
            sent_early[depth] = [
                lax.psum_scatter(grad, "seq", scatter_dimension=0, tiled=True)
                for grad in (lower_full, rest)
            ]
        normed = saved_all[depth][0]
        if depth == 0:
            qkv_parts = [(normed, grad_query), (normed_window, grad_pairs)]
            grad_normed = against_rows(grad_pairs, proj_qkv[:, D:])
            grad_own = grad_normed[inner] + against_rows(grad_query, proj_qkv[:, :D])
            grad_normed = jnp.concatenate(
                [grad_normed[: 2 * rows], grad_own, grad_normed[3 * rows :]], axis=0
            )
            unused, pull_one = jax.vjp(norm_rows, hidden_window, gains_f[0])
        else:
            grad_pairs = return_window(grad_pairs, rows, close).astype(jnp.bfloat16)
            grad_projected = jnp.concatenate([grad_query, grad_pairs], axis=1)
            qkv_parts = [(normed, grad_projected)]
            grad_normed = against_rows(grad_projected, proj_qkv)
            unused, pull_one = jax.vjp(norm_rows, entering[depth], gains_f[2 * depth])
        grad_input, gain_grads[2 * depth] = pull_one(grad_normed)
        if early:
            layer_grads[depth] = [side_by_side(qkv_parts)]
        else:
            layer_grads[depth] = [side_by_side(qkv_parts + rest), lower_full]
        if depth > 0:
            grad_hidden = grad_middle + grad_input
        else:
            grad_hidden = jnp.concatenate(
                [grad_input[: 2 * rows], grad_input[inner] + grad_middle, grad_input[3 * rows :]], axis=0
            )
    grad_w_in = contract_rows(noisy_low.astype(jnp.float32), grad_hidden, HIGH)
    grad_condition = contract_rows(window_hot, grad_hidden, HIGH)
    lead = 2 * channels
    features_at, text_at = lead, lead + D
    audio_at = text_at + text_width
    caption_at = audio_at + D * E // D
    gains_at = caption_at + text_width * E // D
    own_rows_count = -(-other_size // D) + 1
    own_start = rank * other_size
    own_row = own_start // D
    own_at = own_row + jnp.arange(own_rows_count, dtype=jnp.int32)

    def own_part(value, start):
        reach = gains_at + 2 * own_rows_count
        value = jnp.pad(value, ((0, 0), (start, reach - start - value.shape[1])))
        return lax.dynamic_slice_in_dim(value, own_row, own_rows_count, axis=1)

    def own_rows_at(start, amount):
        there = start + jnp.arange(amount, dtype=jnp.int32)
        return (there[:, None] == own_at[None, :]).astype(jnp.float32)

    left_condition = own_part(features, features_at) + own_part(text, text_at)
    early_view = thirds(pooled, grad_audio_side, own_at - audio_at)
    early_view = early_view + thirds(captions, grad_text_side, own_at - caption_at)
    early_view, left_condition, layer_grads[0] = lax.optimization_barrier(
        (early_view, left_condition, layer_grads[0])
    )
    small_grads = (grad_w_in, grad_w_out, grad_condition, jnp.stack(gain_grads))
    if close:
        sent = sent_early[1:]
        late = [layer_grads[depth][0] for depth in range(1, L)] + list(layer_grads[0])
        own_late, twin_late, passed, square_part, small_grads = scatter_grads(
            late,
            [1] * (L - 1) + [UPPER_CUTS, 1],
            [part for parts in sent for part in parts],
            small_grads,
            5,
        )
        own_parts = [(own_late[L - 1], 0, 0), (own_late[L], 0, None)]
        twin_parts = [twin_late[L - 1], twin_late[L]]
        for depth in range(1, L):
            lower, rest = sent[depth - 1]
            own_parts += [(own_late[depth - 1], depth, 0), (rest, depth, 3 * D), (lower, depth, None)]
            twin_parts += [twin_late[depth - 1], passed[2 * depth - 1], passed[2 * depth - 2]]
    else:
        small_grads = lax.psum(small_grads, "seq")
    grad_w_in, grad_w_out, grad_condition, gain_rows = small_grads
    grad_before = pull_silu(grad_condition)[0]
    grad_null = jnp.sum(
        jnp.where(null_flags[:, None] == 1, against_rows(grad_before, w_text_f, HIGH), 0.0), axis=0
    )
    own_view = early_view + contract_rows(left_condition, grad_before, HIGH)
    for value, start in (
        (grad_w_in, 0),
        (grad_w_out.T.reshape(channels, D), channels),
        (gain_rows, gains_at),
        (grad_null[None], gains_at + gain_rows.shape[0]),
    ):
        own_view = own_view + contract_rows(own_rows_at(start, value.shape[0]), value, HIGH)
    other_grad = lax.dynamic_slice_in_dim(own_view.reshape(-1), own_start % D, other_size)
    other_grad_square = jnp.sum(other_grad * other_grad)
    if close:
        other_grad_low = other_grad.astype(jnp.bfloat16)
        twin_other = swapped(other_grad_low).astype(jnp.float32)
        square_part = square_part + other_grad_square
        for parts in sent:
            for grad in parts:
                wide = grad.astype(jnp.float32)
                square_part = square_part + jnp.sum(wide * wide)
        norms = jnp.sqrt(sums_by_group(square_part, 3))
        total_norm = lax.dynamic_index_in_dim(norms, group, keepdims=False)
        twin_norm = lax.dynamic_index_in_dim(norms, 1 - group, keepdims=False)
        factor = jnp.minimum(1.0, clip_at / (total_norm + 1e-06))
        twin_factor = jnp.minimum(1.0, clip_at / (twin_norm + 1e-06))
        views = [flat_view(anchor_layers), first_view, second_view, flat_view(outer_layers)]
        stepped = step_layers(
            jnp.stack([factor, twin_factor]),
            own_parts,
            twin_parts,
            views + twin_views,
            seq_count,
        )
        new_layers, first_l, second_l, mean_layers, momentum_layers = map(from_view, stepped)
        first_o, second_o, _ = adam(other_grad * factor, first_other[0], second_other[0], anchor_other)
        rounded = lax.reduce_precision(other_grad, 8, 7)
        delta_o = delta_of(rounded * factor, first_other[0], second_other[0], anchor_other)
        delta_twin = delta_of(twin_other * twin_factor, *twin_moments, anchor_other)
        mean_other = (delta_o + delta_twin) / 2
    else:
        stacked = jnp.stack(
            [
                flatten(
                    lax.psum_scatter(grad, "seq", scatter_dimension=0, tiled=True).astype(jnp.float32)
                    for grad in grads
                )
                for grads in layer_grads
            ]
        )
        total_norm = jnp.sqrt(lax.psum(jnp.sum(stacked * stacked) + other_grad_square, "seq"))
        factor = jnp.minimum(1.0, clip_at / (total_norm + 1e-06))
        first_l, second_l, delta_l = adam(
            stacked * factor, first_layers[0], second_layers[0], anchor_layers
        )
        first_o, second_o, delta_o = adam(
            other_grad * factor, first_other[0], second_other[0], anchor_other
        )
        mean_layers = group_mean(delta_l, group_count)
        mean_other = group_mean(delta_o, group_count)
        momentum_layers = outer_mu * outer_layers + mean_layers
        new_layers = anchor_layers - outer_rate * (mean_layers + outer_mu * momentum_layers)
    momentum_other = outer_mu * outer_other + mean_other
    new_other = anchor_other - outer_rate * (mean_other + outer_mu * momentum_other)
    return (
        new_layers,
        new_other,
        first_l[None],
        first_o[None],
        second_l[None],
        second_o[None],
        mean_layers,
        mean_other,
        momentum_layers,
        momentum_other,
        loss.reshape(1),
        total_norm.reshape(1),
    )


def solution(mesh):
    placed = (
        P(None, "seq"),
        P("seq"),
        P("grp", None, "seq"),
        P("grp", "seq"),
        P("grp", None, "seq"),
        P("grp", "seq"),
        P(None, "seq"),
        P("seq"),
        P(("grp", "seq"), None),
        P(("grp", "seq"), None),
        P("grp", None),
        P("grp", None),
        P("grp", None),
        P("grp", None, None),
    )
    return jax.shard_map(
        per_device,
        mesh=mesh,
        in_specs=placed,
        out_specs=(
            P(None, "seq"),
            P("seq"),
            P("grp", None, "seq"),
            P("grp", "seq"),
            P("grp", None, "seq"),
            P("grp", "seq"),
            P(None, "seq"),
            P("seq"),
            P(None, "seq"),
            P("seq"),
            P("grp"),
            P("grp"),
        ),
        check_vma=False,
    )
```

```python
import functools
import math

import jax
import jax.numpy as jnp
from jax import lax
from jax.experimental import pallas as pl
from jax.experimental.pallas import tpu as pltpu
from jax.sharding import PartitionSpec as P

D = 768
HEADS = 12
HD = 64
FF = 3072
E = 512
L = 2
TSTEPS = 1000
STEP_COUNT = 10


HIGH = lax.Precision.HIGHEST
beta_one = 0.9
beta_two = 0.95
adam_eps = 1e-08
decay_rate = 0.01
inner_rate = 0.02
outer_rate = 0.7
outer_mu = 0.9
clip_at = 0.01
logit_scale = 30.0
contrast_weight = 0.05


def block_of(rank, close):
    if not close:
        return rank
    turn = (rank // 4) % 2
    return rank + 2 * turn * (1 - 2 * ((rank // 2) % 2))


def passed_along(value, axis, steps, close):
    count = lax.axis_size(axis)
    holder = {block_of(rank, close): rank for rank in range(count)}
    initial, last = (max(0, -steps), min(count, count - steps))
    return lax.ppermute(
        value, axis, [(holder[source], holder[source + steps]) for source in range(initial, last)]
    )


def dense(left, right):
    return jnp.dot(left, right, preferred_element_type=jnp.float32)


def exact(left, right):
    return jnp.dot(left, right, precision=HIGH, preferred_element_type=jnp.float32)


def contract_rows(left, right, precision=None):
    return lax.dot_general(
        left,
        right,
        (((0,), (0,)), ((), ())),
        precision=precision,
        preferred_element_type=jnp.float32,
    )


def against_rows(left, right, precision=None):
    return lax.dot_general(
        left,
        right,
        (((1,), (1,)), ((), ())),
        precision=precision,
        preferred_element_type=jnp.float32,
    )


def carve(flat, shapes):
    pieces = []
    start = 0
    for shape in shapes:
        count = math.prod(shape)
        pieces.append(flat[start : start + count].reshape(shape))
        start += count
    return pieces


def layer_rows(piece, shards):
    cut = D // shards * (4 * D + FF)
    return piece[:cut].reshape(D // shards, 4 * D + FF), piece[cut:].reshape(FF // shards, D)


def split_upper(upper, lower):
    return [upper[:, : 3 * D], upper[:, 3 * D : 4 * D], upper[:, 4 * D :], lower]


def other_shapes(channels, width, text_width, joint_width, blocks):
    return [
        (channels, width),
        (width, channels),
        (width, width),
        (text_width, width),
        (width, joint_width),
        (text_width, joint_width),
        (2 * blocks + 1, width),
        (text_width,),
    ]


def norm_rows(hidden, gain):
    centred = hidden - jnp.mean(hidden, axis=-1, keepdims=True)
    return centred * lax.rsqrt(jnp.mean(centred * centred, axis=-1, keepdims=True) + 1e-05) * gain


def plan(steps):
    angle = (steps.astype(jnp.float32) / TSTEPS + 0.008) / 1.008 * (math.pi / 2)
    return jnp.cos(angle) ** 2


def time_features(steps):
    half = D // 2
    frequency = jnp.exp(-math.log(10000.0) * jnp.arange(half, dtype=jnp.float32) / half)
    angle = steps.astype(jnp.float32)[:, None] * frequency[None, :]
    return jnp.concatenate([jnp.cos(angle), jnp.sin(angle)], axis=1)


def contrast(audio_side, text_side):
    audio_unit = audio_side * lax.rsqrt(
        jnp.sum(audio_side * audio_side, axis=-1, keepdims=True) + 1e-06
    )
    text_unit = text_side * lax.rsqrt(
        jnp.sum(text_side * text_side, axis=-1, keepdims=True) + 1e-06
    )
    logits = logit_scale * jnp.dot(audio_unit, text_unit.T, precision=HIGH)
    diagonal = logit_scale * jnp.sum(audio_unit * text_unit, axis=-1)
    row_terms = jax.nn.logsumexp(logits, axis=1) - diagonal
    column_terms = jax.nn.logsumexp(logits, axis=0) - diagonal
    return 0.5 * (jnp.mean(row_terms) + jnp.mean(column_terms))


def gather_window(local_pairs, close):
    pieces = {}
    for step in (2, 1, -1, -2):
        pieces[step] = passed_along(local_pairs, "seq", step, close)
    return jnp.concatenate([pieces[2], pieces[1], local_pairs, pieces[-1], pieces[-2]], axis=0)


def return_window(grad_window, rows, close):
    total = grad_window[2 * rows : 3 * rows].astype(jnp.float32)
    for slot, step in ((0, 2), (1, 1), (3, -1), (4, -2)):
        total = total + passed_along(
            grad_window[slot * rows : (slot + 1) * rows], "seq", -step, close
        ).astype(jnp.float32)
    return total


LANES = 128
LOG2E = math.log2(math.e)
PAIRS = HEADS * HD // LANES
VMEM_LIMIT = 50 * 1024 * 1024


def lane_masks(dtype):
    lane = lax.broadcasted_iota(jnp.int32, (1, LANES), 1)
    return [(lane < HD).astype(dtype), (lane >= HD).astype(dtype)]


def fill_bias(bias_ref, query_item_ref, key_item_ref):
    keep = key_item_ref[...] == query_item_ref[...]
    bias_ref[...] = jnp.where(keep, 0.0, -1e30).astype(jnp.float32)


def attend_forward_kernel(q_ref, kv_ref, query_item_ref, key_item_ref, o_ref, lse_ref, bias_ref):
    fill_bias(bias_ref, query_item_ref, key_item_ref)
    width = HEADS * HD
    masks = lane_masks(jnp.bfloat16)
    lse_ref[...] = jnp.zeros_like(lse_ref)
    for pair in range(PAIRS):
        cols = slice(pair * LANES, (pair + 1) * LANES)
        query = q_ref[:, cols] * jnp.bfloat16(HD ** (-0.5))
        key_rows = kv_ref[:, cols]
        value_rows = kv_ref[:, width + pair * LANES : width + (pair + 1) * LANES]
        halves = []
        for half in range(2):
            scores = against_rows(key_rows, query * masks[half]) * LOG2E + bias_ref[...]
            peak = jnp.max(scores, axis=0, keepdims=True)
            weights = jnp.exp2(scores - peak)
            total = jnp.sum(weights, axis=0, keepdims=True)
            mixed = contract_rows(value_rows, weights.astype(jnp.bfloat16)) * (1.0 / total)
            halves.append(mixed[half * HD : (half + 1) * HD])
            lse_ref[2 * pair + half : 2 * pair + half + 1, :] = peak + jnp.log2(total)
        o_ref[:, cols] = jnp.concatenate(halves, axis=0).T.astype(o_ref.dtype)


def attend_forward(queries, window, query_item, key_item):
    rows, width = queries.shape
    span = window.shape[0]
    return pl.pallas_call(
        attend_forward_kernel,
        out_shape=(
            jax.ShapeDtypeStruct((rows, width), jnp.bfloat16),
            jax.ShapeDtypeStruct((16, rows), jnp.float32),
        ),
        in_specs=[pl.BlockSpec(memory_space=pltpu.VMEM)] * 4,
        out_specs=(pl.BlockSpec(memory_space=pltpu.VMEM),) * 2,
        scratch_shapes=[pltpu.VMEM((span, rows), jnp.float32)],
        compiler_params=pltpu.CompilerParams(vmem_limit_bytes=VMEM_LIMIT),
        cost_estimate=pl.CostEstimate(
            flops=4 * rows * span * width,
            transcendentals=rows * span * HEADS,
            bytes_accessed=4 * rows * width + 4 * span * width,
        ),
        name="attend_forward",
    )(queries, window, query_item[None, :], key_item[:, None])


def attend_backward_kernel(
    q_ref, kv_ref, do_ref, lse_ref, query_item_ref, key_item_ref, dq_ref, dkv_ref, bias_ref
):
    fill_bias(bias_ref, query_item_ref, key_item_ref)
    width = HEADS * HD
    masks = lane_masks(jnp.bfloat16)
    for pair in range(PAIRS):
        cols = slice(pair * LANES, (pair + 1) * LANES)
        value_cols = slice(width + pair * LANES, width + (pair + 1) * LANES)
        query = q_ref[:, cols] * jnp.bfloat16(HD ** (-0.5))
        key_rows = kv_ref[:, cols]
        value_rows = kv_ref[:, value_cols]
        grad_out = do_ref[:, cols]
        halves = []
        grad_key = grad_value = None
        for half in range(2):
            query_half = query * masks[half]
            grad_half = grad_out * masks[half]
            scores = against_rows(key_rows, query_half) * LOG2E + bias_ref[...]
            shares = jnp.exp2(scores - lse_ref[2 * pair + half : 2 * pair + half + 1, :])
            grad_shares = against_rows(value_rows, grad_half)
            inner = jnp.sum(grad_shares * shares, axis=0, keepdims=True)
            grad_scores = (shares * (grad_shares - inner)).astype(jnp.bfloat16)
            one_value = dense(shares.astype(jnp.bfloat16), grad_half)
            one_key = dense(grad_scores, query_half)
            grad_value = one_value if grad_value is None else grad_value + one_value
            grad_key = one_key if grad_key is None else grad_key + one_key
            one_query = contract_rows(key_rows, grad_scores)
            halves.append(one_query[half * HD : (half + 1) * HD])
        grad_query = jnp.concatenate(halves, axis=0).T * HD ** (-0.5)
        dq_ref[:, cols] = grad_query.astype(dq_ref.dtype)
        dkv_ref[:, cols] = grad_key.astype(dkv_ref.dtype)
        dkv_ref[:, value_cols] = grad_value.astype(dkv_ref.dtype)


def attend_backward(queries, window, grad_out, lse, query_item, key_item):
    rows, width = queries.shape
    span = window.shape[0]
    return pl.pallas_call(
        attend_backward_kernel,
        out_shape=(
            jax.ShapeDtypeStruct((rows, width), jnp.bfloat16),
            jax.ShapeDtypeStruct((span, 2 * width), jnp.bfloat16),
        ),
        in_specs=[pl.BlockSpec(memory_space=pltpu.VMEM)] * 6,
        out_specs=(pl.BlockSpec(memory_space=pltpu.VMEM),) * 2,
        scratch_shapes=[pltpu.VMEM((span, rows), jnp.float32)],
        compiler_params=pltpu.CompilerParams(vmem_limit_bytes=VMEM_LIMIT),
        cost_estimate=pl.CostEstimate(
            flops=10 * rows * span * width,
            transcendentals=rows * span * HEADS,
            bytes_accessed=8 * rows * width + 8 * span * width,
        ),
        name="attend_backward",
    )(queries, window, grad_out, lse, query_item[None, :], key_item[:, None])


def layer_forward(hidden, normed, queries, window, weights, gain_two, items):
    proj_qkv, proj_out, proj_up, proj_down = weights
    attended, lse = attend_forward(queries, window, *items)
    middle = hidden + dense(attended, proj_out)
    second = norm_rows(middle, gain_two).astype(jnp.bfloat16)
    upper = dense(second, proj_up)
    activated = jax.nn.gelu(upper, approximate=True).astype(jnp.bfloat16)
    return (
        middle + dense(activated, proj_down),
        (normed, queries, window, lse, attended, middle, second, upper, activated),
    )


def layer_backward(grad_hidden, weights, gain_two, items, saved, early):
    normed, queries, window, lse, attended, middle, second, upper, activated = saved
    proj_qkv, proj_out, proj_up, proj_down = weights
    branch_top = grad_hidden.astype(jnp.bfloat16)
    grad_activated = against_rows(branch_top, proj_down)
    unused, pull_gelu = jax.vjp(lambda value: jax.nn.gelu(value, approximate=True), upper)
    grad_upper = pull_gelu(grad_activated)[0].astype(jnp.bfloat16)
    grad_second = against_rows(grad_upper, proj_up)
    unused, pull_two = jax.vjp(norm_rows, middle, gain_two)
    grad_middle, grad_gain_two = pull_two(grad_second)
    grad_middle = grad_middle + grad_hidden
    branch_mid = grad_middle.astype(jnp.bfloat16)
    grad_attended = against_rows(branch_mid, proj_out).astype(jnp.bfloat16)
    lower_full = contract_rows(activated, branch_top).astype(jnp.bfloat16)
    pairs = [(attended, branch_mid), (second, grad_upper)]
    if early:
        grad_attended, rest_full = lax.optimization_barrier((grad_attended, side_by_side(pairs)))
    grad_query, grad_window = attend_backward(queries, window, grad_attended, lse, *items)
    return grad_middle, grad_query, grad_window, (rest_full if early else pairs), lower_full, grad_gain_two


def side_by_side(pairs):
    return jnp.concatenate(
        [contract_rows(left, right).astype(jnp.bfloat16) for left, right in pairs], axis=1
    )


def frame_window(frames, gathered_frames, own_block, close):
    if close:
        count = gathered_frames.shape[0]
        parts = [
            lax.dynamic_index_in_dim(
                gathered_frames, jnp.clip(own_block + step, 0, count - 1), keepdims=False
            )
            for step in range(-2, 3)
        ]
    else:
        parts = [passed_along(frames, "seq", -step, close) for step in range(-2, 0)] + [frames]
        parts += [passed_along(frames, "seq", -step, close) for step in range(1, 3)]
    return jnp.concatenate(parts, axis=1)


def thirds(value, right, at):
    joint = right.shape[1]
    half = joint // 2
    inside = (at >= 0) & (at < value.shape[1] * joint // D)
    matrix_row, odd = at // 2 * 3, at % 2
    wanted = jnp.stack(
        [
            jnp.where(inside & (odd == parity), matrix_row + offset, -1)
            for parity, offset in ((0, 0), (0, 1), (1, 1), (1, 2))
        ]
    )
    width = jnp.arange(value.shape[1], dtype=jnp.int32)
    choice = (width[:, None, None] == wanted[None]).astype(jnp.float32)
    left = jnp.einsum("iw,wkv->kiv", value, choice, precision=HIGH)
    rights = jnp.stack(
        [
            jnp.pad(right, ((0, 0), (0, half))),
            jnp.pad(right[:, :half], ((0, 0), (joint, 0))),
            jnp.pad(right[:, half:], ((0, 0), (0, joint))),
            jnp.pad(right, ((0, 0), (half, 0))),
        ]
    )
    return jnp.einsum("kiv,kid->vd", left, rights, precision=HIGH)


def adam(grad, first, second, anchor):
    first = beta_one * first + (1.0 - beta_one) * grad
    second = beta_two * second + (1.0 - beta_two) * grad * grad
    stepped = first * (1.0 / (1.0 - beta_one**STEP_COUNT))
    scaled = second * (1.0 / (1.0 - beta_two**STEP_COUNT))
    delta = inner_rate * (stepped / (jnp.sqrt(scaled) + adam_eps) + decay_rate * anchor)
    return (first, second, delta)


MESH = pl.DeviceIdType.MESH
SUBLANES = 8
CLOSE_RANKS = 16


def greet_seq(me, count):
    group = lax.axis_index("grp")
    barrier = pltpu.get_barrier_semaphore()

    def one(step, carry):
        pl.semaphore_signal(
            barrier, inc=1, device_id=(group, lax.rem(me + step, count)), device_id_type=MESH
        )
        return carry

    lax.fori_loop(1, count, one, 0)
    pl.semaphore_wait(barrier, count - 1)


def sum_kernel(count, x_ref, out_ref, parts, own, totals, send_one, recv_one, send_two, recv_two):
    me = lax.axis_index("seq")
    group = lax.axis_index("grp")
    greet_seq(me, count)

    def slice_copy(step):
        peer = lax.rem(me + step, count)
        return pltpu.make_async_remote_copy(
            src_ref=x_ref.at[peer],
            dst_ref=parts.at[step],
            send_sem=send_one.at[step],
            recv_sem=recv_one.at[step],
            device_id=(group, peer),
            device_id_type=MESH,
        )

    def total_copy(step):
        peer = lax.rem(me + step, count)
        return pltpu.make_async_remote_copy(
            src_ref=own,
            dst_ref=totals.at[step],
            send_sem=send_two.at[step],
            recv_sem=recv_two.at[step],
            device_id=(group, peer),
            device_id_type=MESH,
        )

    def start_of(make):
        def one(step, carry):
            make(step).start()
            return carry

        return one

    lax.fori_loop(1, count, start_of(slice_copy), 0)
    own[...] = x_ref[me]

    def gather_in(step, carry):
        slice_copy(step).wait()
        own[...] += parts[step]
        return carry

    lax.fori_loop(1, count, gather_in, 0)
    lax.fori_loop(1, count, start_of(total_copy), 0)
    out_ref[me] = own[...]

    def spread(step, carry):
        total_copy(step).wait()
        out_ref[lax.rem(me + count - step, count)] = totals[step]
        return carry

    lax.fori_loop(1, count, spread, 0)


def in_slices(values, count):
    size = sum(math.prod(value.shape) for value in values)
    block = -(-size // (count * SUBLANES * LANES)) * SUBLANES
    flat = jnp.concatenate([value.reshape(-1) for value in values])
    return jnp.pad(flat, (0, count * block * LANES - size)).reshape(count, block, LANES)


def sum_over_seq(values, collective):
    count = lax.axis_size("seq")
    if count != CLOSE_RANKS:
        return lax.psum(values, "seq")
    small = in_slices(values, count)
    shape = small.shape
    total = pl.pallas_call(
        functools.partial(sum_kernel, count),
        out_shape=jax.ShapeDtypeStruct(shape, jnp.float32),
        in_specs=[pl.BlockSpec(memory_space=pltpu.VMEM)],
        out_specs=pl.BlockSpec(memory_space=pltpu.VMEM),
        scratch_shapes=[
            pltpu.VMEM(shape, jnp.float32),
            pltpu.VMEM(shape[1:], jnp.float32),
            pltpu.VMEM(shape, jnp.float32),
        ]
        + [pltpu.SemaphoreType.DMA((count,))] * 4,
        compiler_params=pltpu.CompilerParams(collective_id=collective, has_side_effects=True),
        cost_estimate=pl.CostEstimate(
            flops=math.prod(shape), transcendentals=0, bytes_accessed=16 * math.prod(shape)
        ),
        name="sum_over_seq",
    )(small)
    return carve(total.reshape(-1), [value.shape for value in values])


def share_kernel(count, x_ref, out_ref, parts, send_sem, recv_sem):
    seq = lax.axis_size("seq")
    me = lax.axis_index("grp") * seq + lax.axis_index("seq")

    def place(step):
        peer = lax.rem(me + step, count)
        return peer // seq, lax.rem(peer, seq)

    barrier = pltpu.get_barrier_semaphore()

    def greet(step, carry):
        pl.semaphore_signal(barrier, inc=1, device_id=place(step), device_id_type=MESH)
        return carry

    lax.fori_loop(1, count, greet, 0)
    pl.semaphore_wait(barrier, count - 1)

    def copy_of(step):
        return pltpu.make_async_remote_copy(
            src_ref=x_ref,
            dst_ref=parts.at[step],
            send_sem=send_sem.at[step],
            recv_sem=recv_sem.at[step],
            device_id=place(step),
            device_id_type=MESH,
        )

    def start(step, carry):
        copy_of(step).start()
        return carry

    lax.fori_loop(1, count, start, 0)
    out_ref[me] = x_ref[...]

    def finish(step, carry):
        copy_of(step).wait()
        out_ref[lax.rem(me + count - step, count)] = parts[step]
        return carry

    lax.fori_loop(1, count, finish, 0)


def sums_by_group(value, collective):
    groups, count = lax.axis_size("grp"), lax.axis_size("seq")
    shape = (groups * count, SUBLANES, LANES)
    shared = pl.pallas_call(
        functools.partial(share_kernel, groups * count),
        out_shape=jax.ShapeDtypeStruct(shape, jnp.float32),
        in_specs=[pl.BlockSpec(memory_space=pltpu.VMEM)],
        out_specs=pl.BlockSpec(memory_space=pltpu.VMEM),
        scratch_shapes=[pltpu.VMEM(shape, jnp.float32)]
        + [pltpu.SemaphoreType.DMA((groups * count,))] * 2,
        compiler_params=pltpu.CompilerParams(collective_id=collective, has_side_effects=True),
        name="share_over_all",
    )(jnp.full(shape[1:], value, jnp.float32))
    return jnp.sum(shared[:, 0, 0].reshape(groups, count), axis=1)


GRID = (4, 2, 2)
GATHER_Y_LAG = 2
GATHER_X_LAG = 7
GATHER_AHEAD = 0


def place_of(me):
    return me // 4, lax.rem(me // 2, 2), lax.rem(me, 2)


def rank_of(along, across, core):
    return (along * 2 + across) * 2 + core


def gather_kernel(shared, *refs):
    pieces = len(shared)
    own_refs, out_refs = refs[:pieces], refs[pieces : 2 * pieces]
    local_sem, z_send, z_recv, y_send, y_recv, x_send, x_recv, c_send, c_recv = refs[2 * pieces :]
    group, me = lax.axis_index("grp"), lax.axis_index("seq")
    z, y, core = place_of(me)
    z_size = GRID[0]
    across, sibling, twin = (
        (group, rank_of(z, 1 - y, core)),
        (group, rank_of(z, y, 1 - core)),
        (1 - group, me),
    )
    barrier = pltpu.get_barrier_semaphore()
    for there in (across, sibling, twin):
        pl.semaphore_signal(barrier, inc=1, device_id=there, device_id_type=MESH)

    @pl.when(z > 0)
    def _():
        pl.semaphore_signal(
            barrier, inc=1, device_id=(group, rank_of(z - 1, y, core)), device_id_type=MESH
        )

    @pl.when(z < z_size - 1)
    def _():
        pl.semaphore_signal(
            barrier, inc=1, device_id=(group, rank_of(z + 1, y, core)), device_id_type=MESH
        )

    neighbours = (z > 0).astype(jnp.int32) + (z < z_size - 1).astype(jnp.int32)
    pl.semaphore_wait(barrier, 3 + neighbours)

    def half_of(ref, piece, half):
        if half is None:
            return ref
        if ref.shape[-1] == LANES:
            span = ref.shape[-2] // 2
            return ref.at[pl.ds(pl.multiple_of(half * span, ROW_GROUP), span), :]
        span = ref.shape[-1] // 2
        return ref.at[:, pl.ds(pl.multiple_of(half * span, LANES), span)]

    def move(piece, half, there, along, over, send, recv, own=False):
        dst = half_of(out_refs[piece].at[rank_of(along, over, core)], piece, half)
        src = half_of(own_refs[piece], piece, half) if own else dst
        return pltpu.make_async_remote_copy(
            src_ref=src, dst_ref=dst, send_sem=send, recv_sem=recv, device_id=there, device_id_type=MESH
        )

    def z_move(piece, along, forward, own=False):
        there = (group, rank_of(z + (1 if forward else -1), y, core))
        half = group if shared[piece] else None
        return move(
            piece, half, there, along, y, z_send.at[piece, along, int(forward)], z_recv.at[piece, along], own
        )

    def y_move(piece, along, own=False, over=None):
        half = group if shared[piece] else None
        over = y if over is None else over
        return move(piece, half, across, along, over, y_send.at[piece, along], y_recv.at[piece, along], own)

    def x_move(piece, along, over, arriving=False):
        half = 1 - group if arriving else group
        slot = along * 2 + over
        return move(piece, half, twin, along, over, x_send.at[piece, slot], x_recv.at[piece, slot])

    def c_move(piece, along, over, half, slot, own=False):
        return move(
            piece,
            half,
            sibling,
            along,
            over,
            c_send.at[piece, along * 2 + over, slot],
            c_recv.at[piece, along * 2 + over, slot],
            own,
        )

    def each_along(distance, action):
        if distance == 0:
            action(z, True, True)
            return

        @pl.when(z - distance >= 0)
        def _():
            action(z - distance, True, False)

        @pl.when(z + distance < z_size)
        def _():
            action(z + distance, False, True)

    def own_sends(piece):
        pltpu.make_async_copy(own_refs[piece], out_refs[piece].at[me], local_sem.at[piece]).start()

        @pl.when(z + 1 < z_size)
        def _():
            z_move(piece, z, True, own=True).start()

        @pl.when(z > 0)
        def _():
            z_move(piece, z, False, own=True).start()

        y_move(piece, z, own=True).start()
        c_move(piece, z, y, None, 0, own=True).start()

    def z_arrivals(piece, distance):
        if distance == 0:
            return

        def one(along, onward, backward):
            z_move(piece, along, onward).wait_recv()

            @pl.when((z + 1 < z_size) if onward else (z > 0))
            def _():
                z_move(piece, along, onward).start()

            y_move(piece, along).start()
            if shared[piece]:
                x_move(piece, along, y).start()
            c_move(piece, along, y, group if shared[piece] else None, 0).start()

        each_along(distance, one)

    def y_arrivals(piece, distance):
        def one(along, *_):
            y_move(piece, along, over=1 - y).wait_recv()
            if shared[piece]:
                x_move(piece, along, 1 - y).start()
            c_move(piece, along, 1 - y, group if shared[piece] else None, 0).start()

        each_along(distance, one)

    def x_arrivals(piece, distance):
        if not shared[piece]:
            return

        def one(along, *_):
            for turn in range(2):
                over = y if turn == 0 else 1 - y
                if distance == 0 and turn == 0:
                    continue
                x_move(piece, along, over, arriving=True).wait_recv()
                c_move(piece, along, over, 1 - group, 1).start()

        each_along(distance, one)

    def drain(piece, distance):
        def one(along, onward, backward):
            own = distance == 0
            half = group if shared[piece] else None
            for turn in range(2):
                over = y if turn == 0 else 1 - y
                mine = own and turn == 0
                whole = None if mine else half
                c_move(piece, along, over, whole, 0).wait()
                if shared[piece] and not mine:
                    c_move(piece, along, over, 1 - group, 1).wait()
                    x_move(piece, along, over).wait_send()
            y_move(piece, along).wait_send()
            if onward:

                @pl.when(z + 1 < z_size)
                def _():
                    z_move(piece, along, True).wait_send()

            if backward:

                @pl.when(z > 0)
                def _():
                    z_move(piece, along, False).wait_send()

        each_along(distance, one)
        if distance == 0:
            pltpu.make_async_copy(own_refs[piece], out_refs[piece].at[me], local_sem.at[piece]).wait()

    slots = [(piece, distance) for piece in range(pieces) for distance in range(z_size)]
    own_sends(0)
    for turn in range(len(slots) + GATHER_X_LAG):
        if turn < len(slots):
            piece, distance = slots[turn]
            if distance == GATHER_AHEAD and piece + 1 < pieces:
                own_sends(piece + 1)
            z_arrivals(piece, distance)
        if 0 <= turn - GATHER_Y_LAG < len(slots):
            y_arrivals(*slots[turn - GATHER_Y_LAG])
        if 0 <= turn - GATHER_X_LAG < len(slots):
            x_arrivals(*slots[turn - GATHER_X_LAG])
    for slot in slots:
        drain(*slot)


def gather_pieces(pieces, shared, collective):
    count = lax.axis_size("seq")
    if count != math.prod(GRID) or lax.axis_size("grp") != 2:
        return [lax.all_gather(piece, "seq", axis=0) for piece in pieces]
    amount = len(pieces)
    sems = [
        (amount,),
        (amount, 4, 2),
        (amount, 4),
        (amount, 4),
        (amount, 4),
        (amount, 8),
        (amount, 8),
        (amount, 8, 2),
        (amount, 8, 2),
    ]
    return pl.pallas_call(
        functools.partial(gather_kernel, tuple(shared)),
        out_shape=[jax.ShapeDtypeStruct((count,) + piece.shape, piece.dtype) for piece in pieces],
        in_specs=[pl.BlockSpec(memory_space=pl.ANY)] * amount,
        out_specs=[pl.BlockSpec(memory_space=pl.ANY)] * amount,
        scratch_shapes=[pltpu.SemaphoreType.DMA(shape) for shape in sems],
        compiler_params=pltpu.CompilerParams(collective_id=collective, has_side_effects=True),
        name="gather_pieces",
    )(*pieces)


ROW_GROUP = 16
UPPER_CUTS = 3
SCATTER_LAG = 2


def scatter_kernel(pieces, amount, carried, *refs):
    grads, passing = refs[:amount], refs[amount : amount + carried]
    small = refs[amount + carried]
    refs = refs[amount + carried + 1 :]
    outs, twins = refs[:amount], refs[amount : 2 * amount]
    passed = refs[2 * amount : 2 * amount + carried]
    squares, small_out = refs[2 * amount + carried : 2 * amount + carried + 2]
    rest = refs[2 * amount + carried + 2 :]
    count = len(pieces)
    ranks = lax.axis_size("seq")
    own, beside, facing, from_left, from_right, ready = (
        rest[k * count : (k + 1) * count] for k in range(6)
    )
    load_sem, c_send, c_recv, y_send, y_recv, z_send, z_recv, x_send, x_recv = rest[
        6 * count : 6 * count + 9
    ]
    pass_send, pass_recv, parts, own_sum, totals, send_one, recv_one, send_two, recv_two = rest[
        6 * count + 9 :
    ]
    group, me = lax.axis_index("grp"), lax.axis_index("seq")
    z, y, core = place_of(me)
    z_size = GRID[0]
    across, sibling = (group, rank_of(z, 1 - y, core)), (group, rank_of(z, y, 1 - core))
    twin = (1 - group, me)
    left, right = (group, rank_of(z - 1, y, core)), (group, rank_of(z + 1, y, core))
    has_left, has_right = z > 0, z < z_size - 1
    barrier = pltpu.get_barrier_semaphore()
    pl.semaphore_signal(barrier, inc=1, device_id=twin, device_id_type=MESH)

    def greet(step, carry):
        there = (group, lax.rem(me + step, ranks))
        pl.semaphore_signal(barrier, inc=1, device_id=there, device_id_type=MESH)
        return carry

    lax.fori_loop(1, ranks, greet, 0)
    pl.semaphore_wait(barrier, ranks)
    squares[...] = jnp.zeros_like(squares)

    def part(piece, along, over, owner):
        which, row, rows, column, columns = pieces[piece]
        return grads[which].at[rank_of(along, over, owner), pl.ds(row, rows), pl.ds(column, columns)]

    def load(piece, along, over):
        slot = along * 2 + over
        return pltpu.make_async_copy(
            part(piece, along, over, core), own[piece].at[slot], load_sem.at[piece, slot]
        )

    def remote(src, dst, send, recv, there):
        return pltpu.make_async_remote_copy(
            src_ref=src, dst_ref=dst, send_sem=send, recv_sem=recv, device_id=there, device_id_type=MESH
        )

    def c_move(piece, along, over):
        slot = along * 2 + over
        return remote(
            part(piece, along, over, 1 - core),
            beside[piece].at[slot],
            c_send.at[piece, slot],
            c_recv.at[piece, slot],
            sibling,
        )

    def y_move(piece, along):
        return remote(
            own[piece].at[along * 2 + 1 - y],
            facing[piece].at[along],
            y_send.at[piece, along],
            y_recv.at[piece, along],
            across,
        )

    def z_move(piece, along, forward):
        side = 0 if forward else 1
        return remote(
            facing[piece].at[along],
            (from_left if forward else from_right)[piece].at[along],
            z_send.at[piece, along],
            z_recv.at[piece, along, side],
            right if forward else left,
        )

    def x_move(piece):
        which, row, height, column, columns = pieces[piece]
        return remote(
            ready[piece],
            twins[which].at[pl.ds(row, height), pl.ds(column, columns)],
            x_send.at[piece],
            x_recv.at[piece],
            twin,
        )

    def pass_move(k):
        return remote(passing[k], passed[k], pass_send.at[k], pass_recv.at[k], twin)

    def slice_move(step):
        peer = lax.rem(me + step, ranks)
        return remote(
            small.at[peer], parts.at[step], send_one.at[step], recv_one.at[step], (group, peer)
        )

    def total_move(step):
        peer = lax.rem(me + step, ranks)
        return remote(own_sum, totals.at[step], send_two.at[step], recv_two.at[step], (group, peer))

    def small_begin():
        def one(step, carry):
            slice_move(step).start()
            return carry

        lax.fori_loop(1, ranks, one, 0)
        own_sum[...] = small[me]

    def small_middle():
        def gather_in(step, carry):
            slice_move(step).wait()
            own_sum[...] += parts[step]
            return carry

        lax.fori_loop(1, ranks, gather_in, 0)

        def one(step, carry):
            total_move(step).start()
            return carry

        lax.fori_loop(1, ranks, one, 0)
        small_out[me] = own_sum[...]

    def small_end():
        def spread(step, carry):
            total_move(step).wait()
            small_out[lax.rem(me + ranks - step, ranks)] = totals[step]
            return carry

        lax.fori_loop(1, ranks, spread, 0)

    def each_along(distance, action):
        if distance == 0:
            action(z, None)
            return

        @pl.when(z - distance >= 0)
        def _():
            action(z - distance, False)

        @pl.when(z + distance < z_size)
        def _():
            action(z + distance, True)

    def by_rows(piece, body):
        def one(step, carry):
            body(pl.ds(pl.multiple_of(step * ROW_GROUP, ROW_GROUP), ROW_GROUP))
            return carry

        lax.fori_loop(0, pieces[piece][2] // ROW_GROUP, one, 0)

    def wide(ref, slot, rows):
        return ref[slot, rows, :].astype(jnp.float32)

    def begin(piece):
        for distance in reversed(range(z_size)):

            def one(along, _):
                for over in range(2):
                    load(piece, along, over).start()
                    c_move(piece, along, over).start()

            each_along(distance, one)

    def c_stage(piece, distance):
        def one(along, _):
            for turn in range(2):
                over = 1 - y if turn == 0 else y
                slot = along * 2 + over
                load(piece, along, over).wait()
                c_move(piece, along, over).wait_recv()

                def add(rows):
                    total = wide(own[piece], slot, rows) + wide(beside[piece], slot, rows)
                    own[piece][slot, rows, :] = total.astype(jnp.bfloat16)

                by_rows(piece, add)
                if turn == 0:
                    y_move(piece, along).start()

        each_along(distance, one)

    def y_stage(piece, distance):
        which, row, height, column, columns = pieces[piece]

        def one(along, forward):
            y_move(piece, along).wait_recv()
            slot = along * 2 + y
            if forward is None:

                def add(rows):
                    total = wide(own[piece], slot, rows) + wide(facing[piece], along, rows)
                    there = pl.ds(pl.multiple_of(row + rows.start, ROW_GROUP), ROW_GROUP)
                    outs[which][there, pl.ds(column, columns)] = total

                by_rows(piece, add)
                for side, present, source in ((True, has_left, from_left), (False, has_right, from_right)):

                    @pl.when(present)
                    def _():
                        z_move(piece, along, side).wait_recv()

                        def more(rows):
                            there = pl.ds(pl.multiple_of(row + rows.start, ROW_GROUP), ROW_GROUP)
                            outs[which][there, pl.ds(column, columns)] += wide(source[piece], along, rows)

                        by_rows(piece, more)

                def finish(rows):
                    there = pl.ds(pl.multiple_of(row + rows.start, ROW_GROUP), ROW_GROUP)
                    total = outs[which][there, pl.ds(column, columns)]
                    ready[piece][rows, :] = total.astype(jnp.bfloat16)
                    square = total[:SUBLANES] * total[:SUBLANES] + total[SUBLANES:] * total[SUBLANES:]
                    for k in range(columns // LANES):
                        squares[...] += square[:, k * LANES : (k + 1) * LANES]

                by_rows(piece, finish)
                x_move(piece).start()
                return
            source, present = (from_left, has_left) if forward else (from_right, has_right)

            @pl.when(present)
            def _():
                z_move(piece, along, forward).wait_recv()

                def add(rows):
                    total = wide(own[piece], slot, rows) + wide(facing[piece], along, rows)
                    total = total + wide(source[piece], along, rows)
                    facing[piece][along, rows, :] = total.astype(jnp.bfloat16)

                by_rows(piece, add)

            @pl.when(jnp.logical_not(present))
            def _():
                def add(rows):
                    total = wide(own[piece], slot, rows) + wide(facing[piece], along, rows)
                    facing[piece][along, rows, :] = total.astype(jnp.bfloat16)

                by_rows(piece, add)

            z_move(piece, along, forward).start()

        each_along(distance, one)

    def drain(piece, distance):
        def one(along, forward):
            for over in range(2):
                c_move(piece, along, over).wait_send()
            y_move(piece, along).wait_send()
            if forward is not None:
                z_move(piece, along, forward).wait_send()

        each_along(distance, one)

    slots = [(piece, distance) for piece in range(count) for distance in reversed(range(z_size))]
    begin(0)
    small_begin()
    for piece in range(1, min(2, count)):
        begin(piece)
    for k in range(carried):
        pass_move(k).start()
    for turn in range(len(slots) + SCATTER_LAG):
        if turn < len(slots):
            c_stage(*slots[turn])
            if turn == z_size:
                small_middle()
            piece, distance = slots[turn]
            if distance == 0 and piece + 2 < count:
                begin(piece + 2)
        if turn >= SCATTER_LAG:
            y_stage(*slots[turn - SCATTER_LAG])
    for slot in slots:
        drain(*slot)
    for piece in range(count):
        x_move(piece).wait()
    for k in range(carried):
        pass_move(k).wait()
    small_end()


def scatter_grads(grads, cuts, passing, values, collective):
    count = math.prod(GRID)
    grads = [grad.reshape(count, grad.shape[0] // count, grad.shape[1]) for grad in grads]
    pieces = []
    for which, cut in enumerate(cuts):
        rows, columns = grads[which].shape[1:]
        pieces += [(which, 0, rows, k * (columns // cut), columns // cut) for k in range(cut)]
    amount = len(pieces)
    places = math.prod(GRID[:2])

    def room(slots):
        return [pltpu.VMEM((slots, piece[2], piece[4]), jnp.bfloat16) for piece in pieces]

    sems = [
        (amount, places),
        (amount, places),
        (amount, places),
        (amount, GRID[0]),
        (amount, GRID[0]),
        (amount, GRID[0]),
        (amount, GRID[0], 2),
        (amount,),
        (amount,),
    ]
    small = in_slices(values, count)
    slot = small.shape[1:]
    carried = len(passing)
    sems += [(carried,)] * 2
    kinds = len(grads)
    *arrays, squares, total = pl.pallas_call(
        functools.partial(scatter_kernel, tuple(pieces), kinds, carried),
        out_shape=[jax.ShapeDtypeStruct(grad.shape[1:], jnp.float32) for grad in grads]
        + [jax.ShapeDtypeStruct(grad.shape[1:], jnp.bfloat16) for grad in grads]
        + [jax.ShapeDtypeStruct(part.shape, part.dtype) for part in passing]
        + [jax.ShapeDtypeStruct((SUBLANES, LANES), jnp.float32)]
        + [jax.ShapeDtypeStruct(small.shape, jnp.float32)],
        in_specs=[pl.BlockSpec(memory_space=pl.ANY)] * (kinds + carried)
        + [pl.BlockSpec(memory_space=pltpu.VMEM)],
        out_specs=[pl.BlockSpec(memory_space=pltpu.VMEM)] * kinds
        + [pl.BlockSpec(memory_space=pl.ANY)] * (kinds + carried)
        + [pl.BlockSpec(memory_space=pltpu.VMEM)] * 2,
        scratch_shapes=room(places)
        + room(places)
        + room(GRID[0])
        + room(GRID[0])
        + room(GRID[0])
        + [pltpu.VMEM((piece[2], piece[4]), jnp.bfloat16) for piece in pieces]
        + [pltpu.SemaphoreType.DMA(shape) for shape in sems]
        + [
            pltpu.VMEM(small.shape, jnp.float32),
            pltpu.VMEM(slot, jnp.float32),
            pltpu.VMEM(small.shape, jnp.float32),
        ]
        + [pltpu.SemaphoreType.DMA((count,))] * 4,
        compiler_params=pltpu.CompilerParams(
            collective_id=collective, has_side_effects=True, vmem_limit_bytes=VMEM_LIMIT
        ),
        name="scatter_grads",
    )(*grads, *passing, small)
    return (
        arrays[:kinds],
        arrays[kinds : 2 * kinds],
        arrays[2 * kinds :],
        jnp.sum(squares),
        carve(total.reshape(-1), [value.shape for value in values]),
    )


def lay_out_kernel(shards, view_ref, *outs):
    cut = D // shards * (4 * D + FF) // LANES
    for layer in range(L):
        upper, lower = outs[2 * layer : 2 * layer + 2]
        for ref, base in ((upper, 0), (lower, cut)):
            across = ref.shape[1] // LANES
            for row in range(0, ref.shape[0], ROW_GROUP):
                for column in range(across):
                    start = L * (base + row * across + column) + layer
                    rows = view_ref[pl.ds(start, ROW_GROUP, stride=L * across), :]
                    ref[row : row + ROW_GROUP, column * LANES : (column + 1) * LANES] = rows.astype(
                        jnp.bfloat16
                    )


def flat_view(array):
    layers, size = array.shape
    return array.reshape(layers, size // LANES, LANES).transpose(1, 0, 2).reshape(-1, LANES)


def unpack_kernel(size, x_ref, lead_ref, time_ref, text_ref, audio_ref, caption_ref, tail_ref, flat):
    count, rows = x_ref.shape[:2]
    lane = lax.broadcasted_iota(jnp.int32, (rows, LANES), 1)
    for rank in range(count):
        base, phase = divmod(rank * size, LANES)
        shard = x_ref[rank].astype(jnp.float32)
        if phase == 0:
            flat[base : base + rows, :] = shard
            continue
        turned = pltpu.roll(shard, phase, axis=1)
        pltpu.store(flat.at[pl.ds(base, rows), :], turned, mask=lane >= phase)
        pltpu.store(flat.at[pl.ds(base + 1, rows), :], turned, mask=lane < phase)
    start = lead_ref.shape[0]
    lead_ref[...] = flat[:start, :]
    for ref in (time_ref, text_ref, audio_ref, caption_ref):
        across = ref.shape[1] // LANES
        for row in range(0, ref.shape[0], ROW_GROUP):
            for column in range(across):
                ref[row : row + ROW_GROUP, column * LANES : (column + 1) * LANES] = flat[
                    pl.ds(start + row * across + column, ROW_GROUP, stride=across), :
                ].astype(jnp.bfloat16)
        start += ref.shape[0] * across
    tail_ref[...] = flat[start : start + tail_ref.shape[0], :]


def unpack_others(gathered, size, channels, text_width):
    count, rows, lanes = gathered.shape
    lead = 2 * channels * D // LANES
    shapes = [(D, D), (text_width, D), (D, E), (text_width, E)]
    tail = (2 * L + 1 + 1) * D // LANES
    whole = -(-count * size // LANES)
    outs = pl.pallas_call(
        functools.partial(unpack_kernel, size),
        out_shape=[jax.ShapeDtypeStruct((lead, LANES), jnp.float32)]
        + [jax.ShapeDtypeStruct(shape, jnp.bfloat16) for shape in shapes]
        + [jax.ShapeDtypeStruct((tail, LANES), jnp.float32)],
        in_specs=[pl.BlockSpec(memory_space=pltpu.VMEM)],
        out_specs=[pl.BlockSpec(memory_space=pltpu.VMEM)] * 6,
        scratch_shapes=[pltpu.VMEM((whole + 2 * rows, LANES), jnp.float32)],
        compiler_params=pltpu.CompilerParams(vmem_limit_bytes=VMEM_LIMIT),
        name="unpack_others",
    )(gathered)
    w_in, w_out = outs[0].reshape(2, channels * D)
    tail_rows = outs[5].reshape(-1, D)
    return (
        w_in.reshape(channels, D).astype(jnp.bfloat16),
        w_out.reshape(D, channels).astype(jnp.bfloat16),
        *outs[1:5],
        tail_rows[:-1],
        tail_rows[-1],
    )


def lay_out(anchor, shards):
    if shards != math.prod(GRID):
        return [layer_rows(anchor[depth].astype(jnp.bfloat16), shards) for depth in range(L)]
    shapes = [(D // shards, 4 * D + FF), (FF // shards, D)] * L
    outs = pl.pallas_call(
        functools.partial(lay_out_kernel, shards),
        out_shape=[jax.ShapeDtypeStruct(shape, jnp.bfloat16) for shape in shapes],
        in_specs=[pl.BlockSpec(memory_space=pltpu.VMEM)],
        out_specs=[pl.BlockSpec(memory_space=pltpu.VMEM)] * len(shapes),
        compiler_params=pltpu.CompilerParams(vmem_limit_bytes=VMEM_LIMIT),
        name="lay_out",
    )(flat_view(anchor))
    return [(outs[2 * depth], outs[2 * depth + 1]) for depth in range(L)]


def flatten(parts):
    return jnp.concatenate([part.reshape(-1) for part in parts])


def group_mean(delta, count):
    low = lax.reduce_precision(delta, 8, 7)
    total = low
    for step in range(1, count):
        moves = [(source, (source + step) % count) for source in range(count)]
        total = total + lax.ppermute(low.astype(jnp.bfloat16), "grp", moves).astype(jnp.float32)
    return total / count


STEP_BLOCKS = 6


def delta_of(grad, first, second, anchor):
    return adam(grad, first, second, anchor)[2]


def step_kernel(cut, places, factors, *refs):
    amount = len(places)
    own, twin = refs[:amount], refs[amount : 2 * amount]
    anchor, first, second, outer, twin_first, twin_second = refs[2 * amount : 2 * amount + 6]
    new, one, two, mean_out, momentum_out, own_flat, twin_flat = refs[2 * amount + 6 :]
    step = pl.program_id(0)
    block = anchor.shape[0]

    @pl.when(step == 0)
    def _():
        for grads, flat in ((own, own_flat), (twin, twin_flat)):
            for ref, (layer, first_column) in zip(grads, places):
                base, width = (cut, ref.shape[1]) if first_column is None else (0, 4 * D + FF)
                across, skip = width // LANES, (first_column or 0) // LANES
                for row in range(0, ref.shape[0], ROW_GROUP):
                    for column in range(ref.shape[1] // LANES):
                        start = L * (base + row * across + skip + column) + layer
                        flat[pl.ds(start, ROW_GROUP, stride=L * across), :] = ref[
                            row : row + ROW_GROUP, column * LANES : (column + 1) * LANES
                        ].astype(jnp.float32)

    rows = pl.ds(pl.multiple_of(step * block, SUBLANES), block)
    grad, weight = own_flat[rows, :], anchor[...]
    first_own, second_own = first[...], second[...]
    clipped = grad * factors[0]
    one[...] = beta_one * first_own + (1.0 - beta_one) * clipped
    two[...] = beta_two * second_own + (1.0 - beta_two) * clipped * clipped
    rounded = grad.astype(jnp.bfloat16).astype(jnp.float32)
    delta_own = delta_of(rounded * factors[0], first_own, second_own, weight)
    delta_twin = delta_of(twin_flat[rows, :] * factors[1], twin_first[...], twin_second[...], weight)
    mean = (delta_own + delta_twin) * 0.5
    momentum = outer_mu * outer[...] + mean
    mean_out[...] = mean
    momentum_out[...] = momentum
    new[...] = weight - outer_rate * (mean + outer_mu * momentum)


def step_layers(factors, own, twin, views, shards):
    rows = views[0].shape[0]
    places = tuple((layer, column) for _, layer, column in own)
    own = [grad for grad, _, _ in own]
    block = rows // STEP_BLOCKS
    whole = pl.BlockSpec(memory_space=pltpu.VMEM)
    part = pl.BlockSpec((block, LANES), lambda k: (k, 0))
    return pl.pallas_call(
        functools.partial(step_kernel, D // shards * (4 * D + FF) // LANES, places),
        grid=(STEP_BLOCKS,),
        out_shape=[jax.ShapeDtypeStruct((rows, LANES), jnp.float32)] * 5,
        in_specs=[pl.BlockSpec(memory_space=pltpu.SMEM)] + [whole] * (2 * len(own)) + [part] * 6,
        out_specs=[part] * 5,
        scratch_shapes=[pltpu.VMEM((rows, LANES), jnp.float32)] * 2,
        compiler_params=pltpu.CompilerParams(
            vmem_limit_bytes=VMEM_LIMIT, dimension_semantics=("arbitrary",)
        ),
        name="step_layers",
    )(factors, *own, *twin, *views)


def from_view(view):
    rows, lanes = view.shape
    return view.reshape(rows // L, L, lanes).transpose(1, 0, 2).reshape(L, rows // L * lanes)


def swapped(value):
    return lax.ppermute(value, "grp", [(0, 1), (1, 0)])


def per_device(
    anchor_layers,
    anchor_other,
    first_layers,
    first_other,
    second_layers,
    second_other,
    outer_layers,
    outer_other,
    latents,
    noise,
    lengths,
    timesteps,
    null_flags,
    captions,
):
    seq_count = lax.axis_size("seq")
    group_count = lax.axis_size("grp")
    rank = lax.axis_index("seq")
    group = lax.axis_index("grp")
    close = seq_count == math.prod(GRID) and group_count == 2
    rows = latents.shape[0]
    channels = latents.shape[1]
    frames_group = rows * seq_count
    lengths = lengths[0]
    timesteps = timesteps[0]
    null_flags = null_flags[0]
    captions = captions[0]
    item_count = lengths.shape[0]
    text_width = captions.shape[1]
    other_size = anchor_other.shape[0]
    padded = -(-other_size // 4096) * 4096
    other_rows = jnp.pad(anchor_other.astype(jnp.bfloat16), (0, padded - other_size))
    own_rows = lay_out(anchor_layers, seq_count)
    early = L
    own_block = block_of(rank, close)
    frames = jnp.concatenate([latents, noise], axis=1).T
    pieces = [frames, other_rows.reshape(-1, LANES)]
    pieces += [part for pair in own_rows[:early] for part in pair]
    gathered_frames, other_rows, *early_rows = gather_pieces(
        pieces, [False, True] + [True, False] * early, 4
    )
    if close:
        first_view, second_view = flat_view(first_layers[0]), flat_view(second_layers[0])
        (*sources, first_other, second_other), other_rows = lax.optimization_barrier(
            ((first_view, second_view, first_other, second_other), other_rows)
        )
        twin_views = [swapped(value) for value in sources]
        twin_moments = [swapped(value)[0] for value in (first_other, second_other)]
    late_rows = [lax.all_gather(part, "seq", axis=0) for pair in own_rows[early:] for part in pair]
    layer_parts = [part.reshape(-1, part.shape[-1]) for part in early_rows + late_rows]
    gathered = [split_upper(*layer_parts[2 * depth : 2 * depth + 2]) for depth in range(L)]
    if close:
        other_parts = unpack_others(other_rows, other_size, channels, text_width)
    else:
        other_low = other_rows.reshape(seq_count, padded)[:, :other_size].reshape(-1)
        other_parts = carve(other_low, other_shapes(channels, D, text_width, E, L))
    w_in, w_out, w_time, w_text, w_audio, w_caption, gains, null_text = other_parts
    w_time_f = w_time.astype(jnp.float32)
    w_text_f = w_text.astype(jnp.float32)
    w_audio_f = w_audio.astype(jnp.float32)
    w_caption_f = w_caption.astype(jnp.float32)
    gains_f = gains.astype(jnp.float32)
    null_f = null_text.astype(jnp.float32)
    places = own_block * rows + jnp.arange(rows, dtype=jnp.int32)
    order = jnp.arange(item_count, dtype=jnp.int32)
    ends = jnp.sum(jnp.where(order[None, :] <= order[:, None], lengths[None, :], 0), axis=1)
    item = jnp.sum((places[:, None] >= ends[None, :]).astype(jnp.int32), axis=1)
    key_places = own_block * rows + jnp.arange(-2 * rows, 3 * rows, dtype=jnp.int32)
    key_item = jnp.sum((key_places[:, None] >= ends[None, :]).astype(jnp.int32), axis=1)
    key_item = jnp.where((key_places >= 0) & (key_places < frames_group), key_item, -1)
    items = (item, key_item)
    window_hot = (key_item[:, None] == jnp.arange(item_count, dtype=jnp.int32)[None, :]).astype(
        jnp.float32
    )
    inner = slice(2 * rows, 3 * rows)
    onehot = window_hot[inner]
    lengths_f = lengths[:, None].astype(jnp.float32)
    alpha_bar = plan(timesteps)
    mixing = exact(window_hot, jnp.stack([jnp.sqrt(alpha_bar), jnp.sqrt(1.0 - alpha_bar)], axis=1))
    near = frame_window(frames, gathered_frames, own_block, close).T
    noise = near[inner, channels:]
    noisy_low = (mixing[:, 0:1] * near[:, :channels] + mixing[:, 1:2] * near[:, channels:]).astype(
        jnp.bfloat16
    )
    features = time_features(timesteps)

    text = jnp.where(null_flags[:, None] == 1, null_f[None, :], captions)
    before_silu = exact(features, w_time_f) + exact(text, w_text_f)
    condition, pull_silu = jax.vjp(jax.nn.silu, before_silu)
    hidden_window = dense(noisy_low, w_in) + exact(window_hot, condition)
    saved_all = []
    entering = []
    for depth in range(L):
        weights = gathered[depth]
        proj_qkv = weights[0]
        if depth == 0:
            normed_window = norm_rows(hidden_window, gains_f[0]).astype(jnp.bfloat16)
            hidden, normed = hidden_window[inner], normed_window[inner]
            queries = dense(normed, proj_qkv[:, :D]).astype(jnp.bfloat16)
            window = dense(normed_window, proj_qkv[:, D:]).astype(jnp.bfloat16)
        else:
            normed = norm_rows(hidden, gains_f[2 * depth]).astype(jnp.bfloat16)
            window = gather_window(dense(normed, proj_qkv[:, D:]).astype(jnp.bfloat16), close)
            queries = dense(normed, proj_qkv[:, :D]).astype(jnp.bfloat16)
        entering.append(hidden)
        hidden, saved = layer_forward(
            hidden, normed, queries, window, weights, gains_f[2 * depth + 1], items
        )
        saved_all.append(saved)
    final = norm_rows(hidden, gains_f[2 * L])
    final_low = final.astype(jnp.bfloat16)
    predicted = dense(final_low, w_out)
    error = predicted - noise
    part_pool = contract_rows(onehot, final, HIGH)
    squared_sum, pool_sum = sum_over_seq((jnp.sum(error * error), part_pool), 1)
    pooled = pool_sum / lengths_f
    audio_side = exact(pooled, w_audio_f)
    text_side = exact(captions, w_caption_f)
    clash, pull_clash = jax.vjp(contrast, audio_side, text_side)
    loss = squared_sum / (frames_group * channels) + contrast_weight * clash
    grad_audio_side, grad_text_side = pull_clash(jnp.float32(contrast_weight))
    grad_pred = (2.0 / (frames_group * channels) * error).astype(jnp.bfloat16)
    grad_w_out = contract_rows(final_low, grad_pred).reshape(channels, D)
    grad_pooled = against_rows(grad_audio_side, w_audio_f, HIGH) / lengths_f
    grad_final = against_rows(grad_pred, w_out) + exact(onehot, grad_pooled)
    unused, pull_final = jax.vjp(norm_rows, hidden, gains_f[2 * L])
    grad_hidden, grad_gain_final = pull_final(grad_final)
    layer_grads = [None] * L
    sent_early = [None] * L
    gain_grads = [None] * (2 * L + 1)
    gain_grads[2 * L] = grad_gain_final
    for depth in reversed(range(L)):
        weights = gathered[depth]
        proj_qkv = weights[0]
        early = depth > 0 and close
        grad_middle, grad_query, grad_pairs, rest, lower_full, gain_grads[2 * depth + 1] = layer_backward(
            grad_hidden, weights, gains_f[2 * depth + 1], items, saved_all[depth], early
        )
        if early:
            sent_early[depth] = [
                lax.psum_scatter(grad, "seq", scatter_dimension=0, tiled=True)
                for grad in (lower_full, rest)
            ]
        normed = saved_all[depth][0]
        if depth == 0:
            qkv_parts = [(normed, grad_query), (normed_window, grad_pairs)]
            grad_normed = against_rows(grad_pairs, proj_qkv[:, D:])
            grad_own = grad_normed[inner] + against_rows(grad_query, proj_qkv[:, :D])
            grad_normed = jnp.concatenate(
                [grad_normed[: 2 * rows], grad_own, grad_normed[3 * rows :]], axis=0
            )
            unused, pull_one = jax.vjp(norm_rows, hidden_window, gains_f[0])
        else:
            grad_pairs = return_window(grad_pairs, rows, close).astype(jnp.bfloat16)
            grad_projected = jnp.concatenate([grad_query, grad_pairs], axis=1)
            qkv_parts = [(normed, grad_projected)]
            grad_normed = against_rows(grad_projected, proj_qkv)
            unused, pull_one = jax.vjp(norm_rows, entering[depth], gains_f[2 * depth])
        grad_input, gain_grads[2 * depth] = pull_one(grad_normed)
        if early:
            layer_grads[depth] = [side_by_side(qkv_parts)]
        else:
            layer_grads[depth] = [side_by_side(qkv_parts + rest), lower_full]
        if depth > 0:
            grad_hidden = grad_middle + grad_input
        else:
            grad_hidden = jnp.concatenate(
                [grad_input[: 2 * rows], grad_input[inner] + grad_middle, grad_input[3 * rows :]], axis=0
            )
    grad_w_in = contract_rows(noisy_low.astype(jnp.float32), grad_hidden, HIGH)
    grad_condition = contract_rows(window_hot, grad_hidden, HIGH)
    lead = 2 * channels
    features_at, text_at = lead, lead + D
    audio_at = text_at + text_width
    caption_at = audio_at + D * E // D
    gains_at = caption_at + text_width * E // D
    own_rows_count = -(-other_size // D) + 1
    own_start = rank * other_size
    own_row = own_start // D
    own_at = own_row + jnp.arange(own_rows_count, dtype=jnp.int32)

    def own_part(value, start):
        reach = gains_at + 2 * own_rows_count
        value = jnp.pad(value, ((0, 0), (start, reach - start - value.shape[1])))
        return lax.dynamic_slice_in_dim(value, own_row, own_rows_count, axis=1)

    def own_rows_at(start, amount):
        there = start + jnp.arange(amount, dtype=jnp.int32)
        return (there[:, None] == own_at[None, :]).astype(jnp.float32)

    left_condition = own_part(features, features_at) + own_part(text, text_at)
    early_view = thirds(pooled, grad_audio_side, own_at - audio_at)
    early_view = early_view + thirds(captions, grad_text_side, own_at - caption_at)
    left_small = jnp.concatenate(
        [
            own_rows_at(0, lead),
            left_condition,
            own_rows_at(gains_at, 2 * L + 1),
        ],
        axis=0,
    )
    silu_slope = pull_silu(jnp.ones_like(condition))[0]
    slopes = jnp.pad(silu_slope, ((lead, 2 * L + 1), (0, 0)), constant_values=1.0)
    left_null = own_rows_at(gains_at + 2 * L + 1, 1)
    early_view, left_small, slopes, left_null, layer_grads[0] = lax.optimization_barrier(
        (early_view, left_small, slopes, left_null, layer_grads[0])
    )
    small_grads = (jnp.concatenate([grad_w_in, grad_w_out, grad_condition, jnp.stack(gain_grads)]),)
    if close:
        sent = sent_early[1:]
        late = [layer_grads[depth][0] for depth in range(1, L)] + list(layer_grads[0])
        own_late, twin_late, passed, square_part, small_grads = scatter_grads(
            late,
            [1] * (L - 1) + [UPPER_CUTS, 1],
            [part for parts in sent for part in parts],
            small_grads,
            5,
        )
        own_parts = [(own_late[L - 1], 0, 0), (own_late[L], 0, None)]
        twin_parts = [twin_late[L - 1], twin_late[L]]
        for depth in range(1, L):
            lower, rest = sent[depth - 1]
            own_parts += [(own_late[depth - 1], depth, 0), (rest, depth, 3 * D), (lower, depth, None)]
            twin_parts += [twin_late[depth - 1], passed[2 * depth - 1], passed[2 * depth - 2]]
    else:
        small_grads = lax.psum(small_grads, "seq")
    weighted = small_grads[0] * slopes
    grad_before = weighted[lead : lead + item_count]
    flagged = jnp.sum(jnp.where(null_flags[:, None] == 1, grad_before, 0.0), axis=0, keepdims=True)
    grad_null = against_rows(flagged, w_text_f, HIGH)
    own_view = early_view + contract_rows(left_small, weighted, HIGH) + left_null.T * grad_null
    other_grad = lax.dynamic_slice_in_dim(own_view.reshape(-1), own_start % D, other_size)
    other_grad_square = jnp.sum(other_grad * other_grad)
    if close:
        other_grad_low = other_grad.astype(jnp.bfloat16)
        twin_other = swapped(other_grad_low).astype(jnp.float32)
        square_part = square_part + other_grad_square
        for parts in sent:
            for grad in parts:
                wide = grad.astype(jnp.float32)
                square_part = square_part + jnp.sum(wide * wide)
        norms = jnp.sqrt(sums_by_group(square_part, 3))
        total_norm = lax.dynamic_index_in_dim(norms, group, keepdims=False)
        twin_norm = lax.dynamic_index_in_dim(norms, 1 - group, keepdims=False)
        factor = jnp.minimum(1.0, clip_at / (total_norm + 1e-06))
        twin_factor = jnp.minimum(1.0, clip_at / (twin_norm + 1e-06))
        views = [flat_view(anchor_layers), first_view, second_view, flat_view(outer_layers)]
        stepped = step_layers(
            jnp.stack([factor, twin_factor]),
            own_parts,
            twin_parts,
            views + twin_views,
            seq_count,
        )
        new_layers, first_l, second_l, mean_layers, momentum_layers = map(from_view, stepped)
        first_o, second_o, _ = adam(other_grad * factor, first_other[0], second_other[0], anchor_other)
        rounded = lax.reduce_precision(other_grad, 8, 7)
        delta_o = delta_of(rounded * factor, first_other[0], second_other[0], anchor_other)
        delta_twin = delta_of(twin_other * twin_factor, *twin_moments, anchor_other)
        mean_other = (delta_o + delta_twin) / 2
    else:
        stacked = jnp.stack(
            [
                flatten(
                    lax.psum_scatter(grad, "seq", scatter_dimension=0, tiled=True).astype(jnp.float32)
                    for grad in grads
                )
                for grads in layer_grads
            ]
        )
        total_norm = jnp.sqrt(lax.psum(jnp.sum(stacked * stacked) + other_grad_square, "seq"))
        factor = jnp.minimum(1.0, clip_at / (total_norm + 1e-06))
        first_l, second_l, delta_l = adam(
            stacked * factor, first_layers[0], second_layers[0], anchor_layers
        )
        first_o, second_o, delta_o = adam(
            other_grad * factor, first_other[0], second_other[0], anchor_other
        )
        mean_layers = group_mean(delta_l, group_count)
        mean_other = group_mean(delta_o, group_count)
        momentum_layers = outer_mu * outer_layers + mean_layers
        new_layers = anchor_layers - outer_rate * (mean_layers + outer_mu * momentum_layers)
    momentum_other = outer_mu * outer_other + mean_other
    new_other = anchor_other - outer_rate * (mean_other + outer_mu * momentum_other)
    return (
        new_layers,
        new_other,
        first_l[None],
        first_o[None],
        second_l[None],
        second_o[None],
        mean_layers,
        mean_other,
        momentum_layers,
        momentum_other,
        loss.reshape(1),
        total_norm.reshape(1),
    )


def solution(mesh):
    placed = (
        P(None, "seq"),
        P("seq"),
        P("grp", None, "seq"),
        P("grp", "seq"),
        P("grp", None, "seq"),
        P("grp", "seq"),
        P(None, "seq"),
        P("seq"),
        P(("grp", "seq"), None),
        P(("grp", "seq"), None),
        P("grp", None),
        P("grp", None),
        P("grp", None),
        P("grp", None, None),
    )
    return jax.shard_map(
        per_device,
        mesh=mesh,
        in_specs=placed,
        out_specs=(
            P(None, "seq"),
            P("seq"),
            P("grp", None, "seq"),
            P("grp", "seq"),
            P("grp", None, "seq"),
            P("grp", "seq"),
            P(None, "seq"),
            P("seq"),
            P(None, "seq"),
            P("seq"),
            P("grp"),
            P("grp"),
        ),
        check_vma=False,
    )
```

```python
import functools
import math

import jax
import jax.numpy as jnp
from jax import lax
from jax.experimental import pallas as pl
from jax.experimental.pallas import tpu as pltpu
from jax.sharding import PartitionSpec as P

D = 768
HEADS = 12
HD = 64
FF = 3072
E = 512
L = 2
TSTEPS = 1000
STEP_COUNT = 10


HIGH = lax.Precision.HIGHEST
beta_one = 0.9
beta_two = 0.95
adam_eps = 1e-08
decay_rate = 0.01
inner_rate = 0.02
outer_rate = 0.7
outer_mu = 0.9
clip_at = 0.01
logit_scale = 30.0
contrast_weight = 0.05


def block_of(rank, close):
    if not close:
        return rank
    turn = (rank // 4) % 2
    return rank + 2 * turn * (1 - 2 * ((rank // 2) % 2))


def passed_along(value, axis, steps, close):
    count = lax.axis_size(axis)
    holder = {block_of(rank, close): rank for rank in range(count)}
    initial, last = (max(0, -steps), min(count, count - steps))
    return lax.ppermute(
        value, axis, [(holder[source], holder[source + steps]) for source in range(initial, last)]
    )


def dense(left, right):
    return jnp.dot(left, right, preferred_element_type=jnp.float32)


def exact(left, right):
    return jnp.dot(left, right, precision=HIGH, preferred_element_type=jnp.float32)


def contract_rows(left, right, precision=None):
    return lax.dot_general(
        left,
        right,
        (((0,), (0,)), ((), ())),
        precision=precision,
        preferred_element_type=jnp.float32,
    )


def against_rows(left, right, precision=None):
    return lax.dot_general(
        left,
        right,
        (((1,), (1,)), ((), ())),
        precision=precision,
        preferred_element_type=jnp.float32,
    )


def carve(flat, shapes):
    pieces = []
    start = 0
    for shape in shapes:
        count = math.prod(shape)
        pieces.append(flat[start : start + count].reshape(shape))
        start += count
    return pieces


def layer_rows(piece, shards):
    cut = D // shards * (4 * D + FF)
    return piece[:cut].reshape(D // shards, 4 * D + FF), piece[cut:].reshape(FF // shards, D)


def split_upper(upper, lower):
    return [upper[:, : 3 * D], upper[:, 3 * D : 4 * D], upper[:, 4 * D :], lower]


def other_shapes(channels, width, text_width, joint_width, blocks):
    return [
        (channels, width),
        (width, channels),
        (width, width),
        (text_width, width),
        (width, joint_width),
        (text_width, joint_width),
        (2 * blocks + 1, width),
        (text_width,),
    ]


def norm_rows(hidden, gain):
    centred = hidden - jnp.mean(hidden, axis=-1, keepdims=True)
    return centred * lax.rsqrt(jnp.mean(centred * centred, axis=-1, keepdims=True) + 1e-05) * gain


def plan(steps):
    angle = (steps.astype(jnp.float32) / TSTEPS + 0.008) / 1.008 * (math.pi / 2)
    return jnp.cos(angle) ** 2


def time_features(steps):
    half = D // 2
    frequency = jnp.exp(-math.log(10000.0) * jnp.arange(half, dtype=jnp.float32) / half)
    angle = steps.astype(jnp.float32)[:, None] * frequency[None, :]
    return jnp.concatenate([jnp.cos(angle), jnp.sin(angle)], axis=1)


def contrast(audio_side, text_side):
    audio_unit = audio_side * lax.rsqrt(
        jnp.sum(audio_side * audio_side, axis=-1, keepdims=True) + 1e-06
    )
    text_unit = text_side * lax.rsqrt(
        jnp.sum(text_side * text_side, axis=-1, keepdims=True) + 1e-06
    )
    logits = logit_scale * jnp.dot(audio_unit, text_unit.T, precision=HIGH)
    diagonal = logit_scale * jnp.sum(audio_unit * text_unit, axis=-1)
    row_terms = jax.nn.logsumexp(logits, axis=1) - diagonal
    column_terms = jax.nn.logsumexp(logits, axis=0) - diagonal
    return 0.5 * (jnp.mean(row_terms) + jnp.mean(column_terms))


def gather_window(local_pairs, close):
    pieces = {}
    for step in (2, 1, -1, -2):
        pieces[step] = passed_along(local_pairs, "seq", step, close)
    return [jnp.concatenate([pieces[2], pieces[1], local_pairs, pieces[-1], pieces[-2]], axis=0)]


def return_window(grad_window, close):
    total = grad_window[2].astype(jnp.float32)
    for slot, step in ((0, 2), (1, 1), (3, -1), (4, -2)):
        total = total + passed_along(grad_window[slot], "seq", -step, close).astype(jnp.float32)
    return total


LANES = 128
LOG2E = math.log2(math.e)
PAIRS = HEADS * HD // LANES
VMEM_LIMIT = 50 * 1024 * 1024


def lane_masks(dtype):
    lane = lax.broadcasted_iota(jnp.int32, (1, LANES), 1)
    return [(lane < HD).astype(dtype), (lane >= HD).astype(dtype)]


def fill_bias(bias_ref, query_item_ref, key_item_ref):
    keep = key_item_ref[...] == query_item_ref[...]
    bias_ref[...] = jnp.where(keep, 0.0, -1e30).astype(jnp.float32)


def joined(refs, cols):
    if len(refs) == 1:
        return refs[0][:, cols]
    return jnp.concatenate([ref[:, cols] for ref in refs], axis=0)


def attend_forward_kernel(parts, q_ref, *refs):
    kv_refs = refs[:parts]
    query_item_ref, key_item_ref, o_ref, lse_ref, bias_ref = refs[parts:]
    fill_bias(bias_ref, query_item_ref, key_item_ref)
    width = HEADS * HD
    masks = lane_masks(jnp.bfloat16)
    lse_ref[...] = jnp.zeros_like(lse_ref)
    for pair in range(PAIRS):
        cols = slice(pair * LANES, (pair + 1) * LANES)
        query = q_ref[:, cols] * jnp.bfloat16(HD ** (-0.5))
        key_rows = joined(kv_refs, cols)
        value_rows = joined(kv_refs, slice(width + pair * LANES, width + (pair + 1) * LANES))
        halves = []
        for half in range(2):
            scores = against_rows(key_rows, query * masks[half]) * LOG2E + bias_ref[...]
            peak = jnp.max(scores, axis=0, keepdims=True)
            weights = jnp.exp2(scores - peak)
            total = jnp.sum(weights, axis=0, keepdims=True)
            mixed = contract_rows(value_rows, weights.astype(jnp.bfloat16)) * (1.0 / total)
            halves.append(mixed[half * HD : (half + 1) * HD])
            lse_ref[2 * pair + half : 2 * pair + half + 1, :] = peak + jnp.log2(total)
        o_ref[:, cols] = jnp.concatenate(halves, axis=0).T.astype(o_ref.dtype)


def attend_forward(queries, window, query_item, key_item):
    rows, width = queries.shape
    parts, span = len(window), sum(piece.shape[0] for piece in window)
    return pl.pallas_call(
        functools.partial(attend_forward_kernel, parts),
        out_shape=(
            jax.ShapeDtypeStruct((rows, width), jnp.bfloat16),
            jax.ShapeDtypeStruct((16, rows), jnp.float32),
        ),
        in_specs=[pl.BlockSpec(memory_space=pltpu.VMEM)] * (3 + parts),
        out_specs=(pl.BlockSpec(memory_space=pltpu.VMEM),) * 2,
        scratch_shapes=[pltpu.VMEM((span, rows), jnp.float32)],
        compiler_params=pltpu.CompilerParams(vmem_limit_bytes=VMEM_LIMIT),
        cost_estimate=pl.CostEstimate(
            flops=4 * rows * span * width,
            transcendentals=rows * span * HEADS,
            bytes_accessed=4 * rows * width + 4 * span * width,
        ),
        name="attend_forward",
    )(queries, *window, query_item[None, :], key_item[:, None])


def attend_backward_kernel(parts, splits, q_ref, *refs):
    kv_refs = refs[:parts]
    do_ref, lse_ref, query_item_ref, key_item_ref, dq_ref = refs[parts : parts + 5]
    dkv_refs, bias_ref = refs[parts + 5 : parts + 5 + splits], refs[parts + 5 + splits]
    fill_bias(bias_ref, query_item_ref, key_item_ref)
    width = HEADS * HD
    masks = lane_masks(jnp.bfloat16)
    for pair in range(PAIRS):
        cols = slice(pair * LANES, (pair + 1) * LANES)
        value_cols = slice(width + pair * LANES, width + (pair + 1) * LANES)
        query = q_ref[:, cols] * jnp.bfloat16(HD ** (-0.5))
        key_rows = joined(kv_refs, cols)
        value_rows = joined(kv_refs, value_cols)
        grad_out = do_ref[:, cols]
        halves = []
        grad_key = grad_value = None
        for half in range(2):
            query_half = query * masks[half]
            grad_half = grad_out * masks[half]
            scores = against_rows(key_rows, query_half) * LOG2E + bias_ref[...]
            shares = jnp.exp2(scores - lse_ref[2 * pair + half : 2 * pair + half + 1, :])
            grad_shares = against_rows(value_rows, grad_half)
            inner = jnp.sum(grad_shares * shares, axis=0, keepdims=True)
            grad_scores = (shares * (grad_shares - inner)).astype(jnp.bfloat16)
            one_value = dense(shares.astype(jnp.bfloat16), grad_half)
            one_key = dense(grad_scores, query_half)
            grad_value = one_value if grad_value is None else grad_value + one_value
            grad_key = one_key if grad_key is None else grad_key + one_key
            one_query = contract_rows(key_rows, grad_scores)
            halves.append(one_query[half * HD : (half + 1) * HD])
        grad_query = jnp.concatenate(halves, axis=0).T * HD ** (-0.5)
        dq_ref[:, cols] = grad_query.astype(dq_ref.dtype)
        start = 0
        for dkv_ref in dkv_refs:
            there = slice(start, start + dkv_ref.shape[0])
            dkv_ref[:, cols] = grad_key[there].astype(dkv_ref.dtype)
            dkv_ref[:, value_cols] = grad_value[there].astype(dkv_ref.dtype)
            start += dkv_ref.shape[0]


def attend_backward(queries, window, grad_out, lse, query_item, key_item, splits):
    rows, width = queries.shape
    parts, span = len(window), sum(piece.shape[0] for piece in window)
    grad_query, *grad_window = pl.pallas_call(
        functools.partial(attend_backward_kernel, parts, splits),
        out_shape=[jax.ShapeDtypeStruct((rows, width), jnp.bfloat16)]
        + [jax.ShapeDtypeStruct((span // splits, 2 * width), jnp.bfloat16)] * splits,
        in_specs=[pl.BlockSpec(memory_space=pltpu.VMEM)] * (5 + parts),
        out_specs=[pl.BlockSpec(memory_space=pltpu.VMEM)] * (1 + splits),
        scratch_shapes=[pltpu.VMEM((span, rows), jnp.float32)],
        compiler_params=pltpu.CompilerParams(vmem_limit_bytes=VMEM_LIMIT),
        cost_estimate=pl.CostEstimate(
            flops=10 * rows * span * width,
            transcendentals=rows * span * HEADS,
            bytes_accessed=8 * rows * width + 8 * span * width,
        ),
        name="attend_backward",
    )(queries, *window, grad_out, lse, query_item[None, :], key_item[:, None])
    return grad_query, grad_window


def layer_forward(hidden, normed, queries, window, weights, gain_two, items):
    proj_qkv, proj_out, proj_up, proj_down = weights
    attended, lse = attend_forward(queries, window, *items)
    middle = hidden + dense(attended, proj_out)
    second = norm_rows(middle, gain_two).astype(jnp.bfloat16)
    upper = dense(second, proj_up)
    activated = jax.nn.gelu(upper, approximate=True).astype(jnp.bfloat16)
    return (
        middle + dense(activated, proj_down),
        (normed, queries, window, lse, attended, middle, second, upper, activated),
    )


def layer_backward(grad_hidden, weights, gain_two, items, saved, early, splits):
    normed, queries, window, lse, attended, middle, second, upper, activated = saved
    proj_qkv, proj_out, proj_up, proj_down = weights
    branch_top = grad_hidden.astype(jnp.bfloat16)
    grad_activated = against_rows(branch_top, proj_down)
    unused, pull_gelu = jax.vjp(lambda value: jax.nn.gelu(value, approximate=True), upper)
    grad_upper = pull_gelu(grad_activated)[0].astype(jnp.bfloat16)
    grad_second = against_rows(grad_upper, proj_up)
    unused, pull_two = jax.vjp(norm_rows, middle, gain_two)
    grad_middle, grad_gain_two = pull_two(grad_second)
    grad_middle = grad_middle + grad_hidden
    branch_mid = grad_middle.astype(jnp.bfloat16)
    grad_attended = against_rows(branch_mid, proj_out).astype(jnp.bfloat16)
    lower_full = contract_rows(activated, branch_top).astype(jnp.bfloat16)
    pairs = [(attended, branch_mid), (second, grad_upper)]
    if early:
        grad_attended, rest_full = lax.optimization_barrier((grad_attended, side_by_side(pairs)))
    grad_query, grad_window = attend_backward(queries, window, grad_attended, lse, *items, splits)
    return grad_middle, grad_query, grad_window, (rest_full if early else pairs), lower_full, grad_gain_two


def side_by_side(pairs):
    return jnp.concatenate(
        [contract_rows(left, right).astype(jnp.bfloat16) for left, right in pairs], axis=1
    )


def frame_window(frames, gathered_frames, own_block, close):
    if close:
        count = gathered_frames.shape[0]
        parts = [
            lax.dynamic_index_in_dim(
                gathered_frames, jnp.clip(own_block + step, 0, count - 1), keepdims=False
            )
            for step in range(-2, 3)
        ]
    else:
        parts = [passed_along(frames, "seq", -step, close) for step in range(-2, 0)] + [frames]
        parts += [passed_along(frames, "seq", -step, close) for step in range(1, 3)]
    return jnp.concatenate(parts, axis=1)


def thirds_left(value, joint, at):
    inside = (at >= 0) & (at < value.shape[1] * joint // D)
    matrix_row, odd = at // 2 * 3, at % 2
    wanted = jnp.stack(
        [
            jnp.where(inside & (odd == parity), matrix_row + offset, -1)
            for parity, offset in ((0, 0), (0, 1), (1, 1), (1, 2))
        ]
    )
    width = jnp.arange(value.shape[1], dtype=jnp.int32)
    choice = (width[:, None, None] == wanted[None]).astype(jnp.float32)
    return jnp.einsum("iw,wkv->kiv", value, choice, precision=HIGH)


def thirds(left, right):
    joint = right.shape[1]
    half = joint // 2
    rights = jnp.stack(
        [
            jnp.pad(right, ((0, 0), (0, half))),
            jnp.pad(right[:, :half], ((0, 0), (joint, 0))),
            jnp.pad(right[:, half:], ((0, 0), (0, joint))),
            jnp.pad(right, ((0, 0), (half, 0))),
        ]
    )
    return jnp.einsum("kiv,kid->vd", left, rights, precision=HIGH)


def adam(grad, first, second, anchor):
    first = beta_one * first + (1.0 - beta_one) * grad
    second = beta_two * second + (1.0 - beta_two) * grad * grad
    stepped = first * (1.0 / (1.0 - beta_one**STEP_COUNT))
    scaled = second * (1.0 / (1.0 - beta_two**STEP_COUNT))
    delta = inner_rate * (stepped / (jnp.sqrt(scaled) + adam_eps) + decay_rate * anchor)
    return (first, second, delta)


MESH = pl.DeviceIdType.MESH
SUBLANES = 8
CLOSE_RANKS = 16


def greet_seq(me, count):
    group = lax.axis_index("grp")
    barrier = pltpu.get_barrier_semaphore()

    def one(step, carry):
        pl.semaphore_signal(
            barrier, inc=1, device_id=(group, lax.rem(me + step, count)), device_id_type=MESH
        )
        return carry

    lax.fori_loop(1, count, one, 0)
    pl.semaphore_wait(barrier, count - 1)


def sum_kernel(count, x_ref, out_ref, parts, own, totals, send_one, recv_one, send_two, recv_two):
    me = lax.axis_index("seq")
    group = lax.axis_index("grp")
    greet_seq(me, count)

    def slice_copy(step):
        peer = lax.rem(me + step, count)
        return pltpu.make_async_remote_copy(
            src_ref=x_ref.at[peer],
            dst_ref=parts.at[step],
            send_sem=send_one.at[step],
            recv_sem=recv_one.at[step],
            device_id=(group, peer),
            device_id_type=MESH,
        )

    def total_copy(step):
        peer = lax.rem(me + step, count)
        return pltpu.make_async_remote_copy(
            src_ref=own,
            dst_ref=totals.at[step],
            send_sem=send_two.at[step],
            recv_sem=recv_two.at[step],
            device_id=(group, peer),
            device_id_type=MESH,
        )

    def start_of(make):
        def one(step, carry):
            make(step).start()
            return carry

        return one

    lax.fori_loop(1, count, start_of(slice_copy), 0)
    own[...] = x_ref[me]

    def gather_in(step, carry):
        slice_copy(step).wait()
        own[...] += parts[step]
        return carry

    lax.fori_loop(1, count, gather_in, 0)
    lax.fori_loop(1, count, start_of(total_copy), 0)
    out_ref[me] = own[...]

    def spread(step, carry):
        total_copy(step).wait()
        out_ref[lax.rem(me + count - step, count)] = totals[step]
        return carry

    lax.fori_loop(1, count, spread, 0)


def in_slices(values, count):
    size = sum(math.prod(value.shape) for value in values)
    block = -(-size // (count * SUBLANES * LANES)) * SUBLANES
    flat = jnp.concatenate([value.reshape(-1) for value in values])
    return jnp.pad(flat, (0, count * block * LANES - size)).reshape(count, block, LANES)


def sum_over_seq(values, collective):
    count = lax.axis_size("seq")
    if count != CLOSE_RANKS:
        return lax.psum(values, "seq")
    small = in_slices(values, count)
    shape = small.shape
    total = pl.pallas_call(
        functools.partial(sum_kernel, count),
        out_shape=jax.ShapeDtypeStruct(shape, jnp.float32),
        in_specs=[pl.BlockSpec(memory_space=pltpu.VMEM)],
        out_specs=pl.BlockSpec(memory_space=pltpu.VMEM),
        scratch_shapes=[
            pltpu.VMEM(shape, jnp.float32),
            pltpu.VMEM(shape[1:], jnp.float32),
            pltpu.VMEM(shape, jnp.float32),
        ]
        + [pltpu.SemaphoreType.DMA((count,))] * 4,
        compiler_params=pltpu.CompilerParams(collective_id=collective, has_side_effects=True),
        cost_estimate=pl.CostEstimate(
            flops=math.prod(shape), transcendentals=0, bytes_accessed=16 * math.prod(shape)
        ),
        name="sum_over_seq",
    )(small)
    return carve(total.reshape(-1), [value.shape for value in values])


def share_kernel(count, x_ref, out_ref, parts, send_sem, recv_sem):
    seq = lax.axis_size("seq")
    me = lax.axis_index("grp") * seq + lax.axis_index("seq")

    def place(step):
        peer = lax.rem(me + step, count)
        return peer // seq, lax.rem(peer, seq)

    barrier = pltpu.get_barrier_semaphore()

    def greet(step, carry):
        pl.semaphore_signal(barrier, inc=1, device_id=place(step), device_id_type=MESH)
        return carry

    lax.fori_loop(1, count, greet, 0)
    pl.semaphore_wait(barrier, count - 1)

    def copy_of(step):
        return pltpu.make_async_remote_copy(
            src_ref=x_ref,
            dst_ref=parts.at[step],
            send_sem=send_sem.at[step],
            recv_sem=recv_sem.at[step],
            device_id=place(step),
            device_id_type=MESH,
        )

    def start(step, carry):
        copy_of(step).start()
        return carry

    lax.fori_loop(1, count, start, 0)
    out_ref[me] = x_ref[...]

    def finish(step, carry):
        copy_of(step).wait()
        out_ref[lax.rem(me + count - step, count)] = parts[step]
        return carry

    lax.fori_loop(1, count, finish, 0)


def sums_by_group(value, collective):
    groups, count = lax.axis_size("grp"), lax.axis_size("seq")
    shape = (groups * count, SUBLANES, LANES)
    shared = pl.pallas_call(
        functools.partial(share_kernel, groups * count),
        out_shape=jax.ShapeDtypeStruct(shape, jnp.float32),
        in_specs=[pl.BlockSpec(memory_space=pltpu.VMEM)],
        out_specs=pl.BlockSpec(memory_space=pltpu.VMEM),
        scratch_shapes=[pltpu.VMEM(shape, jnp.float32)]
        + [pltpu.SemaphoreType.DMA((groups * count,))] * 2,
        compiler_params=pltpu.CompilerParams(collective_id=collective, has_side_effects=True),
        name="share_over_all",
    )(jnp.full(shape[1:], value, jnp.float32))
    return jnp.sum(shared[:, 0, 0].reshape(groups, count), axis=1)


GRID = (4, 2, 2)
GATHER_Y_LAG = 2
GATHER_X_LAG = 7
GATHER_AHEAD = 0


def place_of(me):
    return me // 4, lax.rem(me // 2, 2), lax.rem(me, 2)


def rank_of(along, across, core):
    return (along * 2 + across) * 2 + core


def gather_kernel(shared, *refs):
    pieces = len(shared)
    own_refs, out_refs = refs[:pieces], refs[pieces : 2 * pieces]
    local_sem, z_send, z_recv, y_send, y_recv, x_send, x_recv, c_send, c_recv = refs[2 * pieces :]
    group, me = lax.axis_index("grp"), lax.axis_index("seq")
    z, y, core = place_of(me)
    z_size = GRID[0]
    across, sibling, twin = (
        (group, rank_of(z, 1 - y, core)),
        (group, rank_of(z, y, 1 - core)),
        (1 - group, me),
    )
    barrier = pltpu.get_barrier_semaphore()
    for there in (across, sibling, twin):
        pl.semaphore_signal(barrier, inc=1, device_id=there, device_id_type=MESH)

    @pl.when(z > 0)
    def _():
        pl.semaphore_signal(
            barrier, inc=1, device_id=(group, rank_of(z - 1, y, core)), device_id_type=MESH
        )

    @pl.when(z < z_size - 1)
    def _():
        pl.semaphore_signal(
            barrier, inc=1, device_id=(group, rank_of(z + 1, y, core)), device_id_type=MESH
        )

    neighbours = (z > 0).astype(jnp.int32) + (z < z_size - 1).astype(jnp.int32)
    pl.semaphore_wait(barrier, 3 + neighbours)

    def half_of(ref, piece, half):
        if half is None:
            return ref
        if ref.shape[-1] == LANES:
            span = ref.shape[-2] // 2
            return ref.at[pl.ds(pl.multiple_of(half * span, ROW_GROUP), span), :]
        span = ref.shape[-1] // 2
        return ref.at[:, pl.ds(pl.multiple_of(half * span, LANES), span)]

    def move(piece, half, there, along, over, send, recv, own=False):
        dst = half_of(out_refs[piece].at[rank_of(along, over, core)], piece, half)
        src = half_of(own_refs[piece], piece, half) if own else dst
        return pltpu.make_async_remote_copy(
            src_ref=src, dst_ref=dst, send_sem=send, recv_sem=recv, device_id=there, device_id_type=MESH
        )

    def z_move(piece, along, forward, own=False):
        there = (group, rank_of(z + (1 if forward else -1), y, core))
        half = group if shared[piece] else None
        return move(
            piece, half, there, along, y, z_send.at[piece, along, int(forward)], z_recv.at[piece, along], own
        )

    def y_move(piece, along, own=False, over=None):
        half = group if shared[piece] else None
        over = y if over is None else over
        return move(piece, half, across, along, over, y_send.at[piece, along], y_recv.at[piece, along], own)

    def x_move(piece, along, over, arriving=False):
        half = 1 - group if arriving else group
        slot = along * 2 + over
        return move(piece, half, twin, along, over, x_send.at[piece, slot], x_recv.at[piece, slot])

    def c_move(piece, along, over, half, slot, own=False):
        return move(
            piece,
            half,
            sibling,
            along,
            over,
            c_send.at[piece, along * 2 + over, slot],
            c_recv.at[piece, along * 2 + over, slot],
            own,
        )

    def each_along(distance, action):
        if distance == 0:
            action(z, True, True)
            return

        @pl.when(z - distance >= 0)
        def _():
            action(z - distance, True, False)

        @pl.when(z + distance < z_size)
        def _():
            action(z + distance, False, True)

    def own_sends(piece):
        pltpu.make_async_copy(own_refs[piece], out_refs[piece].at[me], local_sem.at[piece]).start()

        @pl.when(z + 1 < z_size)
        def _():
            z_move(piece, z, True, own=True).start()

        @pl.when(z > 0)
        def _():
            z_move(piece, z, False, own=True).start()

        y_move(piece, z, own=True).start()
        c_move(piece, z, y, None, 0, own=True).start()

    def z_arrivals(piece, distance):
        if distance == 0:
            return

        def one(along, onward, backward):
            z_move(piece, along, onward).wait_recv()

            @pl.when((z + 1 < z_size) if onward else (z > 0))
            def _():
                z_move(piece, along, onward).start()

            y_move(piece, along).start()
            if shared[piece]:
                x_move(piece, along, y).start()
            c_move(piece, along, y, group if shared[piece] else None, 0).start()

        each_along(distance, one)

    def y_arrivals(piece, distance):
        def one(along, *_):
            y_move(piece, along, over=1 - y).wait_recv()
            if shared[piece]:
                x_move(piece, along, 1 - y).start()
            c_move(piece, along, 1 - y, group if shared[piece] else None, 0).start()

        each_along(distance, one)

    def x_arrivals(piece, distance):
        if not shared[piece]:
            return

        def one(along, *_):
            for turn in range(2):
                over = y if turn == 0 else 1 - y
                if distance == 0 and turn == 0:
                    continue
                x_move(piece, along, over, arriving=True).wait_recv()
                c_move(piece, along, over, 1 - group, 1).start()

        each_along(distance, one)

    def drain(piece, distance):
        def one(along, onward, backward):
            own = distance == 0
            half = group if shared[piece] else None
            for turn in range(2):
                over = y if turn == 0 else 1 - y
                mine = own and turn == 0
                whole = None if mine else half
                c_move(piece, along, over, whole, 0).wait()
                if shared[piece] and not mine:
                    c_move(piece, along, over, 1 - group, 1).wait()
                    x_move(piece, along, over).wait_send()
            y_move(piece, along).wait_send()
            if onward:

                @pl.when(z + 1 < z_size)
                def _():
                    z_move(piece, along, True).wait_send()

            if backward:

                @pl.when(z > 0)
                def _():
                    z_move(piece, along, False).wait_send()

        each_along(distance, one)
        if distance == 0:
            pltpu.make_async_copy(own_refs[piece], out_refs[piece].at[me], local_sem.at[piece]).wait()

    slots = [(piece, distance) for piece in range(pieces) for distance in range(z_size)]
    own_sends(0)
    for turn in range(len(slots) + GATHER_X_LAG):
        if turn < len(slots):
            piece, distance = slots[turn]
            if distance == GATHER_AHEAD and piece + 1 < pieces:
                own_sends(piece + 1)
            z_arrivals(piece, distance)
        if 0 <= turn - GATHER_Y_LAG < len(slots):
            y_arrivals(*slots[turn - GATHER_Y_LAG])
        if 0 <= turn - GATHER_X_LAG < len(slots):
            x_arrivals(*slots[turn - GATHER_X_LAG])
    for slot in slots:
        drain(*slot)


def gather_pieces(pieces, shared, collective):
    count = lax.axis_size("seq")
    if count != math.prod(GRID) or lax.axis_size("grp") != 2:
        return [lax.all_gather(piece, "seq", axis=0) for piece in pieces]
    amount = len(pieces)
    sems = [
        (amount,),
        (amount, 4, 2),
        (amount, 4),
        (amount, 4),
        (amount, 4),
        (amount, 8),
        (amount, 8),
        (amount, 8, 2),
        (amount, 8, 2),
    ]
    return pl.pallas_call(
        functools.partial(gather_kernel, tuple(shared)),
        out_shape=[jax.ShapeDtypeStruct((count,) + piece.shape, piece.dtype) for piece in pieces],
        in_specs=[pl.BlockSpec(memory_space=pl.ANY)] * amount,
        out_specs=[pl.BlockSpec(memory_space=pl.ANY)] * amount,
        scratch_shapes=[pltpu.SemaphoreType.DMA(shape) for shape in sems],
        compiler_params=pltpu.CompilerParams(collective_id=collective, has_side_effects=True),
        name="gather_pieces",
    )(*pieces)


ROW_GROUP = 16
UPPER_CUTS = 3
SCATTER_LAG = 2


def scatter_kernel(pieces, amount, carried, *refs):
    grads, passing = refs[:amount], refs[amount : amount + carried]
    small = refs[amount + carried]
    refs = refs[amount + carried + 1 :]
    outs, twins = refs[:amount], refs[amount : 2 * amount]
    passed = refs[2 * amount : 2 * amount + carried]
    squares, small_out = refs[2 * amount + carried : 2 * amount + carried + 2]
    rest = refs[2 * amount + carried + 2 :]
    count = len(pieces)
    ranks = lax.axis_size("seq")
    own, beside, facing, from_left, from_right, ready = (
        rest[k * count : (k + 1) * count] for k in range(6)
    )
    load_sem, c_send, c_recv, y_send, y_recv, z_send, z_recv, x_send, x_recv = rest[
        6 * count : 6 * count + 9
    ]
    pass_send, pass_recv, parts, own_sum, totals, send_one, recv_one, send_two, recv_two = rest[
        6 * count + 9 :
    ]
    group, me = lax.axis_index("grp"), lax.axis_index("seq")
    z, y, core = place_of(me)
    z_size = GRID[0]
    across, sibling = (group, rank_of(z, 1 - y, core)), (group, rank_of(z, y, 1 - core))
    twin = (1 - group, me)
    left, right = (group, rank_of(z - 1, y, core)), (group, rank_of(z + 1, y, core))
    has_left, has_right = z > 0, z < z_size - 1
    barrier = pltpu.get_barrier_semaphore()
    pl.semaphore_signal(barrier, inc=1, device_id=twin, device_id_type=MESH)

    def greet(step, carry):
        there = (group, lax.rem(me + step, ranks))
        pl.semaphore_signal(barrier, inc=1, device_id=there, device_id_type=MESH)
        return carry

    lax.fori_loop(1, ranks, greet, 0)
    pl.semaphore_wait(barrier, ranks)
    squares[...] = jnp.zeros_like(squares)

    def part(piece, along, over, owner):
        which, row, rows, column, columns = pieces[piece]
        return grads[which].at[rank_of(along, over, owner), pl.ds(row, rows), pl.ds(column, columns)]

    def load(piece, along, over):
        slot = along * 2 + over
        return pltpu.make_async_copy(
            part(piece, along, over, core), own[piece].at[slot], load_sem.at[piece, slot]
        )

    def remote(src, dst, send, recv, there):
        return pltpu.make_async_remote_copy(
            src_ref=src, dst_ref=dst, send_sem=send, recv_sem=recv, device_id=there, device_id_type=MESH
        )

    def c_move(piece, along, over):
        slot = along * 2 + over
        return remote(
            part(piece, along, over, 1 - core),
            beside[piece].at[slot],
            c_send.at[piece, slot],
            c_recv.at[piece, slot],
            sibling,
        )

    def y_move(piece, along):
        return remote(
            own[piece].at[along * 2 + 1 - y],
            facing[piece].at[along],
            y_send.at[piece, along],
            y_recv.at[piece, along],
            across,
        )

    def z_move(piece, along, forward):
        side = 0 if forward else 1
        return remote(
            facing[piece].at[along],
            (from_left if forward else from_right)[piece].at[along],
            z_send.at[piece, along],
            z_recv.at[piece, along, side],
            right if forward else left,
        )

    def x_move(piece):
        which, row, height, column, columns = pieces[piece]
        return remote(
            ready[piece],
            twins[which].at[pl.ds(row, height), pl.ds(column, columns)],
            x_send.at[piece],
            x_recv.at[piece],
            twin,
        )

    def pass_move(k):
        return remote(passing[k], passed[k], pass_send.at[k], pass_recv.at[k], twin)

    def slice_move(step):
        peer = lax.rem(me + step, ranks)
        return remote(
            small.at[peer], parts.at[step], send_one.at[step], recv_one.at[step], (group, peer)
        )

    def total_move(step):
        peer = lax.rem(me + step, ranks)
        return remote(own_sum, totals.at[step], send_two.at[step], recv_two.at[step], (group, peer))

    def small_begin():
        def one(step, carry):
            slice_move(step).start()
            return carry

        lax.fori_loop(1, ranks, one, 0)
        own_sum[...] = small[me]

    def small_middle():
        def gather_in(step, carry):
            slice_move(step).wait()
            own_sum[...] += parts[step]
            return carry

        lax.fori_loop(1, ranks, gather_in, 0)

        def one(step, carry):
            total_move(step).start()
            return carry

        lax.fori_loop(1, ranks, one, 0)
        small_out[me] = own_sum[...]

    def small_end():
        def spread(step, carry):
            total_move(step).wait()
            small_out[lax.rem(me + ranks - step, ranks)] = totals[step]
            return carry

        lax.fori_loop(1, ranks, spread, 0)

    def each_along(distance, action):
        if distance == 0:
            action(z, None)
            return

        @pl.when(z - distance >= 0)
        def _():
            action(z - distance, False)

        @pl.when(z + distance < z_size)
        def _():
            action(z + distance, True)

    def by_rows(piece, body):
        def one(step, carry):
            body(pl.ds(pl.multiple_of(step * ROW_GROUP, ROW_GROUP), ROW_GROUP))
            return carry

        lax.fori_loop(0, pieces[piece][2] // ROW_GROUP, one, 0)

    def wide(ref, slot, rows):
        return ref[slot, rows, :].astype(jnp.float32)

    def begin(piece):
        for distance in reversed(range(z_size)):

            def one(along, _):
                for over in range(2):
                    load(piece, along, over).start()
                    c_move(piece, along, over).start()

            each_along(distance, one)

    def c_stage(piece, distance):
        def one(along, _):
            for turn in range(2):
                over = 1 - y if turn == 0 else y
                slot = along * 2 + over
                load(piece, along, over).wait()
                c_move(piece, along, over).wait_recv()

                def add(rows):
                    total = wide(own[piece], slot, rows) + wide(beside[piece], slot, rows)
                    own[piece][slot, rows, :] = total.astype(jnp.bfloat16)

                by_rows(piece, add)
                if turn == 0:
                    y_move(piece, along).start()

        each_along(distance, one)

    def y_stage(piece, distance):
        which, row, height, column, columns = pieces[piece]

        def one(along, forward):
            y_move(piece, along).wait_recv()
            slot = along * 2 + y
            if forward is None:

                def add(rows):
                    total = wide(own[piece], slot, rows) + wide(facing[piece], along, rows)
                    there = pl.ds(pl.multiple_of(row + rows.start, ROW_GROUP), ROW_GROUP)
                    outs[which][there, pl.ds(column, columns)] = total

                by_rows(piece, add)
                for side, present, source in ((True, has_left, from_left), (False, has_right, from_right)):

                    @pl.when(present)
                    def _():
                        z_move(piece, along, side).wait_recv()

                        def more(rows):
                            there = pl.ds(pl.multiple_of(row + rows.start, ROW_GROUP), ROW_GROUP)
                            outs[which][there, pl.ds(column, columns)] += wide(source[piece], along, rows)

                        by_rows(piece, more)

                def finish(rows):
                    there = pl.ds(pl.multiple_of(row + rows.start, ROW_GROUP), ROW_GROUP)
                    total = outs[which][there, pl.ds(column, columns)]
                    ready[piece][rows, :] = total.astype(jnp.bfloat16)
                    square = total[:SUBLANES] * total[:SUBLANES] + total[SUBLANES:] * total[SUBLANES:]
                    for k in range(columns // LANES):
                        squares[...] += square[:, k * LANES : (k + 1) * LANES]

                by_rows(piece, finish)
                x_move(piece).start()
                return
            source, present = (from_left, has_left) if forward else (from_right, has_right)

            @pl.when(present)
            def _():
                z_move(piece, along, forward).wait_recv()

                def add(rows):
                    total = wide(own[piece], slot, rows) + wide(facing[piece], along, rows)
                    total = total + wide(source[piece], along, rows)
                    facing[piece][along, rows, :] = total.astype(jnp.bfloat16)

                by_rows(piece, add)

            @pl.when(jnp.logical_not(present))
            def _():
                def add(rows):
                    total = wide(own[piece], slot, rows) + wide(facing[piece], along, rows)
                    facing[piece][along, rows, :] = total.astype(jnp.bfloat16)

                by_rows(piece, add)

            z_move(piece, along, forward).start()

        each_along(distance, one)

    def drain(piece, distance):
        def one(along, forward):
            for over in range(2):
                c_move(piece, along, over).wait_send()
            y_move(piece, along).wait_send()
            if forward is not None:
                z_move(piece, along, forward).wait_send()

        each_along(distance, one)

    slots = [(piece, distance) for piece in range(count) for distance in reversed(range(z_size))]
    begin(0)
    small_begin()
    for piece in range(1, min(2, count)):
        begin(piece)
    for k in range(carried):
        pass_move(k).start()
    for turn in range(len(slots) + SCATTER_LAG):
        if turn < len(slots):
            c_stage(*slots[turn])
            if turn == z_size:
                small_middle()
            piece, distance = slots[turn]
            if distance == 0 and piece + 2 < count:
                begin(piece + 2)
        if turn >= SCATTER_LAG:
            y_stage(*slots[turn - SCATTER_LAG])
    for slot in slots:
        drain(*slot)
    for piece in range(count):
        x_move(piece).wait()
    for k in range(carried):
        pass_move(k).wait()
    small_end()


def scatter_grads(grads, cuts, passing, values, collective):
    count = math.prod(GRID)
    grads = [grad.reshape(count, grad.shape[0] // count, grad.shape[1]) for grad in grads]
    pieces = []
    for which, cut in enumerate(cuts):
        rows, columns = grads[which].shape[1:]
        pieces += [(which, 0, rows, k * (columns // cut), columns // cut) for k in range(cut)]
    amount = len(pieces)
    places = math.prod(GRID[:2])

    def room(slots):
        return [pltpu.VMEM((slots, piece[2], piece[4]), jnp.bfloat16) for piece in pieces]

    sems = [
        (amount, places),
        (amount, places),
        (amount, places),
        (amount, GRID[0]),
        (amount, GRID[0]),
        (amount, GRID[0]),
        (amount, GRID[0], 2),
        (amount,),
        (amount,),
    ]
    small = in_slices(values, count)
    slot = small.shape[1:]
    carried = len(passing)
    sems += [(carried,)] * 2
    kinds = len(grads)
    *arrays, squares, total = pl.pallas_call(
        functools.partial(scatter_kernel, tuple(pieces), kinds, carried),
        out_shape=[jax.ShapeDtypeStruct(grad.shape[1:], jnp.float32) for grad in grads]
        + [jax.ShapeDtypeStruct(grad.shape[1:], jnp.bfloat16) for grad in grads]
        + [jax.ShapeDtypeStruct(part.shape, part.dtype) for part in passing]
        + [jax.ShapeDtypeStruct((SUBLANES, LANES), jnp.float32)]
        + [jax.ShapeDtypeStruct(small.shape, jnp.float32)],
        in_specs=[pl.BlockSpec(memory_space=pl.ANY)] * (kinds + carried)
        + [pl.BlockSpec(memory_space=pltpu.VMEM)],
        out_specs=[pl.BlockSpec(memory_space=pltpu.VMEM)] * kinds
        + [pl.BlockSpec(memory_space=pl.ANY)] * (kinds + carried)
        + [pl.BlockSpec(memory_space=pltpu.VMEM)] * 2,
        scratch_shapes=room(places)
        + room(places)
        + room(GRID[0])
        + room(GRID[0])
        + room(GRID[0])
        + [pltpu.VMEM((piece[2], piece[4]), jnp.bfloat16) for piece in pieces]
        + [pltpu.SemaphoreType.DMA(shape) for shape in sems]
        + [
            pltpu.VMEM(small.shape, jnp.float32),
            pltpu.VMEM(slot, jnp.float32),
            pltpu.VMEM(small.shape, jnp.float32),
        ]
        + [pltpu.SemaphoreType.DMA((count,))] * 4,
        compiler_params=pltpu.CompilerParams(
            collective_id=collective, has_side_effects=True, vmem_limit_bytes=VMEM_LIMIT
        ),
        name="scatter_grads",
    )(*grads, *passing, small)
    return (
        arrays[:kinds],
        arrays[kinds : 2 * kinds],
        arrays[2 * kinds :],
        jnp.sum(squares),
        carve(total.reshape(-1), [value.shape for value in values]),
    )


def lay_out_kernel(shards, view_ref, *outs):
    cut = D // shards * (4 * D + FF) // LANES
    for layer in range(L):
        upper, lower = outs[2 * layer : 2 * layer + 2]
        for ref, base in ((upper, 0), (lower, cut)):
            across = ref.shape[1] // LANES
            for row in range(0, ref.shape[0], ROW_GROUP):
                for column in range(across):
                    start = L * (base + row * across + column) + layer
                    rows = view_ref[pl.ds(start, ROW_GROUP, stride=L * across), :]
                    ref[row : row + ROW_GROUP, column * LANES : (column + 1) * LANES] = rows.astype(
                        jnp.bfloat16
                    )


def flat_view(array):
    layers, size = array.shape
    return array.reshape(layers, size // LANES, LANES).transpose(1, 0, 2).reshape(-1, LANES)


def unpack_kernel(size, x_ref, lead_ref, time_ref, text_ref, audio_ref, caption_ref, tail_ref, flat):
    count, rows = x_ref.shape[:2]
    lane = lax.broadcasted_iota(jnp.int32, (rows, LANES), 1)
    for rank in range(count):
        base, phase = divmod(rank * size, LANES)
        shard = x_ref[rank].astype(jnp.float32)
        if phase == 0:
            flat[base : base + rows, :] = shard
            continue
        turned = pltpu.roll(shard, phase, axis=1)
        pltpu.store(flat.at[pl.ds(base, rows), :], turned, mask=lane >= phase)
        pltpu.store(flat.at[pl.ds(base + 1, rows), :], turned, mask=lane < phase)
    start = lead_ref.shape[0]
    lead_ref[...] = flat[:start, :]
    for ref in (time_ref, text_ref, audio_ref, caption_ref):
        across = ref.shape[1] // LANES
        for row in range(0, ref.shape[0], ROW_GROUP):
            for column in range(across):
                ref[row : row + ROW_GROUP, column * LANES : (column + 1) * LANES] = flat[
                    pl.ds(start + row * across + column, ROW_GROUP, stride=across), :
                ].astype(jnp.bfloat16)
        start += ref.shape[0] * across
    tail_ref[...] = flat[start : start + tail_ref.shape[0], :]


def unpack_others(gathered, size, channels, text_width):
    count, rows, lanes = gathered.shape
    lead = 2 * channels * D // LANES
    shapes = [(D, D), (text_width, D), (D, E), (text_width, E)]
    tail = (2 * L + 1 + 1) * D // LANES
    whole = -(-count * size // LANES)
    outs = pl.pallas_call(
        functools.partial(unpack_kernel, size),
        out_shape=[jax.ShapeDtypeStruct((lead, LANES), jnp.float32)]
        + [jax.ShapeDtypeStruct(shape, jnp.bfloat16) for shape in shapes]
        + [jax.ShapeDtypeStruct((tail, LANES), jnp.float32)],
        in_specs=[pl.BlockSpec(memory_space=pltpu.VMEM)],
        out_specs=[pl.BlockSpec(memory_space=pltpu.VMEM)] * 6,
        scratch_shapes=[pltpu.VMEM((whole + 2 * rows, LANES), jnp.float32)],
        compiler_params=pltpu.CompilerParams(vmem_limit_bytes=VMEM_LIMIT),
        name="unpack_others",
    )(gathered)
    w_in, w_out = outs[0].reshape(2, channels * D)
    tail_rows = outs[5].reshape(-1, D)
    return (
        w_in.reshape(channels, D).astype(jnp.bfloat16),
        w_out.reshape(D, channels).astype(jnp.bfloat16),
        *outs[1:5],
        tail_rows[:-1],
        tail_rows[-1],
    )


def lay_out(anchor, shards):
    if shards != math.prod(GRID):
        return [layer_rows(anchor[depth].astype(jnp.bfloat16), shards) for depth in range(L)]
    shapes = [(D // shards, 4 * D + FF), (FF // shards, D)] * L
    outs = pl.pallas_call(
        functools.partial(lay_out_kernel, shards),
        out_shape=[jax.ShapeDtypeStruct(shape, jnp.bfloat16) for shape in shapes],
        in_specs=[pl.BlockSpec(memory_space=pltpu.VMEM)],
        out_specs=[pl.BlockSpec(memory_space=pltpu.VMEM)] * len(shapes),
        compiler_params=pltpu.CompilerParams(vmem_limit_bytes=VMEM_LIMIT),
        name="lay_out",
    )(flat_view(anchor))
    return [(outs[2 * depth], outs[2 * depth + 1]) for depth in range(L)]


def flatten(parts):
    return jnp.concatenate([part.reshape(-1) for part in parts])


def group_mean(delta, count):
    low = lax.reduce_precision(delta, 8, 7)
    total = low
    for step in range(1, count):
        moves = [(source, (source + step) % count) for source in range(count)]
        total = total + lax.ppermute(low.astype(jnp.bfloat16), "grp", moves).astype(jnp.float32)
    return total / count


STEP_BLOCKS = 6


def delta_of(grad, first, second, anchor):
    return adam(grad, first, second, anchor)[2]


def step_kernel(cut, places, factors, *refs):
    amount = len(places)
    own, twin = refs[:amount], refs[amount : 2 * amount]
    anchor, first, second, outer, twin_first, twin_second = refs[2 * amount : 2 * amount + 6]
    new, one, two, mean_out, momentum_out, own_flat, twin_flat = refs[2 * amount + 6 :]
    step = pl.program_id(0)
    block = anchor.shape[0]

    @pl.when(step == 0)
    def _():
        for grads, flat in ((own, own_flat), (twin, twin_flat)):
            for ref, (layer, first_column) in zip(grads, places):
                base, width = (cut, ref.shape[1]) if first_column is None else (0, 4 * D + FF)
                across, skip = width // LANES, (first_column or 0) // LANES
                for row in range(0, ref.shape[0], ROW_GROUP):
                    for column in range(ref.shape[1] // LANES):
                        start = L * (base + row * across + skip + column) + layer
                        flat[pl.ds(start, ROW_GROUP, stride=L * across), :] = ref[
                            row : row + ROW_GROUP, column * LANES : (column + 1) * LANES
                        ].astype(jnp.float32)

    rows = pl.ds(pl.multiple_of(step * block, SUBLANES), block)
    grad, weight = own_flat[rows, :], anchor[...]
    first_own, second_own = first[...], second[...]
    clipped = grad * factors[0]
    one[...] = beta_one * first_own + (1.0 - beta_one) * clipped
    two[...] = beta_two * second_own + (1.0 - beta_two) * clipped * clipped
    rounded = grad.astype(jnp.bfloat16).astype(jnp.float32)
    delta_own = delta_of(rounded * factors[0], first_own, second_own, weight)
    delta_twin = delta_of(twin_flat[rows, :] * factors[1], twin_first[...], twin_second[...], weight)
    mean = (delta_own + delta_twin) * 0.5
    momentum = outer_mu * outer[...] + mean
    mean_out[...] = mean
    momentum_out[...] = momentum
    new[...] = weight - outer_rate * (mean + outer_mu * momentum)


def step_layers(factors, own, twin, views, shards):
    rows = views[0].shape[0]
    places = tuple((layer, column) for _, layer, column in own)
    own = [grad for grad, _, _ in own]
    block = rows // STEP_BLOCKS
    whole = pl.BlockSpec(memory_space=pltpu.VMEM)
    part = pl.BlockSpec((block, LANES), lambda k: (k, 0))
    return pl.pallas_call(
        functools.partial(step_kernel, D // shards * (4 * D + FF) // LANES, places),
        grid=(STEP_BLOCKS,),
        out_shape=[jax.ShapeDtypeStruct((rows, LANES), jnp.float32)] * 5,
        in_specs=[pl.BlockSpec(memory_space=pltpu.SMEM)] + [whole] * (2 * len(own)) + [part] * 6,
        out_specs=[part] * 5,
        scratch_shapes=[pltpu.VMEM((rows, LANES), jnp.float32)] * 2,
        compiler_params=pltpu.CompilerParams(
            vmem_limit_bytes=VMEM_LIMIT, dimension_semantics=("arbitrary",)
        ),
        name="step_layers",
    )(factors, *own, *twin, *views)


def from_view(view):
    rows, lanes = view.shape
    return view.reshape(rows // L, L, lanes).transpose(1, 0, 2).reshape(L, rows // L * lanes)


def swapped(value):
    return lax.ppermute(value, "grp", [(0, 1), (1, 0)])


def per_device(
    anchor_layers,
    anchor_other,
    first_layers,
    first_other,
    second_layers,
    second_other,
    outer_layers,
    outer_other,
    latents,
    noise,
    lengths,
    timesteps,
    null_flags,
    captions,
):
    seq_count = lax.axis_size("seq")
    group_count = lax.axis_size("grp")
    rank = lax.axis_index("seq")
    group = lax.axis_index("grp")
    close = seq_count == math.prod(GRID) and group_count == 2
    rows = latents.shape[0]
    channels = latents.shape[1]
    frames_group = rows * seq_count
    lengths = lengths[0]
    timesteps = timesteps[0]
    null_flags = null_flags[0]
    captions = captions[0]
    item_count = lengths.shape[0]
    text_width = captions.shape[1]
    other_size = anchor_other.shape[0]
    padded = -(-other_size // 4096) * 4096
    other_rows = jnp.pad(anchor_other.astype(jnp.bfloat16), (0, padded - other_size))
    own_rows = lay_out(anchor_layers, seq_count)
    early = L
    own_block = block_of(rank, close)
    frames = jnp.concatenate([latents, noise], axis=1).T
    pieces = [frames, other_rows.reshape(-1, LANES)]
    pieces += [part for pair in own_rows[:early] for part in pair]
    gathered_frames, other_rows, *early_rows = gather_pieces(
        pieces, [False, True] + [True, False] * early, 4
    )
    if close:
        first_view, second_view = flat_view(first_layers[0]), flat_view(second_layers[0])
        (*sources, first_other, second_other), other_rows = lax.optimization_barrier(
            ((first_view, second_view, first_other, second_other), other_rows)
        )
        twin_views = [swapped(value) for value in sources]
        twin_moments = [swapped(value)[0] for value in (first_other, second_other)]
    late_rows = [lax.all_gather(part, "seq", axis=0) for pair in own_rows[early:] for part in pair]
    layer_parts = [part.reshape(-1, part.shape[-1]) for part in early_rows + late_rows]
    gathered = [split_upper(*layer_parts[2 * depth : 2 * depth + 2]) for depth in range(L)]
    if close:
        other_parts = unpack_others(other_rows, other_size, channels, text_width)
    else:
        other_low = other_rows.reshape(seq_count, padded)[:, :other_size].reshape(-1)
        other_parts = carve(other_low, other_shapes(channels, D, text_width, E, L))
    w_in, w_out, w_time, w_text, w_audio, w_caption, gains, null_text = other_parts
    w_time_f = w_time.astype(jnp.float32)
    w_text_f = w_text.astype(jnp.float32)
    w_audio_f = w_audio.astype(jnp.float32)
    w_caption_f = w_caption.astype(jnp.float32)
    gains_f = gains.astype(jnp.float32)
    null_f = null_text.astype(jnp.float32)
    places = own_block * rows + jnp.arange(rows, dtype=jnp.int32)
    order = jnp.arange(item_count, dtype=jnp.int32)
    ends = jnp.sum(jnp.where(order[None, :] <= order[:, None], lengths[None, :], 0), axis=1)
    item = jnp.sum((places[:, None] >= ends[None, :]).astype(jnp.int32), axis=1)
    key_places = own_block * rows + jnp.arange(-2 * rows, 3 * rows, dtype=jnp.int32)
    key_item = jnp.sum((key_places[:, None] >= ends[None, :]).astype(jnp.int32), axis=1)
    key_item = jnp.where((key_places >= 0) & (key_places < frames_group), key_item, -1)
    items = (item, key_item)
    window_hot = (key_item[:, None] == jnp.arange(item_count, dtype=jnp.int32)[None, :]).astype(
        jnp.float32
    )
    inner = slice(2 * rows, 3 * rows)
    onehot = window_hot[inner]
    lengths_f = lengths[:, None].astype(jnp.float32)
    alpha_bar = plan(timesteps)
    mixing = exact(window_hot, jnp.stack([jnp.sqrt(alpha_bar), jnp.sqrt(1.0 - alpha_bar)], axis=1))
    near = frame_window(frames, gathered_frames, own_block, close).T
    noise = near[inner, channels:]
    noisy_low = (mixing[:, 0:1] * near[:, :channels] + mixing[:, 1:2] * near[:, channels:]).astype(
        jnp.bfloat16
    )
    features = time_features(timesteps)

    text = jnp.where(null_flags[:, None] == 1, null_f[None, :], captions)
    before_silu = exact(features, w_time_f) + exact(text, w_text_f)
    condition, pull_silu = jax.vjp(jax.nn.silu, before_silu)
    hidden_window = dense(noisy_low, w_in) + exact(window_hot, condition)
    lead = 2 * channels
    features_at, text_at = lead, lead + D
    audio_at = text_at + text_width
    caption_at = audio_at + D * E // D
    gains_at = caption_at + text_width * E // D
    own_rows_count = -(-other_size // D) + 1
    own_start = rank * other_size
    own_row = own_start // D
    own_at = own_row + jnp.arange(own_rows_count, dtype=jnp.int32)

    def own_part(value, start):
        reach = gains_at + 2 * own_rows_count
        value = jnp.pad(value, ((0, 0), (start, reach - start - value.shape[1])))
        return lax.dynamic_slice_in_dim(value, own_row, own_rows_count, axis=1)

    def own_rows_at(start, amount):
        there = start + jnp.arange(amount, dtype=jnp.int32)
        return (there[:, None] == own_at[None, :]).astype(jnp.float32)

    left_condition = own_part(features, features_at) + own_part(text, text_at)
    caption_left = thirds_left(captions, E, own_at - caption_at)
    saved_all = []
    entering = []
    for depth in range(L):
        weights = gathered[depth]
        proj_qkv = weights[0]
        if depth == 0:
            normed_window = norm_rows(hidden_window, gains_f[0]).astype(jnp.bfloat16)
            hidden, normed = hidden_window[inner], normed_window[inner]
            queries = dense(normed, proj_qkv[:, :D]).astype(jnp.bfloat16)
            window = [dense(normed_window, proj_qkv[:, D:]).astype(jnp.bfloat16)]
        else:
            normed = norm_rows(hidden, gains_f[2 * depth]).astype(jnp.bfloat16)
            window = gather_window(dense(normed, proj_qkv[:, D:]).astype(jnp.bfloat16), close)
            queries = dense(normed, proj_qkv[:, :D]).astype(jnp.bfloat16)
        if depth == 1 and close:
            queries, caption_left, left_condition = lax.optimization_barrier(
                (queries, caption_left, left_condition)
            )
        entering.append(hidden)
        hidden, saved = layer_forward(
            hidden, normed, queries, window, weights, gains_f[2 * depth + 1], items
        )
        saved_all.append(saved)
    final = norm_rows(hidden, gains_f[2 * L])
    final_low = final.astype(jnp.bfloat16)
    predicted = dense(final_low, w_out)
    error = predicted - noise
    part_pool = contract_rows(onehot, final, HIGH)
    squared_sum, pool_sum = sum_over_seq((jnp.sum(error * error), part_pool), 1)
    pooled = pool_sum / lengths_f
    audio_side = exact(pooled, w_audio_f)
    text_side = exact(captions, w_caption_f)
    clash, pull_clash = jax.vjp(contrast, audio_side, text_side)
    loss = squared_sum / (frames_group * channels) + contrast_weight * clash
    grad_audio_side, grad_text_side = pull_clash(jnp.float32(contrast_weight))
    grad_pred = (2.0 / (frames_group * channels) * error).astype(jnp.bfloat16)
    grad_w_out = contract_rows(final_low, grad_pred).reshape(channels, D)
    grad_pooled = against_rows(grad_audio_side, w_audio_f, HIGH) / lengths_f
    grad_final = against_rows(grad_pred, w_out) + exact(onehot, grad_pooled)
    unused, pull_final = jax.vjp(norm_rows, hidden, gains_f[2 * L])
    grad_hidden, grad_gain_final = pull_final(grad_final)
    layer_grads = [None] * L
    sent_early = [None] * L
    gain_grads = [None] * (2 * L + 1)
    gain_grads[2 * L] = grad_gain_final
    for depth in reversed(range(L)):
        weights = gathered[depth]
        proj_qkv = weights[0]
        early = depth > 0 and close
        grad_middle, grad_query, grad_pairs, rest, lower_full, gain_grads[2 * depth + 1] = layer_backward(
            grad_hidden, weights, gains_f[2 * depth + 1], items, saved_all[depth], early, 5 if depth > 0 else 1
        )
        if early:
            sent_early[depth] = [
                lax.psum_scatter(grad, "seq", scatter_dimension=0, tiled=True)
                for grad in (lower_full, rest)
            ]
        normed = saved_all[depth][0]
        if depth == 0:
            (grad_pairs,) = grad_pairs
            qkv_parts = [(normed, grad_query), (normed_window, grad_pairs)]
            grad_normed = against_rows(grad_pairs, proj_qkv[:, D:])
            grad_own = grad_normed[inner] + against_rows(grad_query, proj_qkv[:, :D])
            grad_normed = jnp.concatenate(
                [grad_normed[: 2 * rows], grad_own, grad_normed[3 * rows :]], axis=0
            )
            unused, pull_one = jax.vjp(norm_rows, hidden_window, gains_f[0])
        else:
            grad_pairs = return_window(grad_pairs, close).astype(jnp.bfloat16)
            grad_projected = jnp.concatenate([grad_query, grad_pairs], axis=1)
            qkv_parts = [(normed, grad_projected)]
            grad_normed = against_rows(grad_projected, proj_qkv)
            unused, pull_one = jax.vjp(norm_rows, entering[depth], gains_f[2 * depth])
        grad_input, gain_grads[2 * depth] = pull_one(grad_normed)
        if early:
            layer_grads[depth] = [side_by_side(qkv_parts)]
        else:
            layer_grads[depth] = [side_by_side(qkv_parts + rest), lower_full]
        if depth > 0:
            grad_hidden = grad_middle + grad_input
        else:
            grad_hidden = jnp.concatenate(
                [grad_input[: 2 * rows], grad_input[inner] + grad_middle, grad_input[3 * rows :]], axis=0
            )
    grad_w_in = contract_rows(noisy_low.astype(jnp.float32), grad_hidden, HIGH)
    grad_condition = contract_rows(window_hot, grad_hidden, HIGH)
    early_view = thirds(thirds_left(pooled, E, own_at - audio_at), grad_audio_side)
    early_view = early_view + thirds(caption_left, grad_text_side)
    left_small = jnp.concatenate(
        [
            own_rows_at(0, lead),
            left_condition,
            own_rows_at(gains_at, 2 * L + 1),
        ],
        axis=0,
    )
    silu_slope = pull_silu(jnp.ones_like(condition))[0]
    slopes = jnp.pad(silu_slope, ((lead, 2 * L + 1), (0, 0)), constant_values=1.0)
    left_null = own_rows_at(gains_at + 2 * L + 1, 1)
    early_view, left_small, slopes, left_null, layer_grads[0] = lax.optimization_barrier(
        (early_view, left_small, slopes, left_null, layer_grads[0])
    )
    small_grads = (jnp.concatenate([grad_w_in, grad_w_out, grad_condition, jnp.stack(gain_grads)]),)
    if close:
        sent = sent_early[1:]
        late = [layer_grads[depth][0] for depth in range(1, L)] + list(layer_grads[0])
        own_late, twin_late, passed, square_part, small_grads = scatter_grads(
            late,
            [1] * (L - 1) + [UPPER_CUTS, 1],
            [part for parts in sent for part in parts],
            small_grads,
            5,
        )
        own_parts = [(own_late[L - 1], 0, 0), (own_late[L], 0, None)]
        twin_parts = [twin_late[L - 1], twin_late[L]]
        for depth in range(1, L):
            lower, rest = sent[depth - 1]
            own_parts += [(own_late[depth - 1], depth, 0), (rest, depth, 3 * D), (lower, depth, None)]
            twin_parts += [twin_late[depth - 1], passed[2 * depth - 1], passed[2 * depth - 2]]
    else:
        small_grads = lax.psum(small_grads, "seq")
    weighted = small_grads[0] * slopes
    grad_before = weighted[lead : lead + item_count]
    flagged = jnp.sum(jnp.where(null_flags[:, None] == 1, grad_before, 0.0), axis=0, keepdims=True)
    grad_null = against_rows(flagged, w_text_f, HIGH)
    own_view = early_view + contract_rows(left_small, weighted, HIGH) + left_null.T * grad_null
    other_grad = lax.dynamic_slice_in_dim(own_view.reshape(-1), own_start % D, other_size)
    other_grad_square = jnp.sum(other_grad * other_grad)
    if close:
        other_grad_low = other_grad.astype(jnp.bfloat16)
        twin_other = swapped(other_grad_low).astype(jnp.float32)
        square_part = square_part + other_grad_square
        for parts in sent:
            for grad in parts:
                wide = grad.astype(jnp.float32)
                square_part = square_part + jnp.sum(wide * wide)
        norms = jnp.sqrt(sums_by_group(square_part, 3))
        total_norm = lax.dynamic_index_in_dim(norms, group, keepdims=False)
        twin_norm = lax.dynamic_index_in_dim(norms, 1 - group, keepdims=False)
        factor = jnp.minimum(1.0, clip_at / (total_norm + 1e-06))
        twin_factor = jnp.minimum(1.0, clip_at / (twin_norm + 1e-06))
        views = [flat_view(anchor_layers), first_view, second_view, flat_view(outer_layers)]
        stepped = step_layers(
            jnp.stack([factor, twin_factor]),
            own_parts,
            twin_parts,
            views + twin_views,
            seq_count,
        )
        new_layers, first_l, second_l, mean_layers, momentum_layers = map(from_view, stepped)
        first_o, second_o, _ = adam(other_grad * factor, first_other[0], second_other[0], anchor_other)
        rounded = lax.reduce_precision(other_grad, 8, 7)
        delta_o = delta_of(rounded * factor, first_other[0], second_other[0], anchor_other)
        delta_twin = delta_of(twin_other * twin_factor, *twin_moments, anchor_other)
        mean_other = (delta_o + delta_twin) / 2
    else:
        stacked = jnp.stack(
            [
                flatten(
                    lax.psum_scatter(grad, "seq", scatter_dimension=0, tiled=True).astype(jnp.float32)
                    for grad in grads
                )
                for grads in layer_grads
            ]
        )
        total_norm = jnp.sqrt(lax.psum(jnp.sum(stacked * stacked) + other_grad_square, "seq"))
        factor = jnp.minimum(1.0, clip_at / (total_norm + 1e-06))
        first_l, second_l, delta_l = adam(
            stacked * factor, first_layers[0], second_layers[0], anchor_layers
        )
        first_o, second_o, delta_o = adam(
            other_grad * factor, first_other[0], second_other[0], anchor_other
        )
        mean_layers = group_mean(delta_l, group_count)
        mean_other = group_mean(delta_o, group_count)
        momentum_layers = outer_mu * outer_layers + mean_layers
        new_layers = anchor_layers - outer_rate * (mean_layers + outer_mu * momentum_layers)
    momentum_other = outer_mu * outer_other + mean_other
    new_other = anchor_other - outer_rate * (mean_other + outer_mu * momentum_other)
    return (
        new_layers,
        new_other,
        first_l[None],
        first_o[None],
        second_l[None],
        second_o[None],
        mean_layers,
        mean_other,
        momentum_layers,
        momentum_other,
        loss.reshape(1),
        total_norm.reshape(1),
    )


def solution(mesh):
    placed = (
        P(None, "seq"),
        P("seq"),
        P("grp", None, "seq"),
        P("grp", "seq"),
        P("grp", None, "seq"),
        P("grp", "seq"),
        P(None, "seq"),
        P("seq"),
        P(("grp", "seq"), None),
        P(("grp", "seq"), None),
        P("grp", None),
        P("grp", None),
        P("grp", None),
        P("grp", None, None),
    )
    return jax.shard_map(
        per_device,
        mesh=mesh,
        in_specs=placed,
        out_specs=(
            P(None, "seq"),
            P("seq"),
            P("grp", None, "seq"),
            P("grp", "seq"),
            P("grp", None, "seq"),
            P("grp", "seq"),
            P(None, "seq"),
            P("seq"),
            P(None, "seq"),
            P("seq"),
            P("grp"),
            P("grp"),
        ),
        check_vma=False,
    )
```
